256 devices in a mesh: space: 32 (over y, x, core), chan: 8 (over z).
Axes of the slice: x: 4, y: 4, z: 8, core: 2. Of those that a mesh axis runs over, the one named last changes fastest.
Arguments:
- members: bfloat16 [8, 96, 8, 17280], P(None, 'space', 'chan'), may hold values from -400 to 400, as said below
- gain: float32 [768], P('chan'), may hold values from 0.5 to 1.5
- shift: float32 [768], P('chan'), may hold values from -3 to 3
- w_first: bfloat16 [2, 8, 96, 96], P(None, 'chan'), may hold values from -0.4375 to 0.4375
- b_first: float32 [2, 8, 96], P(None, 'chan'), may hold values from -3 to 3
- w_second: bfloat16 [2, 8, 96, 96], P(None, 'chan'), may hold values from -0.4375 to 0.4375
- b_second: float32 [2, 8, 96], P(None, 'chan'), may hold values from -3 to 3
- cotangent: bfloat16 [8, 96, 8, 17280], P(None, 'space', 'chan'), may hold values from -6 to 6
Outputs:
- mixed: bfloat16 [8, 96, 8, 17280], P(None, 'space', 'chan')
- grad_input: bfloat16 [8, 96, 8, 17280], P(None, 'space', 'chan')
- grad_w_first: float32 [2, 8, 96, 96], P(None, 'chan')
- grad_b_first: float32 [2, 8, 96], P(None, 'chan')
- grad_w_second: float32 [2, 8, 96, 96], P(None, 'chan')
- grad_b_second: float32 [2, 8, 96], P(None, 'chan')
- grad_gain: float32 [768], P('chan')
- grad_shift: float32 [768], P('chan')
The draws below stay inside these ranges and needn't reach their ends.
Inputs may be any that keep to these rules, and one draw needn't show every extreme that they name: `members`: real values of varying channel scale.
All inputs are finite; a program needn't handle non-finite values.
Results may differ from the reference program's by a relative error of at most 0.019.
The reference program's roundings to bfloat16 on the way count: a program that leaves them out, or rounds other values in their place, can miss the bound.
Values may be sent and summed in bfloat16 or wider, within the bound.
A program may use at most 64 MiB of HBM per device.

```python
import math
import jax
import jax.numpy as jnp
from jax import lax

C = 768
NB = 8
H = 96
W = 180
MW = 64
MEMBERS = 8
CB = 96


def stored_layout(tokens):
    split = tokens.reshape((MEMBERS, H, W, NB, C // NB))
    return jnp.transpose(split, (0, 1, 3, 2, 4)).reshape((MEMBERS, H, NB, W * (C // NB)))


def draw_members(key, part):
    key_base, key_rough, key_offset = jax.random.split(key, 3)
    channel_ramp = 3.0 ** (jnp.arange(C, dtype=jnp.float32) / (C - 1))
    channel_rough = jnp.exp(jax.random.uniform(key_rough, (C,), jnp.float32, 0.0, math.log(3.3)))
    channel_offset = jax.random.uniform(key_offset, (C,), jnp.float32, -1.0, 1.0)
    base_draw = jax.random.normal(key_base, (MEMBERS, H, W, C), jnp.float32)
    return stored_layout(0.25 * (base_draw + channel_offset) * channel_ramp * channel_rough).astype(jnp.bfloat16)


def steps_of(stream_key, extent, cuts, low, top_value):
    loudness, own = 1.0, jax.random.fold_in(stream_key, 6)
    for axis_at, shards_of in cuts:
        draws = jnp.exp(jax.random.uniform(jax.random.fold_in(own, axis_at), (shards_of,), jnp.float32, low / len(cuts), top_value / len(cuts)))
        loudness = loudness * jnp.repeat(draws, extent[axis_at] // shards_of).reshape([-1 if axis == axis_at else 1 for axis in range(len(extent))])
    return loudness


def scatter_about(rng, dims, scale, limit, cuts=(), held_as=jnp.bfloat16):
    loudness = steps_of(rng, dims, cuts, -0.22, 0.18) if cuts else 1.0
    entries = jax.random.normal(rng, dims, jnp.float32) * scale * loudness
    return jnp.minimum(jnp.maximum(entries, -limit), limit).astype(held_as)


def setup_inputs(seed: int = 0) -> dict:
    seeds = jax.random.split(jax.random.key(seed), 9)
    return {
        "members": draw_members(jax.random.fold_in(seeds[8], 71), 0),
        "gain": jnp.clip(0.5 + 1.0 * jax.random.uniform(seeds[1], (C,), jnp.float32) ** steps_of(seeds[1], (C,), ((0, 8),), -0.2, 0.2), 0.5, 1.5),
        "shift": scatter_about(seeds[2], (C,), 0.5, 3.0, ((0, 8),), jnp.float32),
        "w_first": scatter_about(seeds[3], (2, NB, CB, CB), (2 * CB) ** -0.5, 0.4375, ((1, 8),)),
        "b_first": scatter_about(seeds[4], (2, NB, CB), 0.5, 3.0, ((1, 8),), jnp.float32),
        "w_second": scatter_about(seeds[5], (2, NB, CB, CB), (2 * CB) ** -0.5, 0.4375, ((1, 8),)),
        "b_second": scatter_about(seeds[6], (2, NB, CB), 0.5, 3.0, ((1, 8),), jnp.float32),
        "cotangent": scatter_about(seeds[7], (MEMBERS, H, NB, W * CB), 1.0, 6.0, ((1, 32), (2, 8))),
    }


shrink_level = 0.05
norm_epsilon = 1e-05
gelu_scale = 0.7978845608
gelu_cubic = 0.044715

def gelu_value(values):
    inner = jnp.tanh(gelu_scale * (values + gelu_cubic * values * values * values))
    return 0.5 * values * (1.0 + inner)

def gelu_slope(values):
    inner = jnp.tanh(gelu_scale * (values + gelu_cubic * values * values * values))
    return 0.5 * (1.0 + inner) + 0.5 * values * (1.0 - inner * inner) * gelu_scale * (1.0 + 3.0 * gelu_cubic * values * values)

def shrink_value(values):
    return values - shrink_level * jnp.tanh(values / shrink_level)

def shrink_slope(values):
    inner = jnp.tanh(values / shrink_level)
    return inner * inner

def twiddle(length, columns):
    row_index = jnp.arange(length, dtype=jnp.int32)[:, None]
    col_index = jnp.arange(columns, dtype=jnp.int32)[None, :]
    angles = (row_index * col_index % length).astype(jnp.float32) * (2.0 * math.pi / length)
    return (jnp.cos(angles).astype(jnp.bfloat16), jnp.sin(angles).astype(jnp.bfloat16))

def product(pattern, first_op, second_op):
    return jnp.einsum(pattern, first_op.astype(jnp.float32), second_op.astype(jnp.float32))

def to_tokens(stored, width):
    lead = stored.shape[:2]
    groups = stored.shape[2]
    columns = stored.shape[3] // width
    split = stored.reshape(lead + (groups, columns, width))
    return jnp.transpose(split, (0, 1, 3, 2, 4)).reshape(lead + (columns, groups * width))

def to_stored(tokens, width):
    lead = tokens.shape[:2]
    columns = tokens.shape[2]
    groups = tokens.shape[3] // width
    split = tokens.reshape(lead + (columns, groups, width))
    return jnp.transpose(split, (0, 1, 3, 2, 4)).reshape(lead + (groups, columns * width))

def latitude_dft(real_part, imag_part, cos_lat, sin_lat, direction):
    factor = 1.0 / math.sqrt(real_part.shape[1])
    pattern = 'kh,bhmc->bkmc'
    out_real = factor * (product(pattern, cos_lat, real_part) - direction * product(pattern, sin_lat, imag_part))
    out_imag = factor * (product(pattern, cos_lat, imag_part) + direction * product(pattern, sin_lat, real_part))
    return (out_real, out_imag)

def as_blocks(values, width):
    return values.reshape(values.shape[:-1] + (values.shape[-1] // width, width))

def from_blocks(values):
    return values.reshape(values.shape[:-2] + (values.shape[-2] * values.shape[-1],))

def complex_apply(real_part, imag_part, weights):
    pattern = 'bkmnc,ncd->bkmnd'
    out_real = product(pattern, real_part, weights[0]) - product(pattern, imag_part, weights[1])
    out_imag = product(pattern, imag_part, weights[0]) + product(pattern, real_part, weights[1])
    return (out_real, out_imag)

def complex_back(real_in, imag_in, grad_real, grad_imag, weights):
    outer = 'bkmnc,bkmnd->ncd'
    grad_weight = jnp.stack([product(outer, real_in, grad_real) + product(outer, imag_in, grad_imag), product(outer, real_in, grad_imag) - product(outer, imag_in, grad_real)])
    grad_bias = jnp.stack([lax.optimization_barrier(jnp.sum(grad_real.astype(jnp.float32), axis=(0, 1, 2))), lax.optimization_barrier(jnp.sum(grad_imag.astype(jnp.float32), axis=(0, 1, 2)))])
    inner = 'bkmnd,ncd->bkmnc'
    back_real = product(inner, grad_real, weights[0]) + product(inner, grad_imag, weights[1])
    back_imag = product(inner, grad_imag, weights[0]) - product(inner, grad_real, weights[1])
    return (grad_weight, grad_bias, back_real, back_imag)

def spectral_forward(lat_real, lat_imag, w_first, b_first, w_second, b_second):
    pre_real, pre_imag = complex_apply(lat_real, lat_imag, w_first)
    pre_real = pre_real + b_first[0]
    pre_imag = pre_imag + b_first[1]
    hidden_real = gelu_value(pre_real).astype(jnp.bfloat16)
    hidden_imag = gelu_value(pre_imag).astype(jnp.bfloat16)
    post_real, post_imag = complex_apply(hidden_real, hidden_imag, w_second)
    post_real = post_real + b_second[0]
    post_imag = post_imag + b_second[1]
    shrunk_real = shrink_value(post_real).astype(jnp.bfloat16)
    shrunk_imag = shrink_value(post_imag).astype(jnp.bfloat16)
    return (shrunk_real, shrunk_imag, (pre_real, pre_imag, hidden_real, hidden_imag, post_real, post_imag))

def spectral_backward(lat_real, lat_imag, saved, grad_real, grad_imag, w_first, w_second):
    pre_real, pre_imag, hidden_real, hidden_imag, post_real, post_imag = saved
    grad_post_real = (grad_real * shrink_slope(post_real)).astype(jnp.bfloat16)
    grad_post_imag = (grad_imag * shrink_slope(post_imag)).astype(jnp.bfloat16)
    grad_w2, grad_b2, grad_hid_real, grad_hid_imag = complex_back(hidden_real, hidden_imag, grad_post_real, grad_post_imag, w_second)
    grad_pre_real = (grad_hid_real * gelu_slope(pre_real)).astype(jnp.bfloat16)
    grad_pre_imag = (grad_hid_imag * gelu_slope(pre_imag)).astype(jnp.bfloat16)
    grad_w1, grad_b1, grad_lat_real, grad_lat_imag = complex_back(lat_real, lat_imag, grad_pre_real, grad_pre_imag, w_first)
    return (grad_w1, grad_b1, grad_w2, grad_b2, grad_lat_real.astype(jnp.bfloat16), grad_lat_imag.astype(jnp.bfloat16))

def reference(members, gain, shift, w_first, b_first, w_second, b_second, cotangent):
    cos_lon, sin_lon = twiddle(W, MW)
    cos_lat, sin_lat = twiddle(H, H)
    lon_factor = 1.0 / math.sqrt(W)
    doubling = jnp.where(jnp.arange(MW) == 0, 1.0, 2.0)
    doubling_half = doubling.astype(jnp.bfloat16)[:, None]
    width = w_first.shape[-1]
    token_members = to_tokens(members, width)
    token_cotangent = to_tokens(cotangent, width)

    def member_step(totals, pair):
        sample, grad_out = pair
        sample = sample[None]
        grad_out = grad_out[None]
        wide = sample.astype(jnp.float32)
        mean_val = lax.optimization_barrier(jnp.sum(wide, -1, keepdims=True)) / C
        square_mean = lax.optimization_barrier(jnp.sum(wide * wide, -1, keepdims=True)) / C
        inv_std = lax.rsqrt(square_mean - mean_val * mean_val + norm_epsilon)
        centred = (wide - mean_val) * inv_std
        normed = (centred * gain + shift).astype(jnp.bfloat16)
        lon_real = (lon_factor * product('bhwc,wm->bhmc', normed, cos_lon)).astype(jnp.bfloat16)
        lon_imag = (-lon_factor * product('bhwc,wm->bhmc', normed, sin_lon)).astype(jnp.bfloat16)
        lat_real, lat_imag = latitude_dft(lon_real, lon_imag, cos_lat, sin_lat, -1.0)
        lat_real = as_blocks(lat_real.astype(jnp.bfloat16), width)
        lat_imag = as_blocks(lat_imag.astype(jnp.bfloat16), width)
        shrunk_real, shrunk_imag, saved = spectral_forward(lat_real, lat_imag, w_first, b_first, w_second, b_second)
        back_real, back_imag = latitude_dft(from_blocks(shrunk_real), from_blocks(shrunk_imag), cos_lat, sin_lat, 1.0)
        rows_real = back_real.astype(jnp.bfloat16) * doubling_half
        rows_imag = back_imag.astype(jnp.bfloat16) * doubling_half
        mixed = (lon_factor * (product('bhmc,wm->bhwc', rows_real, cos_lon) - product('bhmc,wm->bhwc', rows_imag, sin_lon))).astype(jnp.bfloat16)
        grad_back_real = (lon_factor * doubling[:, None] * product('bhwc,wm->bhmc', grad_out, cos_lon)).astype(jnp.bfloat16)
        grad_back_imag = (-lon_factor * doubling[:, None] * product('bhwc,wm->bhmc', grad_out, sin_lon)).astype(jnp.bfloat16)
        grad_shr_real, grad_shr_imag = latitude_dft(grad_back_real, grad_back_imag, cos_lat, sin_lat, -1.0)
        grad_shr_real = as_blocks(grad_shr_real.astype(jnp.bfloat16), width)
        grad_shr_imag = as_blocks(grad_shr_imag.astype(jnp.bfloat16), width)
        grad_w1, grad_b1, grad_w2, grad_b2, grad_lat_real, grad_lat_imag = spectral_backward(lat_real, lat_imag, saved, grad_shr_real, grad_shr_imag, w_first, w_second)
        grad_lon_real, grad_lon_imag = latitude_dft(from_blocks(grad_lat_real), from_blocks(grad_lat_imag), cos_lat, sin_lat, 1.0)
        grad_lon_real = grad_lon_real.astype(jnp.bfloat16)
        grad_lon_imag = grad_lon_imag.astype(jnp.bfloat16)
        grad_normed = lon_factor * (product('bhmc,wm->bhwc', grad_lon_real, cos_lon) - product('bhmc,wm->bhwc', grad_lon_imag, sin_lon))
        grad_gain = lax.optimization_barrier(jnp.sum(grad_normed * centred, axis=(0, 1, 2)))
        grad_shift = lax.optimization_barrier(jnp.sum(grad_normed, axis=(0, 1, 2)))
        grad_centred = grad_normed * gain
        first_mean = lax.optimization_barrier(jnp.sum(grad_centred, -1, keepdims=True)) / C
        second_mean = lax.optimization_barrier(jnp.sum(grad_centred * centred, -1, keepdims=True)) / C
        grad_in = (inv_std * (grad_centred - first_mean - centred * second_mean)).astype(jnp.bfloat16)
        updates = (grad_w1, grad_b1, grad_w2, grad_b2, grad_gain, grad_shift)
        totals = tuple((total + update for total, update in zip(totals, updates)))
        return (totals, (mixed[0], grad_in[0]))
    initial = (jnp.zeros(w_first.shape, jnp.float32), jnp.zeros(b_first.shape, jnp.float32), jnp.zeros(w_second.shape, jnp.float32), jnp.zeros(b_second.shape, jnp.float32), jnp.zeros(gain.shape, jnp.float32), jnp.zeros(shift.shape, jnp.float32))
    totals, outputs = lax.scan(member_step, initial, (token_members, token_cotangent))
    mixed_out = to_stored(outputs[0], width)
    grad_out_stored = to_stored(outputs[1], width)
    return (mixed_out, grad_out_stored, totals[0], totals[1], totals[2], totals[3], totals[4], totals[5])
```

```python
import math

import jax
import jax.numpy as jnp
import ml_dtypes
import numpy as np
from jax import lax
from jax.experimental import pallas as pl
from jax.experimental.pallas import tpu as pltpu
from jax.sharding import PartitionSpec as P

C = 768
CB = 96
W = 180
WP = 192
MW = 64
H = 96
NS = 32
NC = 8
HL = H // NS
LN = 128
QL = 4 * LN

shrink_level = 0.05
norm_epsilon = 1e-05
gelu_scale = 0.7978845608
gelu_cubic = 0.044715
lon_factor = 1.0 / math.sqrt(W)
lat_factor = 1.0 / math.sqrt(H)

F32 = jnp.float32
BF16 = jnp.bfloat16
MESH = pl.DeviceIdType.MESH

RS1, AG1, A2, A1, A4, A3, GWR, GWG, RS2, AG2, GG = range(11)


def twiddle(length, columns):
    rows = np.arange(length)[:, None]
    cols = np.arange(columns)[None, :]
    angles = (rows * cols % length).astype(np.float32) * np.float32(2.0 * math.pi / length)
    return (
        np.cos(angles).astype(np.float32),
        np.sin(angles).astype(np.float32),
    )


def tables():
    bf = ml_dtypes.bfloat16
    cos_lon, sin_lon = (t.astype(bf).astype(np.float32) for t in twiddle(W, MW))
    cos_lat, sin_lat = (t.astype(bf).astype(np.float32) for t in twiddle(H, H))
    lon = np.zeros((NS, 2, 2, 2, 2, WP), np.float32)
    scaled = np.zeros_like(lon)
    for d in range(NS):
        for mm in range(2):
            m = 2 * d + mm
            twice = 1.0 if m == 0 else 2.0
            for b in range(2):
                lon[d, 0, mm, b, b, :W] = cos_lon[:, m]
                lon[d, 1, mm, b, b, :W] = -sin_lon[:, m]
                scaled[d, :, mm, b] = twice * lon[d, :, mm, b]
    lon = lon.reshape(8 * NS, 2 * WP)
    scaled = scaled.reshape(8 * NS, 2 * WP)
    lat = np.zeros((HL, 2, 2, 2, H, NS, 2, 2, 2), np.float32)
    for hh in range(HL):
        cos_part = cos_lat[:, hh::HL]
        sin_part = sin_lat[:, hh::HL]
        for mm in range(2):
            for b in range(2):
                lat[hh, mm, b, 0, :, :, 0, mm, b] = cos_part
                lat[hh, mm, b, 0, :, :, 1, mm, b] = sin_part
                lat[hh, mm, b, 1, :, :, 0, mm, b] = -sin_part
                lat[hh, mm, b, 1, :, :, 1, mm, b] = cos_part
    lat = lat.reshape(HL, 8 * H, 8 * NS)
    return (
        np.stack([lon, scaled]).astype(bf),
        np.stack([lon.T, scaled.T]).astype(bf),
        lat.astype(bf),
        np.swapaxes(lat, 1, 2).astype(bf),
    )


def dot(left, right):
    return lax.dot_general(left, right, (((1,), (0,)), ((), ())), preferred_element_type=F32)


def dot_nt(left, right):
    return lax.dot_general(left, right, (((1,), (1,)), ((), ())), preferred_element_type=F32)


def dot_tn(left, right):
    return lax.dot_general(left, right, (((0,), (0,)), ((), ())), preferred_element_type=F32)


def unpack(source, target, h):
    lane = lax.broadcasted_iota(jnp.int32, (8, LN), 1)

    def step(it, carry):
        for u in range(15):
            i = it * 15 + u
            chunk = source[h, 0, :, pl.ds(pl.multiple_of(i * 384, 128), 384)].astype(F32)
            v0, v1, v2 = chunk[:, :128], chunk[:, 128:256], chunk[:, 256:]
            parts = (
                v0,
                pltpu.roll(jnp.where(lane >= 96, v0, v1), 32, 1),
                pltpu.roll(jnp.where(lane >= 64, v1, v2), 64, 1),
                pltpu.roll(v2, 96, 1),
            )
            for q in range(4):
                target[h, pl.ds(pl.multiple_of(i * 32 + 8 * q, 8), 8), :] = jnp.where(
                    lane < CB, parts[q], 0.0
                )
        return carry

    lax.fori_loop(0, 3, step, 0)


def pack(source, target, h):
    lane = lax.broadcasted_iota(jnp.int32, (8, LN), 1)

    def step(it, carry):
        for u in range(15):
            i = it * 15 + u
            p0, p1, p2, p3 = (
                source[h, pl.ds(pl.multiple_of(i * 32 + 8 * q, 8), 8), :] for q in range(4)
            )
            r1 = pltpu.roll(p1, 96, 1)
            r2 = pltpu.roll(p2, 64, 1)
            r3 = pltpu.roll(p3, 32, 1)
            chunk = jnp.concatenate(
                [
                    jnp.where(lane < 96, p0, r1),
                    jnp.where(lane < 64, r1, r2),
                    jnp.where(lane < 32, r2, r3),
                ],
                axis=1,
            )
            target[h, 0, :, pl.ds(pl.multiple_of(i * 384, 128), 384)] = chunk.astype(BF16)
        return carry

    lax.fori_loop(0, 3, step, 0)


def layer(
    x_hbm, cot_hbm, gain_ref, shift_ref, w1_ref, b1_ref, w2_ref, b2_ref,
    d_hbm, e_hbm, l_hbm, m_hbm,
    mixed_hbm, gin_hbm, gw1_ref, gb1_ref, gw2_ref, gb2_ref, gg_ref, gs_ref,
    xv, cv, dv, ev, lv, mv, tx, tc, xn, cen, gc,
    send1, send2, send3, send4, recv1, recv2, recv3, recv4, rc,
    lt, gsh, hid, gpost, gpre, sh, glat, wc, vec,
    acc, st, rb, ags, ab, at, st2, rb2, ags2, ab2, at2,
    gb, gr, gas, ga, ggs, ggr,
    in_sems, out_sems, send_sems, recv_sems,
):
    me_s = lax.axis_index("space")
    me_c = lax.axis_index("chan")

    loads = [pltpu.make_async_copy(x_hbm.at[h], xv.at[h], in_sems.at[h]) for h in range(HL)]
    loads += [pltpu.make_async_copy(cot_hbm.at[h], cv.at[h], in_sems.at[3 + h]) for h in range(HL)]
    loads += [
        pltpu.make_async_copy(d_hbm, dv, in_sems.at[6]),
        pltpu.make_async_copy(e_hbm, ev, in_sems.at[7]),
        pltpu.make_async_copy(l_hbm, lv, in_sems.at[8]),
        pltpu.make_async_copy(m_hbm, mv, in_sems.at[9]),
    ]
    for load in loads:
        load.start()

    barrier = pltpu.get_barrier_semaphore()

    def greet_space(r, carry):
        pl.semaphore_signal(
            barrier, inc=1, device_id={"space": lax.rem(me_s + r, NS)}, device_id_type=MESH
        )
        return carry

    def greet_chan(r, carry):
        pl.semaphore_signal(
            barrier, inc=1, device_id={"chan": lax.rem(me_c + r, NC)}, device_id_type=MESH
        )
        return carry

    lax.fori_loop(1, NC, greet_chan, 0)
    lax.fori_loop(1, NS, greet_space, 0)

    def spread(axis, index, piece, target):
        count, me = (NS, me_s) if axis == "space" else (NC, me_c)

        def step(r, carry):
            t = lax.rem(me + r, count)
            pltpu.make_async_remote_copy(
                src_ref=piece(t),
                dst_ref=target.at[me],
                send_sem=send_sems.at[index],
                recv_sem=recv_sems.at[index],
                device_id={axis: t},
                device_id_type=MESH,
            ).start()
            return carry

        lax.fori_loop(1, count, step, 0)
        pltpu.make_async_copy(piece(me), target.at[me], recv_sems.at[index]).start()

    def arrived(index, target):
        pltpu.make_async_copy(target, target, recv_sems.at[index]).wait()

    def sent(index, target, count):
        rest = target.at[pl.ds(0, count - 1)]
        pltpu.make_async_copy(rest, rest, send_sems.at[index]).wait()

    vec[...] = jnp.zeros_like(vec)
    vec[0:1, 0:CB] = gain_ref[...]
    vec[1:2, 0:CB] = shift_ref[...]
    for layer_at, (b_ref, w_ref) in enumerate(((b1_ref, w1_ref), (b2_ref, w2_ref))):
        vec[2 + layer_at : 3 + layer_at, 0:CB] = b_ref[0]
        vec[2 + layer_at : 3 + layer_at, LN : LN + CB] = b_ref[1]
        wc[layer_at] = jnp.zeros((2 * LN, 2 * LN), BF16)
        w_real, w_imag = w_ref[0, 0], w_ref[1, 0]
        wc[layer_at, 0:CB, 0:CB] = w_real
        wc[layer_at, 0:CB, LN : LN + CB] = w_imag
        wc[layer_at, LN : LN + CB, 0:CB] = -w_imag
        wc[layer_at, LN : LN + CB, LN : LN + CB] = w_real
    tx[:, 8 * W :, :] = jnp.zeros((HL, 8 * (WP - W), LN), F32)
    tc[:, 8 * W :, :] = jnp.zeros((HL, 8 * (WP - W), LN), F32)
    acc[...] = jnp.zeros_like(acc)
    ab[NC:] = jnp.zeros((NC, 8, 256), F32)
    ab2[NC:] = jnp.zeros((NC, 8, 256), F32)

    lane_w = lax.broadcasted_iota(jnp.int32, (WP, LN), 1)

    def members_of(array, h, b):
        return array[h, pl.ds(b, WP, stride=8), :]

    def pieces_of_sums(target):
        for hi in range(2):
            turned = jnp.transpose(acc[hi])
            for lo in range(4):
                target[4 * hi + lo] = turned[8 * lo : 8 * lo + 8, :]

    for h in range(HL):
        loads[h].wait()
        unpack(xv, tx, h)
    for hi in range(2):
        total = jnp.zeros((WP, LN), F32)
        for lo in range(4):
            for h in range(HL):
                tile = members_of(tx, h, 4 * hi + lo)
                one = jnp.sum(tile, axis=1, keepdims=True)
                two = jnp.sum(tile * tile, axis=1, keepdims=True)
                total = jnp.where(lane_w == 8 * lo + h, one, total)
                total = jnp.where(lane_w == 8 * lo + 3 + h, two, total)
        acc[hi, 0:WP, :] = total
    pieces_of_sums(st)
    pl.semaphore_wait(barrier, NS - 1 + NC - 1)
    spread("chan", RS1, lambda t: st.at[t], rb)

    for h in range(HL):
        loads[3 + h].wait()
        unpack(cv, tc, h)
    loads[6].wait()
    for h in range(HL):
        for b in range(8):
            hi, lo = divmod(b, 4)
            xn[h, WP * hi : WP * hi + WP, LN * lo : LN * lo + LN] = members_of(tc, h, b).astype(
                BF16
            )
        out = dot(dv[1], xn[h]) * lon_factor
        send2[:, :, QL * h : QL * h + QL] = out.reshape(NS, 8, QL).astype(BF16)

    arrived(RS1, rb)
    sums = jnp.sum(rb[...], axis=0) * (1.0 / C)
    mean = sums
    var_in = pltpu.roll(sums, 5, 0)
    inv = lax.rsqrt(var_in - mean * mean + norm_epsilon)
    row8 = lax.broadcasted_iota(jnp.int32, (8, 256), 0)
    ags[...] = jnp.where(row8 < 3, mean, jnp.where(row8 < 6, pltpu.roll(inv, 3, 0), 0.0))
    spread("chan", AG1, lambda t: ags, ab)
    spread("space", A2, lambda t: send2.at[t], recv2)

    arrived(AG1, ab.at[pl.ds(0, NC)])
    at[...] = jnp.transpose(ab[...].reshape(2 * NC * 8, 256))
    gain_row = vec[0:1, 0:LN]
    shift_row = vec[1:2, 0:LN]
    for h in range(HL):
        for b in range(8):
            hi, lo = divmod(b, 4)
            mean_col = at[0:WP, 8 * b + h : 8 * b + h + 1]
            inv_col = at[0:WP, 8 * b + 3 + h : 8 * b + 4 + h]
            centred = (members_of(tx, h, b) - mean_col) * inv_col
            rows, lanes = pl.ds(WP * hi, WP), pl.ds(LN * lo, LN)
            cen[h, rows, lanes] = centred
            xn[h, rows, lanes] = (centred * gain_row + shift_row).astype(BF16)
        out = dot(dv[0], xn[h]) * lon_factor
        send1[:, :, QL * h : QL * h + QL] = out.reshape(NS, 8, QL).astype(BF16)
    spread("space", A1, lambda t: send1.at[t], recv1)

    def latitude(received, target, ones):
        lane = lax.broadcasted_iota(jnp.int32, (H, LN), 1)
        for h in range(HL):
            rc[h] = received[:, :, QL * h : QL * h + QL].reshape(8 * NS, QL)

        def step(g, carry):
            rows = pl.ds(pl.multiple_of(g * 192, 192), 192)
            out = dot(lv[0, rows, :], rc[0])
            for h in range(1, HL):
                out = out + dot(lv[h, rows, :], rc[h])
            out = out * lat_factor
            for part in range(2):
                for lo in range(4):
                    tile = out[H * part : H * part + H, LN * lo : LN * lo + LN]
                    if ones and part == 0:
                        tile = jnp.where(lane == CB, 1.0, tile)
                    target[g, H * lo : H * lo + H, LN * part : LN * part + LN] = tile.astype(BF16)
            return carry

        lax.fori_loop(0, 4, step, 0)

    loads[8].wait()
    arrived(A2, recv2)
    latitude(recv2, gsh, False)
    arrived(A1, recv1)
    latitude(recv1, lt, True)

    def mix(g, carry):
        lane = lax.broadcasted_iota(jnp.int32, (4 * H, 2 * LN), 1)
        pre = dot(lt[g], wc[0]) + vec[2:3, :]
        t = jnp.tanh(gelu_scale * (pre + gelu_cubic * pre * pre * pre))
        hidden = 0.5 * pre * (1.0 + t)
        hidden = jnp.where(lane == CB, 1.0, hidden).astype(BF16)
        slope = 0.5 * (1.0 + t) + 0.5 * pre * (1.0 - t * t) * gelu_scale * (
            1.0 + 3.0 * gelu_cubic * pre * pre
        )
        hid[g] = hidden
        post = dot(hidden, wc[1]) + vec[3:4, :]
        s = jnp.tanh(post * (1.0 / shrink_level))
        shrunk = (post - shrink_level * s).astype(BF16)
        grad_post = (gsh[g].astype(F32) * (s * s)).astype(BF16)
        gpost[g] = grad_post
        grad_pre = (dot_nt(grad_post, wc[1]) * slope).astype(BF16)
        gpre[g] = grad_pre
        grad_lat = dot_nt(grad_pre, wc[0]).astype(BF16)
        for part in range(2):
            for lo in range(4):
                rows, lanes = slice(H * part, H * part + H), slice(LN * lo, LN * lo + LN)
                from_rows = slice(H * lo, H * lo + H)
                from_lanes = slice(LN * part, LN * part + LN)
                sh[g, rows, lanes] = shrunk[from_rows, from_lanes]
                glat[g, rows, lanes] = grad_lat[from_rows, from_lanes]
        return carry

    lax.fori_loop(0, 4, mix, 0)

    def back(source, target):
        spectrum = source[...].reshape(8 * H, QL)
        for h in range(HL):
            out = dot(mv[h], spectrum) * lat_factor
            target[:, :, QL * h : QL * h + QL] = out.reshape(NS, 8, QL).astype(BF16)

    loads[9].wait()
    back(glat, send4)
    spread("space", A4, lambda t: send4.at[t], recv4)
    back(sh, send3)
    spread("space", A3, lambda t: send3.at[t], recv3)

    for layer_at, (left, right) in enumerate(((lt, gpre), (hid, gpost))):
        outer = dot_tn(left[...].reshape(16 * H, 2 * LN), right[...].reshape(16 * H, 2 * LN))
        real = outer[0:LN, 0:LN] + outer[LN:, LN:]
        imag = outer[0:LN, LN:] - outer[LN:, 0:LN]
        gb[16 * layer_at : 16 * layer_at + 8] = real.reshape(8, 16, LN).astype(BF16)
        gb[16 * layer_at + 8 : 16 * layer_at + 16] = imag.reshape(8, 16, LN).astype(BF16)
    spread("space", GWR, lambda t: gb.at[t], gr)

    loads[7].wait()
    arrived(A4, recv4)
    gain_sum = jnp.zeros((8, LN), F32)
    shift_sum = jnp.zeros((8, LN), F32)
    totals = [jnp.zeros((WP, LN), F32), jnp.zeros((WP, LN), F32)]
    for h in range(HL):
        out = dot(ev[0], recv4[:, :, QL * h : QL * h + QL].reshape(8 * NS, QL)) * lon_factor
        for b in range(8):
            hi, lo = divmod(b, 4)
            rows, lanes = slice(WP * hi, WP * hi + WP), slice(LN * lo, LN * lo + LN)
            grad_normed = out[rows, lanes]
            centred = cen[h, rows, lanes]
            gain_sum = gain_sum + jnp.sum((grad_normed * centred).reshape(WP // 8, 8, LN), axis=0)
            shift_sum = shift_sum + jnp.sum(grad_normed.reshape(WP // 8, 8, LN), axis=0)
            grad_centred = grad_normed * gain_row
            gc[h, rows, lanes] = grad_centred
            one = jnp.sum(grad_centred, axis=1, keepdims=True)
            two = jnp.sum(grad_centred * centred, axis=1, keepdims=True)
            totals[hi] = jnp.where(lane_w == 8 * lo + h, one, totals[hi])
            totals[hi] = jnp.where(lane_w == 8 * lo + 3 + h, two, totals[hi])
    for hi in range(2):
        acc[hi, 0:WP, :] = totals[hi]
    pieces_of_sums(st2)
    spread("chan", RS2, lambda t: st2.at[t], rb2)
    ggs[0:1, :] = jnp.sum(gain_sum, axis=0, keepdims=True)
    ggs[1:2, :] = jnp.sum(shift_sum, axis=0, keepdims=True)
    spread("space", GG, lambda t: ggs, ggr)

    arrived(GWR, gr)
    gas[...] = jnp.sum(gr[...].astype(F32), axis=0).astype(BF16)
    spread("space", GWG, lambda t: gas, ga)

    arrived(A3, recv3)
    stores = []

    def put_mixed(h):
        out = dot(ev[1], recv3[:, :, QL * h : QL * h + QL].reshape(8 * NS, QL)) * lon_factor
        for b in range(8):
            hi, lo = divmod(b, 4)
            tc[h, pl.ds(b, WP, stride=8), :] = out[
                WP * hi : WP * hi + WP, LN * lo : LN * lo + LN
            ]
        pack(tc, cv, h)
        store = pltpu.make_async_copy(cv.at[h], mixed_hbm.at[h], out_sems.at[h])
        store.start()
        stores.append(store)

    put_mixed(0)
    arrived(RS2, rb2)
    ags2[...] = jnp.sum(rb2[...], axis=0) * (1.0 / C)
    spread("chan", AG2, lambda t: ags2, ab2)
    put_mixed(1)
    put_mixed(2)

    arrived(AG2, ab2.at[pl.ds(0, NC)])
    at2[...] = jnp.transpose(ab2[...].reshape(2 * NC * 8, 256))
    for h in range(HL):
        for b in range(8):
            hi, lo = divmod(b, 4)
            rows, lanes = slice(WP * hi, WP * hi + WP), slice(LN * lo, LN * lo + LN)
            inv_col = at[0:WP, 8 * b + 3 + h : 8 * b + 4 + h]
            first = at2[0:WP, 8 * b + h : 8 * b + h + 1]
            second = at2[0:WP, 8 * b + 3 + h : 8 * b + 4 + h]
            tx[h, pl.ds(b, WP, stride=8), :] = inv_col * (
                gc[h, rows, lanes] - first - cen[h, rows, lanes] * second
            )
        pack(tx, xv, h)
        store = pltpu.make_async_copy(xv.at[h], gin_hbm.at[h], out_sems.at[3 + h])
        store.start()
        stores.append(store)

    arrived(GG, ggr)
    both = jnp.sum(ggr[...], axis=0)
    gg_ref[...] = both[0:1, 0:CB]
    gs_ref[...] = both[1:2, 0:CB]
    arrived(GWG, ga)
    for layer_at, (gw_ref, gbias_ref) in enumerate(((gw1_ref, gb1_ref), (gw2_ref, gb2_ref))):
        for part in range(2):
            at_piece = 16 * layer_at + 8 * part
            block = ga[at_piece : at_piece + 8].astype(F32).reshape(LN, LN)
            gw_ref[part, 0] = block[0:CB, 0:CB]
            gbias_ref[part] = block[CB : CB + 1, 0:CB]

    sent(RS1, rb, NC)
    sent(AG1, ab, NC)
    sent(RS2, rb2, NC)
    sent(AG2, ab2, NC)
    sent(A2, recv2, NS)
    sent(A1, recv1, NS)
    sent(A4, recv4, NS)
    sent(A3, recv3, NS)
    sent(GWR, gr, NS)
    sent(GWG, ga, NS)
    sent(GG, ggr, NS)
    for store in stores:
        store.wait()


def on_device(members, gain, shift, w_first, b_first, w_second, b_second, cotangent):
    lon_out, lon_back, lat_out, lat_back = (jnp.asarray(t) for t in tables())
    anywhere = pl.BlockSpec(memory_space=pl.ANY)
    vmem = pl.BlockSpec(memory_space=pltpu.VMEM)
    token = (HL, 1, 8, W * CB)
    piece = (NS, 8, HL * QL)
    spectral = (4, 4 * H, 2 * LN)
    folded = (4, 2 * H, QL)
    outs = pl.pallas_call(
        layer,
        out_shape=(
            jax.ShapeDtypeStruct(token, BF16),
            jax.ShapeDtypeStruct(token, BF16),
            jax.ShapeDtypeStruct((2, 1, CB, CB), F32),
            jax.ShapeDtypeStruct((2, 1, CB), F32),
            jax.ShapeDtypeStruct((2, 1, CB, CB), F32),
            jax.ShapeDtypeStruct((2, 1, CB), F32),
            jax.ShapeDtypeStruct((1, CB), F32),
            jax.ShapeDtypeStruct((1, CB), F32),
        ),
        in_specs=[anywhere] * 2 + [vmem] * 6 + [anywhere] * 4,
        out_specs=tuple([anywhere] * 2 + [vmem] * 6),
        scratch_shapes=[
            pltpu.VMEM(token, BF16),
            pltpu.VMEM(token, BF16),
            pltpu.VMEM((2, 8 * NS, 2 * WP), BF16),
            pltpu.VMEM((2, 2 * WP, 8 * NS), BF16),
            pltpu.VMEM((HL, 8 * H, 8 * NS), BF16),
            pltpu.VMEM((HL, 8 * NS, 8 * H), BF16),
            pltpu.VMEM((HL, 8 * WP, LN), F32),
            pltpu.VMEM((HL, 8 * WP, LN), F32),
            pltpu.VMEM((HL, 2 * WP, QL), BF16),
            pltpu.VMEM((HL, 2 * WP, QL), F32),
            pltpu.VMEM((HL, 2 * WP, QL), F32),
        ]
        + [pltpu.VMEM(piece, BF16)] * 8
        + [pltpu.VMEM((HL, 8 * NS, QL), BF16)]
        + [pltpu.VMEM(spectral, BF16)] * 5
        + [pltpu.VMEM(folded, BF16)] * 2
        + [
            pltpu.VMEM((2, 2 * LN, 2 * LN), BF16),
            pltpu.VMEM((8, 2 * LN), F32),
            pltpu.VMEM((2, 256, LN), F32),
        ]
        + [
            pltpu.VMEM((NC, 8, 256), F32),
            pltpu.VMEM((NC, 8, 256), F32),
            pltpu.VMEM((8, 256), F32),
            pltpu.VMEM((2 * NC, 8, 256), F32),
            pltpu.VMEM((256, 2 * NC * 8), F32),
        ]
        * 2
        + [
            pltpu.VMEM((NS, 16, LN), BF16),
            pltpu.VMEM((NS, 16, LN), BF16),
            pltpu.VMEM((16, LN), BF16),
            pltpu.VMEM((NS, 16, LN), BF16),
            pltpu.VMEM((2, LN), F32),
            pltpu.VMEM((NS, 2, LN), F32),
            pltpu.SemaphoreType.DMA((10,)),
            pltpu.SemaphoreType.DMA((6,)),
            pltpu.SemaphoreType.DMA((11,)),
            pltpu.SemaphoreType.DMA((11,)),
        ],
        compiler_params=pltpu.CompilerParams(
            collective_id=0, has_side_effects=True, vmem_limit_bytes=56 * 1024 * 1024
        ),
    )(
        jnp.transpose(members, (1, 2, 0, 3)),
        jnp.transpose(cotangent, (1, 2, 0, 3)),
        gain.reshape(1, CB),
        shift.reshape(1, CB),
        w_first,
        b_first,
        w_second,
        b_second,
        lon_out,
        lon_back,
        lat_out,
        lat_back,
    )
    mixed, grad_input, gw1, gb1, gw2, gb2, gg, gs = outs
    return (
        jnp.transpose(mixed, (2, 0, 1, 3)),
        jnp.transpose(grad_input, (2, 0, 1, 3)),
        gw1,
        gb1,
        gw2,
        gb2,
        gg.reshape(CB),
        gs.reshape(CB),
    )


def solution(mesh):
    placed = (
        P(None, "space", "chan", None),
        P("chan"),
        P("chan"),
        P(None, "chan", None, None),
        P(None, "chan", None),
        P(None, "chan", None, None),
        P(None, "chan", None),
        P(None, "space", "chan", None),
    )
    return jax.shard_map(
        on_device,
        mesh=mesh,
        in_specs=placed,
        out_specs=(
            P(None, "space", "chan", None),
            P(None, "space", "chan", None),
            P(None, "chan", None, None),
            P(None, "chan", None),
            P(None, "chan", None, None),
            P(None, "chan", None),
            P("chan"),
            P("chan"),
        ),
        check_vma=False,
    )
```

```python
import math

import jax
import jax.numpy as jnp
import ml_dtypes
import numpy as np
from jax import lax
from jax.experimental import pallas as pl
from jax.experimental.pallas import tpu as pltpu
from jax.sharding import PartitionSpec as P

C = 768
CB = 96
W = 180
WP = 192
MW = 64
H = 96
NS = 32
NC = 8
HL = H // NS
LN = 128
PL = 5 * LN
HB = 2 * CB

shrink_level = 0.05
norm_epsilon = 1e-05
gelu_scale = 0.7978845608
gelu_cubic = 0.044715
lon_factor = 1.0 / math.sqrt(W)
lat_factor = 1.0 / math.sqrt(H)

F32 = jnp.float32
BF16 = jnp.bfloat16
MESH = pl.DeviceIdType.MESH

RS1, AG1, A2, A1, A4, A3, RS2, AG2 = range(0, 16, 2)
GWR, GWG, GG = range(16, 19)


def twiddle(length, columns):
    rows = np.arange(length)[:, None]
    cols = np.arange(columns)[None, :]
    angles = (rows * cols % length).astype(np.float32) * np.float32(2.0 * math.pi / length)
    return (
        np.cos(angles).astype(np.float32),
        np.sin(angles).astype(np.float32),
    )


def tables():
    bf = ml_dtypes.bfloat16
    cos_lon, sin_lon = (t.astype(bf).astype(np.float32) for t in twiddle(W, MW))
    cos_lat, sin_lat = (t.astype(bf).astype(np.float32) for t in twiddle(H, H))
    lon = np.zeros((NS, 2, 2, 2, 2, WP), np.float32)
    scaled = np.zeros_like(lon)
    for d in range(NS):
        for mm in range(2):
            m = 2 * d + mm
            twice = 1.0 if m == 0 else 2.0
            for b in range(2):
                lon[d, 0, mm, b, b, :W] = cos_lon[:, m]
                lon[d, 1, mm, b, b, :W] = -sin_lon[:, m]
                scaled[d, :, mm, b] = twice * lon[d, :, mm, b]
    lon = lon.reshape(8 * NS, 2 * WP)
    scaled = scaled.reshape(8 * NS, 2 * WP)
    lat = np.zeros((HL, 2, 2, 2, H, NS, 2, 2, 2), np.float32)
    for hh in range(HL):
        cos_part = cos_lat[:, hh::HL]
        sin_part = sin_lat[:, hh::HL]
        for mm in range(2):
            for b in range(2):
                lat[hh, mm, b, 0, :, :, 0, mm, b] = cos_part
                lat[hh, mm, b, 0, :, :, 1, mm, b] = sin_part
                lat[hh, mm, b, 1, :, :, 0, mm, b] = -sin_part
                lat[hh, mm, b, 1, :, :, 1, mm, b] = cos_part
    lat = lat.reshape(HL, 8 * H, 8 * NS)
    return (
        np.stack([lon, scaled]).astype(bf),
        np.stack([lon.T, scaled.T]).astype(bf),
        lat.astype(bf),
        np.swapaxes(lat, 1, 2).astype(bf),
    )


def dot(left, right):
    return lax.dot_general(left, right, (((1,), (0,)), ((), ())), preferred_element_type=F32)


def dot_nt(left, right):
    return lax.dot_general(left, right, (((1,), (1,)), ((), ())), preferred_element_type=F32)


def dot_tn(left, right):
    return lax.dot_general(left, right, (((0,), (0,)), ((), ())), preferred_element_type=F32)


def unpack(source, target, h):
    lane = lax.broadcasted_iota(jnp.int32, (8, LN), 1)

    def step(it, carry):
        for u in range(15):
            i = it * 15 + u
            chunk = source[h, 0, :, pl.ds(pl.multiple_of(i * 384, 128), 384)].astype(F32)
            v0, v1, v2 = chunk[:, :128], chunk[:, 128:256], chunk[:, 256:]
            parts = (
                v0,
                pltpu.roll(jnp.where(lane >= 96, v0, v1), 32, 1),
                pltpu.roll(jnp.where(lane >= 64, v1, v2), 64, 1),
                pltpu.roll(v2, 96, 1),
            )
            for q in range(4):
                target[h, pl.ds(pl.multiple_of(i * 32 + 8 * q, 8), 8), :] = parts[q]
        return carry

    lax.fori_loop(0, 3, step, 0)


def pack(source, target, h):
    lane = lax.broadcasted_iota(jnp.int32, (8, LN), 1)

    def step(it, carry):
        for u in range(15):
            i = it * 15 + u
            p0, p1, p2, p3 = (
                source[h, pl.ds(pl.multiple_of(i * 32 + 8 * q, 8), 8), :] for q in range(4)
            )
            r1 = pltpu.roll(p1, 96, 1)
            r2 = pltpu.roll(p2, 64, 1)
            r3 = pltpu.roll(p3, 32, 1)
            chunk = jnp.concatenate(
                [
                    jnp.where(lane < 96, p0, r1),
                    jnp.where(lane < 64, r1, r2),
                    jnp.where(lane < 32, r2, r3),
                ],
                axis=1,
            )
            target[h, 0, :, pl.ds(pl.multiple_of(i * 384, 128), 384)] = chunk.astype(BF16)
        return carry

    lax.fori_loop(0, 3, step, 0)


def layer(
    x_hbm, cot_hbm, gain_ref, shift_ref, w1_ref, b1_ref, w2_ref, b2_ref,
    d_hbm, e_hbm, l_hbm, m_hbm,
    mixed_out, gin_out, gw1_ref, gb1_ref, gw2_ref, gb2_ref, gg_ref, gs_ref,
    xv, cv, dv, ev, lv, mv, tx, tc, xn, cen, gc,
    send1, send2, send3, send4, recv1, recv2, recv3, recv4,
    lt, gsh, hid, gpost, gpre, sh, glat, wc, vec,
    acc, st, rb, ags, ab, at, acc2, st2, rb2, ags2, ab2, at2,
    gb, gr, gas, ga, ggs, ggr,
    in_sems, send_sems, recv_sems,
):
    me_s = lax.axis_index("space")
    me_c = lax.axis_index("chan")

    loads = [pltpu.make_async_copy(x_hbm.at[h], xv.at[h], in_sems.at[h]) for h in range(HL)]
    loads += [pltpu.make_async_copy(cot_hbm.at[h], cv.at[h], in_sems.at[3 + h]) for h in range(HL)]
    loads += [
        pltpu.make_async_copy(d_hbm, dv, in_sems.at[6]),
        pltpu.make_async_copy(e_hbm, ev, in_sems.at[7]),
        pltpu.make_async_copy(l_hbm, lv, in_sems.at[8]),
        pltpu.make_async_copy(m_hbm, mv, in_sems.at[9]),
    ]
    for load in loads:
        load.start()

    barrier = pltpu.get_barrier_semaphore()

    def greet_space(r, carry):
        pl.semaphore_signal(
            barrier, inc=1, device_id={"space": lax.rem(me_s + r, NS)}, device_id_type=MESH
        )
        return carry

    def greet_chan(r, carry):
        pl.semaphore_signal(
            barrier, inc=1, device_id={"chan": lax.rem(me_c + r, NC)}, device_id_type=MESH
        )
        return carry

    lax.fori_loop(1, NC, greet_chan, 0)
    lax.fori_loop(1, NS, greet_space, 0)

    def spread(axis, index, piece, target):
        count, me = (NS, me_s) if axis == "space" else (NC, me_c)

        def step(r, carry):
            t = lax.rem(me + r, count)
            pltpu.make_async_remote_copy(
                src_ref=piece(t),
                dst_ref=target.at[me],
                send_sem=send_sems.at[index],
                recv_sem=recv_sems.at[index],
                device_id={axis: t},
                device_id_type=MESH,
            ).start()
            return carry

        lax.fori_loop(1, count, step, 0)
        pltpu.make_async_copy(piece(me), target.at[me], recv_sems.at[index]).start()

    def arrived(index, target):
        pltpu.make_async_copy(target, target, recv_sems.at[index]).wait()

    def sent(index, target, count):
        rest = target.at[pl.ds(0, count - 1)]
        pltpu.make_async_copy(rest, rest, send_sems.at[index]).wait()

    vec[...] = jnp.zeros_like(vec)
    vec[0:1, 0:CB] = gain_ref[...]
    vec[1:2, 0:CB] = shift_ref[...]
    for layer_at, (b_ref, w_ref) in enumerate(((b1_ref, w1_ref), (b2_ref, w2_ref))):
        vec[2 + layer_at : 3 + layer_at, 0:CB] = b_ref[0]
        vec[2 + layer_at : 3 + layer_at, LN : LN + CB] = b_ref[1]
        wc[layer_at] = jnp.zeros((2 * LN, 2 * LN), BF16)
        w_real, w_imag = w_ref[0, 0], w_ref[1, 0]
        wc[layer_at, 0:CB, 0:CB] = w_real
        wc[layer_at, 0:CB, LN : LN + CB] = w_imag
        wc[layer_at, LN : LN + CB, 0:CB] = -w_imag
        wc[layer_at, LN : LN + CB, LN : LN + CB] = w_real
    tx[:, 8 * W :, :] = jnp.zeros((HL, 8 * (WP - W), LN), F32)
    tc[:, 8 * W :, :] = jnp.zeros((HL, 8 * (WP - W), LN), F32)
    acc[...] = jnp.zeros_like(acc)
    acc2[...] = jnp.zeros_like(acc2)
    ab[:, NC:] = jnp.zeros((2, NC, 8, LN), F32)
    ab2[:, NC:] = jnp.zeros((2, NC, 8, LN), F32)
    lane_t = lax.broadcasted_iota(jnp.int32, (4 * H, 2 * LN), 1)
    for s in range(2):
        send3[s, :, :, PL - LN :] = jnp.zeros((NS, 8, LN), BF16)
        send4[s, :, :, PL - LN :] = jnp.zeros((NS, 8, LN), BF16)
        for g in range(2):
            lt[s, g] = jnp.where(lane_t == CB, 1.0, 0.0).astype(BF16)
            gsh[s, g] = jnp.zeros((4 * H, 2 * LN), BF16)

    lane_w = lax.broadcasted_iota(jnp.int32, (WP, LN), 1)
    gain_row = vec[0:1, 0:LN]
    shift_row = vec[1:2, 0:LN]

    def members_of(array, h, b):
        return array[h, pl.ds(b, WP, stride=8), :]

    def pair_of(m):
        return m // 2, m % 2

    def dense(tiles):
        t0, t1, t2, t3, t4, t5 = tiles
        r1, r2, r3 = pltpu.roll(t1, 96, 1), pltpu.roll(t2, 64, 1), pltpu.roll(t3, 32, 1)
        r5 = pltpu.roll(t5, 96, 1)
        return (
            jnp.where(lane_w < 96, t0, r1),
            jnp.where(lane_w < 64, r1, r2),
            jnp.where(lane_w < 32, r2, r3),
            jnp.where(lane_w < 96, t4, r5),
            jnp.where(lane_w < 64, r5, 0.0),
        )

    def tile_of(array, h, m):
        pair, one = pair_of(m)
        rows = slice(WP * pair, WP * pair + WP)
        start = HB * h + CB * one
        first, shift = start // LN * LN, start % LN
        left = array[rows, first : first + LN]
        if shift == 0:
            return left
        if shift > 32:
            right = array[rows, first + LN : first + 2 * LN]
            left = jnp.where(lane_w >= shift, left, right)
        return pltpu.roll(left, LN - shift, 1)

    def store_dense(s, pair, tiles):
        for i, column in enumerate(dense(tiles)):
            xn[s, WP * pair : WP * pair + WP, LN * i : LN * i + LN] = column.astype(BF16)

    def pieces_of_sums(source, target):
        turned = jnp.transpose(source[...])
        for part in range(2):
            for m in range(4):
                target[4 * part + m] = turned[8 * m : 8 * m + 8, LN * part : LN * part + LN]

    def columns_of(source, target):
        turned = jnp.transpose(source[...].reshape(LN, LN))
        target[0:LN, 0:32] = turned[:, 0:32]
        target[LN:, 0:32] = turned[:, 32:64]

    for h in range(HL):
        loads[h].wait()
        unpack(xv, tx, h)

    def token_sums(s):
        total = jnp.zeros((WP, LN), F32)
        for m in range(4):
            for h in range(HL):
                tile = jnp.where(lane_w < CB, members_of(tx, h, 4 * s + m), 0.0)
                one = jnp.sum(tile, axis=1, keepdims=True)
                two = jnp.sum(tile * tile, axis=1, keepdims=True)
                total = jnp.where(lane_w == 8 * m + h, one, total)
                total = jnp.where(lane_w == 8 * m + 3 + h, two, total)
        acc[s, 0:WP, :] = total
        pieces_of_sums(acc.at[s], st.at[s])

    token_sums(0)
    pl.semaphore_wait(barrier, NS - 1 + NC - 1)
    spread("chan", RS1, lambda t: st.at[0, t], rb.at[0])
    token_sums(1)
    spread("chan", RS1 + 1, lambda t: st.at[1, t], rb.at[1])

    for h in range(HL):
        loads[3 + h].wait()
        unpack(cv, tc, h)
    loads[6].wait()

    def send_cotangent(s):
        for pair in range(2):
            store_dense(
                s,
                pair,
                [
                    members_of(tc, h, 4 * s + 2 * pair + one)
                    for h in range(HL)
                    for one in range(2)
                ],
            )
        out = dot(dv[1], xn[s]) * lon_factor
        send2[s] = out.reshape(NS, 8, PL).astype(BF16)
        spread("space", A2 + s, lambda t: send2.at[s, t], recv2.at[s])

    def share_statistics(s):
        arrived(RS1 + s, rb.at[s])
        sums = jnp.sum(rb[s], axis=0) * (1.0 / C)
        var_in = pltpu.roll(sums, 5, 0)
        inv = lax.rsqrt(var_in - sums * sums + norm_epsilon)
        row8 = lax.broadcasted_iota(jnp.int32, (8, LN), 0)
        ags[s] = jnp.where(row8 < 3, sums, jnp.where(row8 < 6, pltpu.roll(inv, 3, 0), 0.0))
        spread("chan", AG1 + s, lambda t: ags.at[s], ab.at[s])

    send_cotangent(0)
    share_statistics(0)
    share_statistics(1)
    send_cotangent(1)

    def send_normed(s):
        arrived(AG1 + s, ab.at[s, pl.ds(0, NC)])
        columns_of(ab.at[s], at.at[s])
        for pair in range(2):
            tiles = []
            for h in range(HL):
                for one in range(2):
                    m = 2 * pair + one
                    column = 8 * m + h
                    mean_col = at[s, 0:WP, column : column + 1]
                    inv_col = at[s, 0:WP, column + 3 : column + 4]
                    centred = (members_of(tx, h, 4 * s + m) - mean_col) * inv_col
                    cen[s, 4 * h + m] = centred
                    tiles.append(centred * gain_row + shift_row)
            store_dense(s, pair, tiles)
        out = dot(dv[0], xn[s]) * lon_factor
        send1[s] = out.reshape(NS, 8, PL).astype(BF16)
        spread("space", A1 + s, lambda t: send1.at[s, t], recv1.at[s])

    send_normed(0)
    send_normed(1)

    def latitude(received, target):
        whole = received[...].reshape(8 * NS, PL)
        spectra = [whole[:, HB * h : HB * h + HB] for h in range(HL)]
        for g in range(4):
            rows = slice(2 * H * g, 2 * H * g + 2 * H)
            out = dot(lv[0, rows, :], spectra[0])
            for h in range(1, HL):
                out = out + dot(lv[h, rows, :], spectra[h])
            out = (out * lat_factor).astype(BF16)
            for part in range(2):
                for one in range(2):
                    at_row = HB * (g % 2) + H * one
                    target[g // 2, at_row : at_row + H, LN * part : LN * part + CB] = out[
                        H * part : H * part + H, CB * one : CB * one + CB
                    ]

    loads[8].wait()

    def mix(s):
        def step(i, carry):
            pre = dot(lt[s, i], wc[0]) + vec[2:3, :]
            t = jnp.tanh(gelu_scale * (pre + gelu_cubic * pre * pre * pre))
            hidden = 0.5 * pre * (1.0 + t)
            hidden = jnp.where(lane_t == CB, 1.0, hidden).astype(BF16)
            slope = 0.5 * (1.0 + t) + 0.5 * pre * (1.0 - t * t) * gelu_scale * (
                1.0 + 3.0 * gelu_cubic * pre * pre
            )
            hid[s, i] = hidden
            post = dot(hidden, wc[1]) + vec[3:4, :]
            shape = jnp.tanh(post * (1.0 / shrink_level))
            shrunk = (post - shrink_level * shape).astype(BF16)
            grad_post = (gsh[s, i].astype(F32) * (shape * shape)).astype(BF16)
            gpost[s, i] = grad_post
            grad_pre = (dot_nt(grad_post, wc[1]) * slope).astype(BF16)
            gpre[s, i] = grad_pre
            grad_lat = dot_nt(grad_pre, wc[0]).astype(BF16)
            for pair in range(2):
                for part in range(2):
                    for one in range(2):
                        rows = slice(HB * pair + H * part, HB * pair + H * part + H)
                        lanes = slice(CB * one, CB * one + CB)
                        from_rows = slice(HB * pair + H * one, HB * pair + H * one + H)
                        from_lanes = slice(LN * part, LN * part + CB)
                        sh[s, i, rows, lanes] = shrunk[from_rows, from_lanes]
                        glat[s, i, rows, lanes] = grad_lat[from_rows, from_lanes]
            return carry

        lax.fori_loop(0, 2, step, 0)

    def back(source, target):
        spectrum = source[...].reshape(8 * H, HB)
        for h in range(HL):
            out = dot(mv[h], spectrum) * lat_factor
            target[:, :, HB * h : HB * h + HB] = out.reshape(NS, 8, HB).astype(BF16)

    for s in range(2):
        arrived(A2 + s, recv2.at[s])
        latitude(recv2.at[s], gsh.at[s])
    loads[9].wait()
    for s in range(2):
        arrived(A1 + s, recv1.at[s])
        latitude(recv1.at[s], lt.at[s])
        mix(s)
        back(glat.at[s], send4.at[s])
        spread("space", A4 + s, lambda t, s=s: send4.at[s, t], recv4.at[s])
        back(sh.at[s], send3.at[s])
    for s in range(2):
        spread("space", A3 + s, lambda t, s=s: send3.at[s, t], recv3.at[s])

    for layer_at, (left, right) in enumerate(((lt, gpre), (hid, gpost))):
        outer = dot_tn(left[...].reshape(16 * H, 2 * LN), right[...].reshape(16 * H, 2 * LN))
        real = outer[0:LN, 0:LN] + outer[LN:, LN:]
        imag = outer[0:LN, LN:] - outer[LN:, 0:LN]
        gb[16 * layer_at : 16 * layer_at + 8] = real.reshape(8, 16, LN).astype(BF16)
        gb[16 * layer_at + 8 : 16 * layer_at + 16] = imag.reshape(8, 16, LN).astype(BF16)
    spread("space", GWR, lambda t: gb.at[t], gr)

    loads[7].wait()
    norm_sums = [jnp.zeros((8, LN), F32), jnp.zeros((8, LN), F32)]

    def gradient_sums(s):
        arrived(A4 + s, recv4.at[s])
        out = dot(ev[0], recv4[s].reshape(8 * NS, PL)) * lon_factor
        total = jnp.zeros((WP, LN), F32)
        for h in range(HL):
            for m in range(4):
                grad_normed = tile_of(out, h, m)
                centred = cen[s, 4 * h + m]
                product = grad_normed * centred
                norm_sums[0] = norm_sums[0] + jnp.sum(product.reshape(WP // 8, 8, LN), axis=0)
                norm_sums[1] = norm_sums[1] + jnp.sum(grad_normed.reshape(WP // 8, 8, LN), axis=0)
                grad_centred = grad_normed * gain_row
                gc[s, 4 * h + m] = grad_centred
                one = jnp.sum(grad_centred, axis=1, keepdims=True)
                two = jnp.sum(grad_centred * centred, axis=1, keepdims=True)
                total = jnp.where(lane_w == 8 * m + h, one, total)
                total = jnp.where(lane_w == 8 * m + 3 + h, two, total)
        acc2[s, 0:WP, :] = total
        pieces_of_sums(acc2.at[s], st2.at[s])
        spread("chan", RS2 + s, lambda t: st2.at[s, t], rb2.at[s])

    gradient_sums(0)
    gradient_sums(1)
    ggs[0:1, :] = jnp.sum(norm_sums[0], axis=0, keepdims=True)
    ggs[1:2, :] = jnp.sum(norm_sums[1], axis=0, keepdims=True)
    spread("space", GG, lambda t: ggs, ggr)

    def share_gradient_sums(s):
        arrived(RS2 + s, rb2.at[s])
        ags2[s] = jnp.sum(rb2[s], axis=0) * (1.0 / C)
        spread("chan", AG2 + s, lambda t: ags2.at[s], ab2.at[s])

    share_gradient_sums(0)
    arrived(GWR, gr)
    gas[...] = jnp.sum(gr[...].astype(F32), axis=0).astype(BF16)
    spread("space", GWG, lambda t: gas, ga)
    share_gradient_sums(1)

    def put_mixed(s):
        arrived(A3 + s, recv3.at[s])
        out = dot(ev[1], recv3[s].reshape(8 * NS, PL)) * lon_factor
        for h in range(HL):
            for m in range(4):
                put_members(tc, h, 4 * s + m, tile_of(out, h, m))

    def put_members(array, h, b, tile):
        array[h, pl.ds(b, WP, stride=8), :] = tile

    def put_gradient(s):
        arrived(AG2 + s, ab2.at[s, pl.ds(0, NC)])
        columns_of(ab2.at[s], at2.at[s])
        for h in range(HL):
            for m in range(4):
                column = 8 * m + h
                inv_col = at[s, 0:WP, column + 3 : column + 4]
                first = at2[s, 0:WP, column : column + 1]
                second = at2[s, 0:WP, column + 3 : column + 4]
                put_members(
                    tx,
                    h,
                    4 * s + m,
                    inv_col * (gc[s, 4 * h + m] - first - cen[s, 4 * h + m] * second),
                )

    put_mixed(0)
    put_gradient(0)
    put_gradient(1)
    for h in range(HL):
        pack(tx, gin_out, h)
    put_mixed(1)
    for h in range(HL):
        pack(tc, mixed_out, h)

    arrived(GG, ggr)
    both = jnp.sum(ggr[...], axis=0)
    gg_ref[...] = both[0:1, 0:CB]
    gs_ref[...] = both[1:2, 0:CB]
    arrived(GWG, ga)
    for layer_at, (gw_ref, gbias_ref) in enumerate(((gw1_ref, gb1_ref), (gw2_ref, gb2_ref))):
        for part in range(2):
            at_piece = 16 * layer_at + 8 * part
            block = ga[at_piece : at_piece + 8].astype(F32).reshape(LN, LN)
            gw_ref[part, 0] = block[0:CB, 0:CB]
            gbias_ref[part] = block[CB : CB + 1, 0:CB]

    for s in range(2):
        sent(RS1 + s, rb.at[s], NC)
        sent(AG1 + s, ab.at[s], NC)
        sent(RS2 + s, rb2.at[s], NC)
        sent(AG2 + s, ab2.at[s], NC)
        sent(A2 + s, recv2.at[s], NS)
        sent(A1 + s, recv1.at[s], NS)
        sent(A4 + s, recv4.at[s], NS)
        sent(A3 + s, recv3.at[s], NS)
    sent(GWR, gr, NS)
    sent(GWG, ga, NS)
    sent(GG, ggr, NS)


def write_out(*refs):
    count = (len(refs) - 1) // 2
    sems = refs[-1]
    copies = [
        pltpu.make_async_copy(refs[i], refs[count + i], sems.at[i]) for i in range(count)
    ]
    for copy in copies:
        copy.start()
    for copy in copies:
        copy.wait()


def on_device(members, gain, shift, w_first, b_first, w_second, b_second, cotangent):
    lon_out, lon_back, lat_out, lat_back = (jnp.asarray(t) for t in tables())
    anywhere = pl.BlockSpec(memory_space=pl.ANY)
    vmem = pl.BlockSpec(memory_space=pltpu.VMEM)
    token = (HL, 1, 8, W * CB)
    piece = (2, NS, 8, PL)
    spectral = (2, 2, 4 * H, 2 * LN)
    folded = (2, 2, 4 * H, HB)
    results = (
        jax.ShapeDtypeStruct(token, BF16),
        jax.ShapeDtypeStruct(token, BF16),
        jax.ShapeDtypeStruct((2, 1, CB, CB), F32),
        jax.ShapeDtypeStruct((2, 1, CB), F32),
        jax.ShapeDtypeStruct((2, 1, CB, CB), F32),
        jax.ShapeDtypeStruct((2, 1, CB), F32),
        jax.ShapeDtypeStruct((1, CB), F32),
        jax.ShapeDtypeStruct((1, CB), F32),
    )
    outs = pl.pallas_call(
        layer,
        out_shape=tuple(pltpu.VMEM(r.shape, r.dtype) for r in results),
        in_specs=[anywhere] * 2 + [vmem] * 6 + [anywhere] * 4,
        out_specs=tuple([vmem] * 8),
        scratch_shapes=[
            pltpu.VMEM(token, BF16),
            pltpu.VMEM(token, BF16),
            pltpu.VMEM((2, 8 * NS, 2 * WP), BF16),
            pltpu.VMEM((2, 2 * WP, 8 * NS), BF16),
            pltpu.VMEM((HL, 8 * H, 8 * NS), BF16),
            pltpu.VMEM((HL, 8 * NS, 8 * H), BF16),
            pltpu.VMEM((HL, 8 * WP, LN), F32),
            pltpu.VMEM((HL, 8 * WP, LN), F32),
            pltpu.VMEM((2, 2 * WP, PL), BF16),
            pltpu.VMEM((2, 4 * HL, WP, LN), F32),
            pltpu.VMEM((2, 4 * HL, WP, LN), F32),
        ]
        + [pltpu.VMEM(piece, BF16)] * 8
        + [pltpu.VMEM(spectral, BF16)] * 5
        + [pltpu.VMEM(folded, BF16)] * 2
        + [
            pltpu.VMEM((2, 2 * LN, 2 * LN), BF16),
            pltpu.VMEM((8, 2 * LN), F32),
        ]
        + [
            pltpu.VMEM((2, 2 * LN, LN), F32),
            pltpu.VMEM((2, NC, 8, LN), F32),
            pltpu.VMEM((2, NC, 8, LN), F32),
            pltpu.VMEM((2, 8, LN), F32),
            pltpu.VMEM((2, 2 * NC, 8, LN), F32),
            pltpu.VMEM((2, 2 * LN, LN), F32),
        ]
        * 2
        + [
            pltpu.VMEM((NS, 16, LN), BF16),
            pltpu.VMEM((NS, 16, LN), BF16),
            pltpu.VMEM((16, LN), BF16),
            pltpu.VMEM((NS, 16, LN), BF16),
            pltpu.VMEM((2, LN), F32),
            pltpu.VMEM((NS, 2, LN), F32),
            pltpu.SemaphoreType.DMA((10,)),
            pltpu.SemaphoreType.DMA((19,)),
            pltpu.SemaphoreType.DMA((19,)),
        ],
        compiler_params=pltpu.CompilerParams(
            collective_id=0, has_side_effects=True, vmem_limit_bytes=52 * 1024 * 1024
        ),
    )(
        jnp.transpose(members, (1, 2, 0, 3)),
        jnp.transpose(cotangent, (1, 2, 0, 3)),
        gain.reshape(1, CB),
        shift.reshape(1, CB),
        w_first,
        b_first,
        w_second,
        b_second,
        lon_out,
        lon_back,
        lat_out,
        lat_back,
    )
    outs = [pltpu.with_memory_space_constraint(o, pltpu.VMEM) for o in outs]
    mixed, grad_input, gw1, gb1, gw2, gb2, gg, gs = pl.pallas_call(
        write_out,
        out_shape=results,
        in_specs=[vmem] * 8,
        out_specs=tuple([anywhere] * 8),
        scratch_shapes=[pltpu.SemaphoreType.DMA((8,))],
    )(*outs)
    return (
        jnp.transpose(mixed, (2, 0, 1, 3)),
        jnp.transpose(grad_input, (2, 0, 1, 3)),
        gw1,
        gb1,
        gw2,
        gb2,
        gg.reshape(CB),
        gs.reshape(CB),
    )


def solution(mesh):
    placed = (
        P(None, "space", "chan", None),
        P("chan"),
        P("chan"),
        P(None, "chan", None, None),
        P(None, "chan", None),
        P(None, "chan", None, None),
        P(None, "chan", None),
        P(None, "space", "chan", None),
    )
    return jax.shard_map(
        on_device,
        mesh=mesh,
        in_specs=placed,
        out_specs=(
            P(None, "space", "chan", None),
            P(None, "space", "chan", None),
            P(None, "chan", None, None),
            P(None, "chan", None),
            P(None, "chan", None, None),
            P(None, "chan", None),
            P("chan"),
            P("chan"),
        ),
        check_vma=False,
    )
```

```python
import math

import jax
import jax.numpy as jnp
import ml_dtypes
import numpy as np
from jax import lax
from jax.experimental import pallas as pl
from jax.experimental.pallas import tpu as pltpu
from jax.sharding import PartitionSpec as P

C = 768
CB = 96
W = 180
WP = 192
MW = 64
H = 96
NS = 32
NC = 8
HL = H // NS
LN = 128
PL = 5 * LN
HB = 2 * CB

shrink_level = 0.05
norm_epsilon = 1e-05
gelu_scale = 0.7978845608
gelu_cubic = 0.044715
lon_factor = 1.0 / math.sqrt(W)
lat_factor = 1.0 / math.sqrt(H)

F32 = jnp.float32
BF16 = jnp.bfloat16
MESH = pl.DeviceIdType.MESH

RS1, AG1, A2, A1, A4, A3, RS2, AG2 = range(0, 16, 2)
GWR, GWG, GG = range(16, 19)


def twiddle(length, columns):
    rows = np.arange(length)[:, None]
    cols = np.arange(columns)[None, :]
    angles = (rows * cols % length).astype(np.float32) * np.float32(2.0 * math.pi / length)
    return (
        np.cos(angles).astype(np.float32),
        np.sin(angles).astype(np.float32),
    )


def tables():
    bf = ml_dtypes.bfloat16
    cos_lon, sin_lon = (t.astype(bf).astype(np.float32) for t in twiddle(W, MW))
    cos_lat, sin_lat = (t.astype(bf).astype(np.float32) for t in twiddle(H, H))
    lon = np.zeros((NS, 2, 2, 2, 2, WP), np.float32)
    scaled = np.zeros_like(lon)
    for d in range(NS):
        for mm in range(2):
            m = 2 * d + mm
            twice = 1.0 if m == 0 else 2.0
            for b in range(2):
                lon[d, 0, mm, b, b, :W] = cos_lon[:, m]
                lon[d, 1, mm, b, b, :W] = -sin_lon[:, m]
                scaled[d, :, mm, b] = twice * lon[d, :, mm, b]
    lon = lon.reshape(8 * NS, 2 * WP)
    scaled = scaled.reshape(8 * NS, 2 * WP)
    lat = np.zeros((HL, 2, 2, 2, H, NS, 2, 2, 2), np.float32)
    for hh in range(HL):
        cos_part = cos_lat[:, hh::HL]
        sin_part = sin_lat[:, hh::HL]
        for mm in range(2):
            for b in range(2):
                lat[hh, mm, b, 0, :, :, 0, mm, b] = cos_part
                lat[hh, mm, b, 0, :, :, 1, mm, b] = sin_part
                lat[hh, mm, b, 1, :, :, 0, mm, b] = -sin_part
                lat[hh, mm, b, 1, :, :, 1, mm, b] = cos_part
    lat = lat.reshape(HL, 8 * H, 8 * NS)
    return (
        np.stack([lon, scaled]).astype(bf),
        np.stack([lon.T, scaled.T]).astype(bf),
        lat.astype(bf),
        np.swapaxes(lat, 1, 2).astype(bf),
    )


def dot(left, right):
    return lax.dot_general(left, right, (((1,), (0,)), ((), ())), preferred_element_type=F32)


def dot_nt(left, right):
    return lax.dot_general(left, right, (((1,), (1,)), ((), ())), preferred_element_type=F32)


def dot_tn(left, right):
    return lax.dot_general(left, right, (((0,), (0,)), ((), ())), preferred_element_type=F32)


def unpack(source, target, h):
    lane = lax.broadcasted_iota(jnp.int32, (8, LN), 1)

    def step(it, carry):
        for u in range(15):
            i = it * 15 + u
            chunk = source[h, 0, :, pl.ds(pl.multiple_of(i * 384, 128), 384)].astype(F32)
            v0, v1, v2 = chunk[:, :128], chunk[:, 128:256], chunk[:, 256:]
            parts = (
                v0,
                pltpu.roll(jnp.where(lane >= 96, v0, v1), 32, 1),
                pltpu.roll(jnp.where(lane >= 64, v1, v2), 64, 1),
                pltpu.roll(v2, 96, 1),
            )
            for q in range(4):
                target[h, pl.ds(pl.multiple_of(i * 32 + 8 * q, 8), 8), :] = parts[q]
        return carry

    lax.fori_loop(0, 3, step, 0)


def pack(source, target, h):
    lane = lax.broadcasted_iota(jnp.int32, (8, LN), 1)

    def step(it, carry):
        for u in range(15):
            i = it * 15 + u
            p0, p1, p2, p3 = (
                source[h, pl.ds(pl.multiple_of(i * 32 + 8 * q, 8), 8), :] for q in range(4)
            )
            r1 = pltpu.roll(p1, 96, 1)
            r2 = pltpu.roll(p2, 64, 1)
            r3 = pltpu.roll(p3, 32, 1)
            chunk = jnp.concatenate(
                [
                    jnp.where(lane < 96, p0, r1),
                    jnp.where(lane < 64, r1, r2),
                    jnp.where(lane < 32, r2, r3),
                ],
                axis=1,
            )
            target[h, 0, :, pl.ds(pl.multiple_of(i * 384, 128), 384)] = chunk.astype(BF16)
        return carry

    lax.fori_loop(0, 3, step, 0)


def layer(
    x_hbm, cot_hbm, gain_hbm, shift_hbm, w1_hbm, b1_hbm, w2_hbm, b2_hbm,
    d_hbm, e_hbm, l_hbm, m_hbm,
    mixed_out, gin_out, gw1_ref, gb1_ref, gw2_ref, gb2_ref, gg_ref, gs_ref,
    xv, cv, dv, ev, lv, mv, tx, tc, xn, cen, gc,
    send1, send2, send3, send4, recv1, recv2, recv3, recv4,
    lt, gsh, hid, gpost, gpre, sh, glat, wc, vec,
    acc, st, rb, ags, ab, at, acc2, st2, rb2, ags2, ab2, at2,
    gb, gr, gas, ga, ggs, ggr, small, w1_v, w2_v, b1_v, b2_v,
    in_sems, send_sems, recv_sems,
):
    me_s = lax.axis_index("space")
    me_c = lax.axis_index("chan")

    loads = [pltpu.make_async_copy(x_hbm.at[h], xv.at[h], in_sems.at[h]) for h in range(HL)]
    loads += [pltpu.make_async_copy(cot_hbm.at[h], cv.at[h], in_sems.at[3 + h]) for h in range(HL)]
    loads += [
        pltpu.make_async_copy(d_hbm, dv, in_sems.at[6]),
        pltpu.make_async_copy(e_hbm, ev, in_sems.at[7]),
        pltpu.make_async_copy(l_hbm, lv, in_sems.at[8]),
        pltpu.make_async_copy(m_hbm, mv, in_sems.at[9]),
        pltpu.make_async_copy(gain_hbm, small.at[0], in_sems.at[10]),
        pltpu.make_async_copy(shift_hbm, small.at[1], in_sems.at[11]),
        pltpu.make_async_copy(w1_hbm, w1_v, in_sems.at[12]),
        pltpu.make_async_copy(b1_hbm, b1_v, in_sems.at[13]),
        pltpu.make_async_copy(w2_hbm, w2_v, in_sems.at[14]),
        pltpu.make_async_copy(b2_hbm, b2_v, in_sems.at[15]),
    ]
    for load in loads:
        load.start()

    barrier = pltpu.get_barrier_semaphore()

    def greet_space(r, carry):
        pl.semaphore_signal(
            barrier, inc=1, device_id={"space": lax.rem(me_s + r, NS)}, device_id_type=MESH
        )
        return carry

    def greet_chan(r, carry):
        pl.semaphore_signal(
            barrier, inc=1, device_id={"chan": lax.rem(me_c + r, NC)}, device_id_type=MESH
        )
        return carry

    lax.fori_loop(1, NC, greet_chan, 0)
    lax.fori_loop(1, NS, greet_space, 0)

    def spread(axis, index, piece, target):
        count, me = (NS, me_s) if axis == "space" else (NC, me_c)

        def step(r, carry):
            t = lax.rem(me + r, count)
            pltpu.make_async_remote_copy(
                src_ref=piece(t),
                dst_ref=target.at[me],
                send_sem=send_sems.at[index],
                recv_sem=recv_sems.at[index],
                device_id={axis: t},
                device_id_type=MESH,
            ).start()
            return carry

        lax.fori_loop(1, count, step, 0)
        pltpu.make_async_copy(piece(me), target.at[me], recv_sems.at[index]).start()

    def arrived(index, target):
        pltpu.make_async_copy(target, target, recv_sems.at[index]).wait()

    def sent(index, target, count):
        rest = target.at[pl.ds(0, count - 1)]
        pltpu.make_async_copy(rest, rest, send_sems.at[index]).wait()

    tx[:, 8 * W :, :] = jnp.zeros((HL, 8 * (WP - W), LN), F32)
    tc[:, 8 * W :, :] = jnp.zeros((HL, 8 * (WP - W), LN), F32)
    acc[...] = jnp.zeros_like(acc)
    acc2[...] = jnp.zeros_like(acc2)
    ab[:, NC:] = jnp.zeros((2, NC, 8, LN), F32)
    ab2[:, NC:] = jnp.zeros((2, NC, 8, LN), F32)
    lane_t = lax.broadcasted_iota(jnp.int32, (4 * H, 2 * LN), 1)
    for s in range(2):
        send3[s, :, :, PL - LN :] = jnp.zeros((NS, 8, LN), BF16)
        send4[s, :, :, PL - LN :] = jnp.zeros((NS, 8, LN), BF16)
        for g in range(2):
            lt[s, g] = jnp.where(lane_t == CB, 1.0, 0.0).astype(BF16)
            gsh[s, g] = jnp.zeros((4 * H, 2 * LN), BF16)

    lane_w = lax.broadcasted_iota(jnp.int32, (WP, LN), 1)

    def members_of(array, h, b):
        return array[h, pl.ds(b, WP, stride=8), :]

    def pair_of(m):
        return m // 2, m % 2

    def dense(tiles):
        t0, t1, t2, t3, t4, t5 = tiles
        r1, r2, r3 = pltpu.roll(t1, 96, 1), pltpu.roll(t2, 64, 1), pltpu.roll(t3, 32, 1)
        r5 = pltpu.roll(t5, 96, 1)
        return (
            jnp.where(lane_w < 96, t0, r1),
            jnp.where(lane_w < 64, r1, r2),
            jnp.where(lane_w < 32, r2, r3),
            jnp.where(lane_w < 96, t4, r5),
            jnp.where(lane_w < 64, r5, 0.0),
        )

    def tile_of(array, h, m):
        pair, one = pair_of(m)
        rows = slice(WP * pair, WP * pair + WP)
        start = HB * h + CB * one
        first, shift = start // LN * LN, start % LN
        left = array[rows, first : first + LN]
        if shift == 0:
            return left
        if shift > 32:
            right = array[rows, first + LN : first + 2 * LN]
            left = jnp.where(lane_w >= shift, left, right)
        return pltpu.roll(left, LN - shift, 1)

    def store_dense(s, pair, tiles):
        for i, column in enumerate(dense(tiles)):
            xn[s, WP * pair : WP * pair + WP, LN * i : LN * i + LN] = column.astype(BF16)

    def pieces_of_sums(source, target):
        turned = jnp.transpose(source[...])
        for part in range(2):
            for m in range(4):
                target[4 * part + m] = turned[8 * m : 8 * m + 8, LN * part : LN * part + LN]

    def columns_of(source, target):
        turned = jnp.transpose(source[...].reshape(LN, LN))
        target[0:LN, 0:32] = turned[:, 0:32]
        target[LN:, 0:32] = turned[:, 32:64]

    for h in range(HL):
        loads[h].wait()
        unpack(xv, tx, h)

    def token_sums(s):
        total = jnp.zeros((WP, LN), F32)
        for m in range(4):
            for h in range(HL):
                tile = jnp.where(lane_w < CB, members_of(tx, h, 4 * s + m), 0.0)
                one = jnp.sum(tile, axis=1, keepdims=True)
                two = jnp.sum(tile * tile, axis=1, keepdims=True)
                total = jnp.where(lane_w == 8 * m + h, one, total)
                total = jnp.where(lane_w == 8 * m + 3 + h, two, total)
        acc[s, 0:WP, :] = total
        pieces_of_sums(acc.at[s], st.at[s])

    token_sums(0)
    pl.semaphore_wait(barrier, NS - 1 + NC - 1)
    spread("chan", RS1, lambda t: st.at[0, t], rb.at[0])
    token_sums(1)
    spread("chan", RS1 + 1, lambda t: st.at[1, t], rb.at[1])

    for k in range(10, 16):
        loads[k].wait()
    vec[...] = jnp.zeros_like(vec)
    vec[0:1, 0:CB] = small[0]
    vec[1:2, 0:CB] = small[1]
    for layer_at, (b_ref, w_ref) in enumerate(((b1_v, w1_v), (b2_v, w2_v))):
        vec[2 + layer_at : 3 + layer_at, 0:CB] = b_ref[0]
        vec[2 + layer_at : 3 + layer_at, LN : LN + CB] = b_ref[1]
        wc[layer_at] = jnp.zeros((2 * LN, 2 * LN), BF16)
        w_real, w_imag = w_ref[0, 0], w_ref[1, 0]
        wc[layer_at, 0:CB, 0:CB] = w_real
        wc[layer_at, 0:CB, LN : LN + CB] = w_imag
        wc[layer_at, LN : LN + CB, 0:CB] = -w_imag
        wc[layer_at, LN : LN + CB, LN : LN + CB] = w_real
    gain_row = vec[0:1, 0:LN]
    shift_row = vec[1:2, 0:LN]

    for h in range(HL):
        loads[3 + h].wait()
        unpack(cv, tc, h)
    loads[6].wait()

    def send_cotangent(s):
        for pair in range(2):
            store_dense(
                s,
                pair,
                [
                    members_of(tc, h, 4 * s + 2 * pair + one)
                    for h in range(HL)
                    for one in range(2)
                ],
            )
        out = dot(dv[1], xn[s]) * lon_factor
        send2[s] = out.reshape(NS, 8, PL).astype(BF16)
        spread("space", A2 + s, lambda t: send2.at[s, t], recv2.at[s])

    def share_statistics(s):
        arrived(RS1 + s, rb.at[s])
        sums = jnp.sum(rb[s], axis=0) * (1.0 / C)
        var_in = pltpu.roll(sums, 5, 0)
        inv = lax.rsqrt(var_in - sums * sums + norm_epsilon)
        row8 = lax.broadcasted_iota(jnp.int32, (8, LN), 0)
        ags[s] = jnp.where(row8 < 3, sums, jnp.where(row8 < 6, pltpu.roll(inv, 3, 0), 0.0))
        spread("chan", AG1 + s, lambda t: ags.at[s], ab.at[s])

    send_cotangent(0)
    share_statistics(0)
    share_statistics(1)
    send_cotangent(1)

    def send_normed(s):
        arrived(AG1 + s, ab.at[s, pl.ds(0, NC)])
        columns_of(ab.at[s], at.at[s])
        for pair in range(2):
            tiles = []
            for h in range(HL):
                for one in range(2):
                    m = 2 * pair + one
                    column = 8 * m + h
                    mean_col = at[s, 0:WP, column : column + 1]
                    inv_col = at[s, 0:WP, column + 3 : column + 4]
                    centred = (members_of(tx, h, 4 * s + m) - mean_col) * inv_col
                    cen[s, 4 * h + m] = centred
                    tiles.append(centred * gain_row + shift_row)
            store_dense(s, pair, tiles)
        out = dot(dv[0], xn[s]) * lon_factor
        send1[s] = out.reshape(NS, 8, PL).astype(BF16)
        spread("space", A1 + s, lambda t: send1.at[s, t], recv1.at[s])

    send_normed(0)
    send_normed(1)

    def latitude(received, target):
        whole = received[...].reshape(8 * NS, PL)
        spectra = [whole[:, HB * h : HB * h + HB] for h in range(HL)]
        for g in range(4):
            rows = slice(2 * H * g, 2 * H * g + 2 * H)
            out = dot(lv[0, rows, :], spectra[0])
            for h in range(1, HL):
                out = out + dot(lv[h, rows, :], spectra[h])
            out = (out * lat_factor).astype(BF16)
            for part in range(2):
                for one in range(2):
                    at_row = HB * (g % 2) + H * one
                    target[g // 2, at_row : at_row + H, LN * part : LN * part + CB] = out[
                        H * part : H * part + H, CB * one : CB * one + CB
                    ]

    loads[8].wait()

    def mix(s):
        def step(i, carry):
            pre = dot(lt[s, i], wc[0]) + vec[2:3, :]
            t = jnp.tanh(gelu_scale * (pre + gelu_cubic * pre * pre * pre))
            hidden = 0.5 * pre * (1.0 + t)
            hidden = jnp.where(lane_t == CB, 1.0, hidden).astype(BF16)
            slope = 0.5 * (1.0 + t) + 0.5 * pre * (1.0 - t * t) * gelu_scale * (
                1.0 + 3.0 * gelu_cubic * pre * pre
            )
            hid[s, i] = hidden
            post = dot(hidden, wc[1]) + vec[3:4, :]
            shape = jnp.tanh(post * (1.0 / shrink_level))
            shrunk = (post - shrink_level * shape).astype(BF16)
            grad_post = (gsh[s, i].astype(F32) * (shape * shape)).astype(BF16)
            gpost[s, i] = grad_post
            grad_pre = (dot_nt(grad_post, wc[1]) * slope).astype(BF16)
            gpre[s, i] = grad_pre
            grad_lat = dot_nt(grad_pre, wc[0]).astype(BF16)
            for pair in range(2):
                for part in range(2):
                    for one in range(2):
                        rows = slice(HB * pair + H * part, HB * pair + H * part + H)
                        lanes = slice(CB * one, CB * one + CB)
                        from_rows = slice(HB * pair + H * one, HB * pair + H * one + H)
                        from_lanes = slice(LN * part, LN * part + CB)
                        sh[s, i, rows, lanes] = shrunk[from_rows, from_lanes]
                        glat[s, i, rows, lanes] = grad_lat[from_rows, from_lanes]
            return carry

        lax.fori_loop(0, 2, step, 0)

    def back(source, target):
        spectrum = source[...].reshape(8 * H, HB)
        for h in range(HL):
            out = dot(mv[h], spectrum) * lat_factor
            target[:, :, HB * h : HB * h + HB] = out.reshape(NS, 8, HB).astype(BF16)

    for s in range(2):
        arrived(A2 + s, recv2.at[s])
        latitude(recv2.at[s], gsh.at[s])
    loads[9].wait()
    for s in range(2):
        arrived(A1 + s, recv1.at[s])
        latitude(recv1.at[s], lt.at[s])
        mix(s)
        back(glat.at[s], send4.at[s])
        spread("space", A4 + s, lambda t, s=s: send4.at[s, t], recv4.at[s])
        if s == 1:
            spread("space", A3, lambda t: send3.at[0, t], recv3.at[0])
        back(sh.at[s], send3.at[s])

    for layer_at, (left, right) in enumerate(((lt, gpre), (hid, gpost))):
        outer = dot_tn(left[...].reshape(16 * H, 2 * LN), right[...].reshape(16 * H, 2 * LN))
        real = outer[0:LN, 0:LN] + outer[LN:, LN:]
        imag = outer[0:LN, LN:] - outer[LN:, 0:LN]
        gb[16 * layer_at : 16 * layer_at + 8] = real.reshape(8, 16, LN).astype(BF16)
        gb[16 * layer_at + 8 : 16 * layer_at + 16] = imag.reshape(8, 16, LN).astype(BF16)
    spread("space", GWR, lambda t: gb.at[t], gr)
    spread("space", A3 + 1, lambda t: send3.at[1, t], recv3.at[1])

    loads[7].wait()
    norm_sums = [jnp.zeros((8, LN), F32), jnp.zeros((8, LN), F32)]

    def gradient_sums(s):
        arrived(A4 + s, recv4.at[s])
        out = dot(ev[0], recv4[s].reshape(8 * NS, PL)) * lon_factor
        total = jnp.zeros((WP, LN), F32)
        for h in range(HL):
            for m in range(4):
                grad_normed = tile_of(out, h, m)
                centred = cen[s, 4 * h + m]
                product = grad_normed * centred
                norm_sums[0] = norm_sums[0] + jnp.sum(product.reshape(WP // 8, 8, LN), axis=0)
                norm_sums[1] = norm_sums[1] + jnp.sum(grad_normed.reshape(WP // 8, 8, LN), axis=0)
                grad_centred = grad_normed * gain_row
                gc[s, 4 * h + m] = grad_centred
                one = jnp.sum(grad_centred, axis=1, keepdims=True)
                two = jnp.sum(grad_centred * centred, axis=1, keepdims=True)
                total = jnp.where(lane_w == 8 * m + h, one, total)
                total = jnp.where(lane_w == 8 * m + 3 + h, two, total)
        acc2[s, 0:WP, :] = total
        pieces_of_sums(acc2.at[s], st2.at[s])
        spread("chan", RS2 + s, lambda t: st2.at[s, t], rb2.at[s])

    gradient_sums(0)
    gradient_sums(1)

    def share_gradient_sums(s):
        arrived(RS2 + s, rb2.at[s])
        ags2[s] = jnp.sum(rb2[s], axis=0) * (1.0 / C)
        spread("chan", AG2 + s, lambda t: ags2.at[s], ab2.at[s])

    share_gradient_sums(0)
    ggs[0:1, :] = jnp.sum(norm_sums[0], axis=0, keepdims=True)
    ggs[1:2, :] = jnp.sum(norm_sums[1], axis=0, keepdims=True)
    spread("space", GG, lambda t: ggs, ggr)

    def put_mixed(s):
        arrived(A3 + s, recv3.at[s])
        out = dot(ev[1], recv3[s].reshape(8 * NS, PL)) * lon_factor
        for h in range(HL):
            for m in range(4):
                put_members(tc, h, 4 * s + m, tile_of(out, h, m))

    def put_members(array, h, b, tile):
        array[h, pl.ds(b, WP, stride=8), :] = tile

    def put_gradient(s):
        arrived(AG2 + s, ab2.at[s, pl.ds(0, NC)])
        columns_of(ab2.at[s], at2.at[s])
        for h in range(HL):
            for m in range(4):
                column = 8 * m + h
                inv_col = at[s, 0:WP, column + 3 : column + 4]
                first = at2[s, 0:WP, column : column + 1]
                second = at2[s, 0:WP, column + 3 : column + 4]
                put_members(
                    tx,
                    h,
                    4 * s + m,
                    inv_col * (gc[s, 4 * h + m] - first - cen[s, 4 * h + m] * second),
                )

    put_mixed(0)
    share_gradient_sums(1)
    put_gradient(0)
    arrived(GWR, gr)
    gas[...] = jnp.sum(gr[...].astype(F32), axis=0).astype(BF16)
    spread("space", GWG, lambda t: gas, ga)
    put_gradient(1)
    for h in range(HL):
        pack(tx, gin_out, h)
    put_mixed(1)
    for h in range(HL):
        pack(tc, mixed_out, h)

    arrived(GG, ggr)
    both = jnp.sum(ggr[...], axis=0)
    gg_ref[...] = both[0:1, 0:CB]
    gs_ref[...] = both[1:2, 0:CB]
    arrived(GWG, ga)
    for layer_at, (gw_ref, gbias_ref) in enumerate(((gw1_ref, gb1_ref), (gw2_ref, gb2_ref))):
        for part in range(2):
            at_piece = 16 * layer_at + 8 * part
            block = ga[at_piece : at_piece + 8].astype(F32).reshape(LN, LN)
            gw_ref[part, 0] = block[0:CB, 0:CB]
            gbias_ref[part] = block[CB : CB + 1, 0:CB]

    for s in range(2):
        sent(RS1 + s, rb.at[s], NC)
        sent(AG1 + s, ab.at[s], NC)
        sent(RS2 + s, rb2.at[s], NC)
        sent(AG2 + s, ab2.at[s], NC)
        sent(A2 + s, recv2.at[s], NS)
        sent(A1 + s, recv1.at[s], NS)
        sent(A4 + s, recv4.at[s], NS)
        sent(A3 + s, recv3.at[s], NS)
    sent(GWR, gr, NS)
    sent(GWG, ga, NS)
    sent(GG, ggr, NS)


def write_out(*refs):
    count = (len(refs) - 1) // 2
    sems = refs[-1]
    copies = [
        pltpu.make_async_copy(refs[i], refs[count + i], sems.at[i]) for i in range(count)
    ]
    for copy in copies:
        copy.start()
    for copy in copies:
        copy.wait()


def on_device(members, gain, shift, w_first, b_first, w_second, b_second, cotangent):
    lon_out, lon_back, lat_out, lat_back = (jnp.asarray(t) for t in tables())
    anywhere = pl.BlockSpec(memory_space=pl.ANY)
    vmem = pl.BlockSpec(memory_space=pltpu.VMEM)
    stays = pl.BlockSpec(memory_space=pltpu.HBM)
    token = (HL, 1, 8, W * CB)
    piece = (2, NS, 8, PL)
    spectral = (2, 2, 4 * H, 2 * LN)
    folded = (2, 2, 4 * H, HB)
    results = (
        jax.ShapeDtypeStruct(token, BF16),
        jax.ShapeDtypeStruct(token, BF16),
        jax.ShapeDtypeStruct((2, 1, CB, CB), F32),
        jax.ShapeDtypeStruct((2, 1, CB), F32),
        jax.ShapeDtypeStruct((2, 1, CB, CB), F32),
        jax.ShapeDtypeStruct((2, 1, CB), F32),
        jax.ShapeDtypeStruct((1, CB), F32),
        jax.ShapeDtypeStruct((1, CB), F32),
    )
    outs = pl.pallas_call(
        layer,
        out_shape=tuple(pltpu.VMEM(r.shape, r.dtype) for r in results),
        in_specs=[stays] * 12,
        out_specs=tuple([vmem] * 8),
        scratch_shapes=[
            pltpu.VMEM(token, BF16),
            pltpu.VMEM(token, BF16),
            pltpu.VMEM((2, 8 * NS, 2 * WP), BF16),
            pltpu.VMEM((2, 2 * WP, 8 * NS), BF16),
            pltpu.VMEM((HL, 8 * H, 8 * NS), BF16),
            pltpu.VMEM((HL, 8 * NS, 8 * H), BF16),
            pltpu.VMEM((HL, 8 * WP, LN), F32),
            pltpu.VMEM((HL, 8 * WP, LN), F32),
            pltpu.VMEM((2, 2 * WP, PL), BF16),
            pltpu.VMEM((2, 4 * HL, WP, LN), F32),
            pltpu.VMEM((2, 4 * HL, WP, LN), F32),
        ]
        + [pltpu.VMEM(piece, BF16)] * 8
        + [pltpu.VMEM(spectral, BF16)] * 5
        + [pltpu.VMEM(folded, BF16)] * 2
        + [
            pltpu.VMEM((2, 2 * LN, 2 * LN), BF16),
            pltpu.VMEM((8, 2 * LN), F32),
        ]
        + [
            pltpu.VMEM((2, 2 * LN, LN), F32),
            pltpu.VMEM((2, NC, 8, LN), F32),
            pltpu.VMEM((2, NC, 8, LN), F32),
            pltpu.VMEM((2, 8, LN), F32),
            pltpu.VMEM((2, 2 * NC, 8, LN), F32),
            pltpu.VMEM((2, 2 * LN, LN), F32),
        ]
        * 2
        + [
            pltpu.VMEM((NS, 16, LN), BF16),
            pltpu.VMEM((NS, 16, LN), BF16),
            pltpu.VMEM((16, LN), BF16),
            pltpu.VMEM((NS, 16, LN), BF16),
            pltpu.VMEM((2, LN), F32),
            pltpu.VMEM((NS, 2, LN), F32),
            pltpu.VMEM((2, 1, CB), F32),
            pltpu.VMEM((2, 1, CB, CB), BF16),
            pltpu.VMEM((2, 1, CB, CB), BF16),
            pltpu.VMEM((2, 1, CB), F32),
            pltpu.VMEM((2, 1, CB), F32),
            pltpu.SemaphoreType.DMA((16,)),
            pltpu.SemaphoreType.DMA((19,)),
            pltpu.SemaphoreType.DMA((19,)),
        ],
        compiler_params=pltpu.CompilerParams(
            collective_id=0, has_side_effects=True, vmem_limit_bytes=60 * 1024 * 1024
        ),
    )(
        jnp.transpose(members, (1, 2, 0, 3)),
        jnp.transpose(cotangent, (1, 2, 0, 3)),
        gain.reshape(1, CB),
        shift.reshape(1, CB),
        w_first,
        b_first,
        w_second,
        b_second,
        lon_out,
        lon_back,
        lat_out,
        lat_back,
    )
    outs = [pltpu.with_memory_space_constraint(o, pltpu.VMEM) for o in outs]
    mixed, grad_input, gw1, gb1, gw2, gb2, gg, gs = pl.pallas_call(
        write_out,
        out_shape=results,
        in_specs=[vmem] * 8,
        out_specs=tuple([anywhere] * 8),
        scratch_shapes=[pltpu.SemaphoreType.DMA((8,))],
    )(*outs)
    return (
        jnp.transpose(mixed, (2, 0, 1, 3)),
        jnp.transpose(grad_input, (2, 0, 1, 3)),
        gw1,
        gb1,
        gw2,
        gb2,
        gg.reshape(CB),
        gs.reshape(CB),
    )


def solution(mesh):
    placed = (
        P(None, "space", "chan", None),
        P("chan"),
        P("chan"),
        P(None, "chan", None, None),
        P(None, "chan", None),
        P(None, "chan", None, None),
        P(None, "chan", None),
        P(None, "space", "chan", None),
    )
    return jax.shard_map(
        on_device,
        mesh=mesh,
        in_specs=placed,
        out_specs=(
            P(None, "space", "chan", None),
            P(None, "space", "chan", None),
            P(None, "chan", None, None),
            P(None, "chan", None),
            P(None, "chan", None, None),
            P(None, "chan", None),
            P("chan"),
            P("chan"),
        ),
        check_vma=False,
    )
```

```python
import math

import jax
import jax.numpy as jnp
import ml_dtypes
import numpy as np
from jax import lax
from jax.experimental import pallas as pl
from jax.experimental.pallas import tpu as pltpu
from jax.sharding import PartitionSpec as P

C = 768
CB = 96
W = 180
WP = 192
MW = 64
H = 96
NS = 32
NC = 8
HL = H // NS
LN = 128
PL = 9 * LN
HB = 4 * CB

shrink_level = 0.05
norm_epsilon = 1e-05
gelu_scale = 0.7978845608
gelu_cubic = 0.044715
lon_factor = 1.0 / math.sqrt(W)
lat_factor = 1.0 / math.sqrt(H)

F32 = jnp.float32
BF16 = jnp.bfloat16
MESH = pl.DeviceIdType.MESH

RS1, AG1, A2, A1, A4, A3, RS2, AG2 = range(0, 16, 2)
GWR, GWG, GG = range(16, 19)


def twiddle(length, columns):
    rows = np.arange(length)[:, None]
    cols = np.arange(columns)[None, :]
    angles = (rows * cols % length).astype(np.float32) * np.float32(2.0 * math.pi / length)
    return (
        np.cos(angles).astype(np.float32),
        np.sin(angles).astype(np.float32),
    )


def tables():
    bf = ml_dtypes.bfloat16
    cos_lon, sin_lon = (t.astype(bf).astype(np.float32) for t in twiddle(W, MW))
    cos_lat, sin_lat = (t.astype(bf).astype(np.float32) for t in twiddle(H, H))
    lon = np.zeros((NS, 2, 2, WP), np.float32)
    scaled = np.zeros_like(lon)
    for d in range(NS):
        for mm in range(2):
            m = 2 * d + mm
            lon[d, 0, mm, :W] = cos_lon[:, m]
            lon[d, 1, mm, :W] = -sin_lon[:, m]
            scaled[d, :, mm] = (1.0 if m == 0 else 2.0) * lon[d, :, mm]
    lon = lon.reshape(4 * NS, WP)
    scaled = scaled.reshape(4 * NS, WP)
    lat = np.zeros((2, 2, H, HL, NS, 2, 2), np.float32)
    for hh in range(HL):
        cos_part = cos_lat[:, hh::HL]
        sin_part = sin_lat[:, hh::HL]
        for mm in range(2):
            lat[mm, 0, :, hh, :, 0, mm] = cos_part
            lat[mm, 0, :, hh, :, 1, mm] = sin_part
            lat[mm, 1, :, hh, :, 0, mm] = -sin_part
            lat[mm, 1, :, hh, :, 1, mm] = cos_part
    lat = lat.reshape(4 * H, 4 * H)
    return (
        np.stack([lon, scaled]).astype(bf),
        np.stack([lon.T, scaled.T]).astype(bf),
        lat.astype(bf),
        lat.T.astype(bf),
    )


def dot(left, right):
    return lax.dot_general(left, right, (((1,), (0,)), ((), ())), preferred_element_type=F32)


def dot_nt(left, right):
    return lax.dot_general(left, right, (((1,), (1,)), ((), ())), preferred_element_type=F32)


def dot_tn(left, right):
    return lax.dot_general(left, right, (((0,), (0,)), ((), ())), preferred_element_type=F32)


def unpack(source, target, h):
    lane = lax.broadcasted_iota(jnp.int32, (8, LN), 1)

    def step(it, carry):
        for u in range(15):
            i = it * 15 + u
            chunk = source[h, 0, :, pl.ds(pl.multiple_of(i * 384, 128), 384)].astype(F32)
            v0, v1, v2 = chunk[:, :128], chunk[:, 128:256], chunk[:, 256:]
            parts = (
                v0,
                pltpu.roll(jnp.where(lane >= 96, v0, v1), 32, 1),
                pltpu.roll(jnp.where(lane >= 64, v1, v2), 64, 1),
                pltpu.roll(v2, 96, 1),
            )
            for q in range(4):
                target[h, pl.ds(pl.multiple_of(i * 32 + 8 * q, 8), 8), :] = parts[q]
        return carry

    lax.fori_loop(0, 3, step, 0)


def pack(source, target, h):
    lane = lax.broadcasted_iota(jnp.int32, (8, LN), 1)

    def step(it, carry):
        for u in range(15):
            i = it * 15 + u
            p0, p1, p2, p3 = (
                source[h, pl.ds(pl.multiple_of(i * 32 + 8 * q, 8), 8), :] for q in range(4)
            )
            r1 = pltpu.roll(p1, 96, 1)
            r2 = pltpu.roll(p2, 64, 1)
            r3 = pltpu.roll(p3, 32, 1)
            chunk = jnp.concatenate(
                [
                    jnp.where(lane < 96, p0, r1),
                    jnp.where(lane < 64, r1, r2),
                    jnp.where(lane < 32, r2, r3),
                ],
                axis=1,
            )
            target[h, 0, :, pl.ds(pl.multiple_of(i * 384, 128), 384)] = chunk.astype(BF16)
        return carry

    lax.fori_loop(0, 3, step, 0)


def layer(
    x_hbm, cot_hbm, gain_hbm, shift_hbm, w1_hbm, b1_hbm, w2_hbm, b2_hbm,
    d_hbm, e_hbm, l_hbm, m_hbm,
    mixed_out, gin_out, gw1_ref, gb1_ref, gw2_ref, gb2_ref, gg_ref, gs_ref,
    xv, cv, dv, ev, lv, mv, tx, tc, xn, cen, gc,
    send1, send2, send3, send4, recv1, recv2, recv3, recv4,
    rc, lt, gsh, hid, gpost, gpre, sh, glat, wc, vec,
    acc, st, rb, ags, ab, at, acc2, st2, rb2, ags2, ab2, at2,
    gb, gr, gas, ga, ggs, ggr, small, w1_v, w2_v, b1_v, b2_v,
    in_sems, send_sems, recv_sems,
):
    me_s = lax.axis_index("space")
    me_c = lax.axis_index("chan")

    loads = [pltpu.make_async_copy(x_hbm.at[h], xv.at[h], in_sems.at[h]) for h in range(HL)]
    loads += [pltpu.make_async_copy(cot_hbm.at[h], cv.at[h], in_sems.at[3 + h]) for h in range(HL)]
    loads += [
        pltpu.make_async_copy(d_hbm, dv, in_sems.at[6]),
        pltpu.make_async_copy(e_hbm, ev, in_sems.at[7]),
        pltpu.make_async_copy(l_hbm, lv, in_sems.at[8]),
        pltpu.make_async_copy(m_hbm, mv, in_sems.at[9]),
        pltpu.make_async_copy(gain_hbm, small.at[0], in_sems.at[10]),
        pltpu.make_async_copy(shift_hbm, small.at[1], in_sems.at[11]),
        pltpu.make_async_copy(w1_hbm, w1_v, in_sems.at[12]),
        pltpu.make_async_copy(b1_hbm, b1_v, in_sems.at[13]),
        pltpu.make_async_copy(w2_hbm, w2_v, in_sems.at[14]),
        pltpu.make_async_copy(b2_hbm, b2_v, in_sems.at[15]),
    ]
    for load in loads:
        load.start()

    barrier = pltpu.get_barrier_semaphore()

    def greet_space(r, carry):
        pl.semaphore_signal(
            barrier, inc=1, device_id={"space": lax.rem(me_s + r, NS)}, device_id_type=MESH
        )
        return carry

    def greet_chan(r, carry):
        pl.semaphore_signal(
            barrier, inc=1, device_id={"chan": lax.rem(me_c + r, NC)}, device_id_type=MESH
        )
        return carry

    lax.fori_loop(1, NC, greet_chan, 0)
    lax.fori_loop(1, NS, greet_space, 0)

    def spread(axis, index, piece, target):
        count, me = (NS, me_s) if axis == "space" else (NC, me_c)

        def step(r, carry):
            t = lax.rem(me + r, count)
            pltpu.make_async_remote_copy(
                src_ref=piece(t),
                dst_ref=target.at[me],
                send_sem=send_sems.at[index],
                recv_sem=recv_sems.at[index],
                device_id={axis: t},
                device_id_type=MESH,
            ).start()
            return carry

        lax.fori_loop(1, count, step, 0)
        pltpu.make_async_copy(piece(me), target.at[me], recv_sems.at[index]).start()

    def arrived(index, target):
        pltpu.make_async_copy(target, target, recv_sems.at[index]).wait()

    def sent(index, target, count):
        rest = target.at[pl.ds(0, count - 1)]
        pltpu.make_async_copy(rest, rest, send_sems.at[index]).wait()

    tx[:, 8 * W :, :] = jnp.zeros((HL, 8 * (WP - W), LN), F32)
    tc[:, 8 * W :, :] = jnp.zeros((HL, 8 * (WP - W), LN), F32)
    acc[...] = jnp.zeros_like(acc)
    acc2[...] = jnp.zeros_like(acc2)
    ab[:, NC:] = jnp.zeros((2, NC, 8, LN), F32)
    ab2[:, NC:] = jnp.zeros((2, NC, 8, LN), F32)
    lane_t = lax.broadcasted_iota(jnp.int32, (4 * H, 2 * LN), 1)
    lane_h = lax.broadcasted_iota(jnp.int32, (H, LN), 1)
    lane_w = lax.broadcasted_iota(jnp.int32, (WP, LN), 1)

    def members_of(array, h, b):
        return array[h, pl.ds(b, WP, stride=8), :]

    def dense(tiles, lane):
        r1, r2, r3 = (pltpu.roll(tiles[i], LN - 32 * i, 1) for i in range(1, 4))
        return (
            jnp.where(lane < 96, tiles[0], r1),
            jnp.where(lane < 64, r1, r2),
            jnp.where(lane < 32, r2, r3),
        )

    def tile_of(array, rows, h, m, lane):
        start = HB * h + CB * m
        first, shift = start // LN * LN, start % LN
        left = array[rows, first : first + LN]
        if shift == 0:
            return left
        if shift > 32:
            right = array[rows, first + LN : first + 2 * LN]
            left = jnp.where(lane >= shift, left, right)
        return pltpu.roll(left, LN - shift, 1)

    def store_dense(s, h, tiles):
        for i, column in enumerate(dense(tiles, lane_w)):
            xn[s, :, HB * h + LN * i : HB * h + LN * i + LN] = column.astype(BF16)

    def pieces_of_sums(source, target):
        turned = jnp.transpose(source[...])
        for part in range(2):
            for m in range(4):
                target[4 * part + m] = turned[8 * m : 8 * m + 8, LN * part : LN * part + LN]

    def columns_of(source, target):
        turned = jnp.transpose(source[...].reshape(LN, LN))
        target[0:LN, 0:32] = turned[:, 0:32]
        target[LN:, 0:32] = turned[:, 32:64]

    for h in range(HL):
        loads[h].wait()
        unpack(xv, tx, h)

    def token_sums(s):
        total = jnp.zeros((WP, LN), F32)
        for m in range(4):
            for h in range(HL):
                tile = jnp.where(lane_w < CB, members_of(tx, h, 4 * s + m), 0.0)
                one = jnp.sum(tile, axis=1, keepdims=True)
                two = jnp.sum(tile * tile, axis=1, keepdims=True)
                total = jnp.where(lane_w == 8 * m + h, one, total)
                total = jnp.where(lane_w == 8 * m + 3 + h, two, total)
        acc[s, 0:WP, :] = total
        pieces_of_sums(acc.at[s], st.at[s])

    token_sums(0)
    pl.semaphore_wait(barrier, NS - 1 + NC - 1)
    spread("chan", RS1, lambda t: st.at[0, t], rb.at[0])
    token_sums(1)
    spread("chan", RS1 + 1, lambda t: st.at[1, t], rb.at[1])

    for k in range(10, 16):
        loads[k].wait()
    vec[...] = jnp.zeros_like(vec)
    vec[0:1, 0:CB] = small[0]
    vec[1:2, 0:CB] = small[1]
    for layer_at, (b_ref, w_ref) in enumerate(((b1_v, w1_v), (b2_v, w2_v))):
        vec[2 + layer_at : 3 + layer_at, 0:CB] = b_ref[0]
        vec[2 + layer_at : 3 + layer_at, LN : LN + CB] = b_ref[1]
        wc[layer_at] = jnp.zeros((2 * LN, 2 * LN), BF16)
        w_real, w_imag = w_ref[0, 0], w_ref[1, 0]
        wc[layer_at, 0:CB, 0:CB] = w_real
        wc[layer_at, 0:CB, LN : LN + CB] = w_imag
        wc[layer_at, LN : LN + CB, 0:CB] = -w_imag
        wc[layer_at, LN : LN + CB, LN : LN + CB] = w_real
    gain_row = vec[0:1, 0:LN]
    shift_row = vec[1:2, 0:LN]

    for h in range(HL):
        loads[3 + h].wait()
        unpack(cv, tc, h)
    loads[6].wait()

    def send_cotangent(s):
        for h in range(HL):
            store_dense(s, h, [members_of(tc, h, 4 * s + m) for m in range(4)])
        out = dot(dv[1], xn[s]) * lon_factor
        send2[s] = out.reshape(NS, 4, PL).astype(BF16)
        spread("space", A2 + s, lambda t: send2.at[s, t], recv2.at[s])

    def share_statistics(s):
        arrived(RS1 + s, rb.at[s])
        sums = jnp.sum(rb[s], axis=0) * (1.0 / C)
        var_in = pltpu.roll(sums, 5, 0)
        inv = lax.rsqrt(var_in - sums * sums + norm_epsilon)
        row8 = lax.broadcasted_iota(jnp.int32, (8, LN), 0)
        ags[s] = jnp.where(row8 < 3, sums, jnp.where(row8 < 6, pltpu.roll(inv, 3, 0), 0.0))
        spread("chan", AG1 + s, lambda t: ags.at[s], ab.at[s])

    send_cotangent(0)
    share_statistics(0)
    share_statistics(1)
    send_cotangent(1)

    def send_normed(s):
        arrived(AG1 + s, ab.at[s, pl.ds(0, NC)])
        columns_of(ab.at[s], at.at[s])
        for h in range(HL):
            tiles = []
            for m in range(4):
                column = 8 * m + h
                mean_col = at[s, 0:WP, column : column + 1]
                inv_col = at[s, 0:WP, column + 3 : column + 4]
                centred = (members_of(tx, h, 4 * s + m) - mean_col) * inv_col
                cen[s, 4 * h + m] = centred
                tiles.append(centred * gain_row + shift_row)
            store_dense(s, h, tiles)
        out = dot(dv[0], xn[s]) * lon_factor
        send1[s] = out.reshape(NS, 4, PL).astype(BF16)
        spread("space", A1 + s, lambda t: send1.at[s, t], recv1.at[s])

    send_normed(0)
    send_normed(1)

    def latitude(received, target, ones):
        for h in range(HL):
            rc[LN * h : LN * h + LN, :] = received[:, :, HB * h : HB * h + HB].reshape(LN, HB)
        out = dot(lv[...], rc[...]) * lat_factor
        for mm in range(2):
            for part in range(2):
                rows = slice(2 * H * mm + H * part, 2 * H * mm + H * part + H)
                for m in range(4):
                    tile = tile_of(out, rows, 0, m, lane_h)
                    if ones:
                        tile = jnp.where(lane_h == CB, 1.0 - part, tile)
                    target[mm, H * m : H * m + H, LN * part : LN * part + LN] = tile.astype(BF16)

    loads[8].wait()

    def mix(s):
        def step(i, carry):
            pre = dot(lt[s, i], wc[0]) + vec[2:3, :]
            t = jnp.tanh(gelu_scale * (pre + gelu_cubic * pre * pre * pre))
            hidden = 0.5 * pre * (1.0 + t)
            hidden = jnp.where(lane_t == CB, 1.0, hidden).astype(BF16)
            slope = 0.5 * (1.0 + t) + 0.5 * pre * (1.0 - t * t) * gelu_scale * (
                1.0 + 3.0 * gelu_cubic * pre * pre
            )
            hid[s, i] = hidden
            post = dot(hidden, wc[1]) + vec[3:4, :]
            shape = jnp.tanh(post * (1.0 / shrink_level))
            shrunk = post - shrink_level * shape
            grad_post = (gsh[s, i].astype(F32) * (shape * shape)).astype(BF16)
            gpost[s, i] = grad_post
            grad_pre = (dot_nt(grad_post, wc[1]) * slope).astype(BF16)
            gpre[s, i] = grad_pre
            grad_lat = dot_nt(grad_pre, wc[0])
            for source, target in ((shrunk, sh), (grad_lat, glat)):
                for part in range(2):
                    tiles = [
                        source[H * m : H * m + H, LN * part : LN * part + LN] for m in range(4)
                    ]
                    for j, column in enumerate(dense(tiles, lane_h)):
                        target[s, i, H * part : H * part + H, LN * j : LN * j + LN] = (
                            column.astype(BF16)
                        )
            return carry

        lax.fori_loop(0, 2, step, 0)

    def back(source, target):
        out = dot(mv[...], source[...].reshape(4 * H, HB)) * lat_factor
        for h in range(HL):
            piece = out[LN * h : LN * h + LN, :].reshape(NS, 4, HB)
            target[:, :, HB * h : HB * h + HB] = piece.astype(BF16)

    for s in range(2):
        arrived(A2 + s, recv2.at[s])
        latitude(recv2.at[s], gsh.at[s], False)
    loads[9].wait()
    for s in range(2):
        arrived(A1 + s, recv1.at[s])
        latitude(recv1.at[s], lt.at[s], True)
        mix(s)
        back(glat.at[s], send4.at[s])
        spread("space", A4 + s, lambda t, s=s: send4.at[s, t], recv4.at[s])
        if s == 1:
            spread("space", A3, lambda t: send3.at[0, t], recv3.at[0])
        back(sh.at[s], send3.at[s])

    for layer_at, (left, right) in enumerate(((lt, gpre), (hid, gpost))):
        outer = dot_tn(left[...].reshape(16 * H, 2 * LN), right[...].reshape(16 * H, 2 * LN))
        real = outer[0:LN, 0:LN] + outer[LN:, LN:]
        imag = outer[0:LN, LN:] - outer[LN:, 0:LN]
        gb[16 * layer_at : 16 * layer_at + 8] = real.reshape(8, 16, LN).astype(BF16)
        gb[16 * layer_at + 8 : 16 * layer_at + 16] = imag.reshape(8, 16, LN).astype(BF16)
    spread("space", GWR, lambda t: gb.at[t], gr)
    spread("space", A3 + 1, lambda t: send3.at[1, t], recv3.at[1])

    loads[7].wait()
    norm_sums = [jnp.zeros((8, LN), F32), jnp.zeros((8, LN), F32)]

    def gradient_sums(s):
        arrived(A4 + s, recv4.at[s])
        out = dot(ev[0], recv4[s].reshape(4 * NS, PL)) * lon_factor
        total = jnp.zeros((WP, LN), F32)
        for h in range(HL):
            for m in range(4):
                grad_normed = tile_of(out, slice(0, WP), h, m, lane_w)
                centred = cen[s, 4 * h + m]
                product = grad_normed * centred
                norm_sums[0] = norm_sums[0] + jnp.sum(product.reshape(WP // 8, 8, LN), axis=0)
                norm_sums[1] = norm_sums[1] + jnp.sum(grad_normed.reshape(WP // 8, 8, LN), axis=0)
                grad_centred = grad_normed * gain_row
                gc[s, 4 * h + m] = grad_centred
                one = jnp.sum(grad_centred, axis=1, keepdims=True)
                two = jnp.sum(grad_centred * centred, axis=1, keepdims=True)
                total = jnp.where(lane_w == 8 * m + h, one, total)
                total = jnp.where(lane_w == 8 * m + 3 + h, two, total)
        acc2[s, 0:WP, :] = total
        pieces_of_sums(acc2.at[s], st2.at[s])
        spread("chan", RS2 + s, lambda t: st2.at[s, t], rb2.at[s])

    gradient_sums(0)
    gradient_sums(1)

    def share_gradient_sums(s):
        arrived(RS2 + s, rb2.at[s])
        ags2[s] = jnp.sum(rb2[s], axis=0) * (1.0 / C)
        spread("chan", AG2 + s, lambda t: ags2.at[s], ab2.at[s])

    share_gradient_sums(0)
    ggs[0:1, :] = jnp.sum(norm_sums[0], axis=0, keepdims=True)
    ggs[1:2, :] = jnp.sum(norm_sums[1], axis=0, keepdims=True)
    spread("space", GG, lambda t: ggs, ggr)

    def put_mixed(s):
        arrived(A3 + s, recv3.at[s])
        out = dot(ev[1], recv3[s].reshape(4 * NS, PL)) * lon_factor
        for h in range(HL):
            for m in range(4):
                put_members(tc, h, 4 * s + m, tile_of(out, slice(0, WP), h, m, lane_w))

    def put_members(array, h, b, tile):
        array[h, pl.ds(b, WP, stride=8), :] = tile

    def put_gradient(s):
        arrived(AG2 + s, ab2.at[s, pl.ds(0, NC)])
        columns_of(ab2.at[s], at2.at[s])
        for h in range(HL):
            for m in range(4):
                column = 8 * m + h
                inv_col = at[s, 0:WP, column + 3 : column + 4]
                first = at2[s, 0:WP, column : column + 1]
                second = at2[s, 0:WP, column + 3 : column + 4]
                put_members(
                    tx,
                    h,
                    4 * s + m,
                    inv_col * (gc[s, 4 * h + m] - first - cen[s, 4 * h + m] * second),
                )

    put_mixed(0)
    share_gradient_sums(1)
    put_gradient(0)
    arrived(GWR, gr)
    gas[...] = jnp.sum(gr[...].astype(F32), axis=0).astype(BF16)
    spread("space", GWG, lambda t: gas, ga)
    put_gradient(1)
    for h in range(HL):
        pack(tx, gin_out, h)
    put_mixed(1)
    for h in range(HL):
        pack(tc, mixed_out, h)

    arrived(GG, ggr)
    both = jnp.sum(ggr[...], axis=0)
    gg_ref[...] = both[0:1, 0:CB]
    gs_ref[...] = both[1:2, 0:CB]
    arrived(GWG, ga)
    for layer_at, (gw_ref, gbias_ref) in enumerate(((gw1_ref, gb1_ref), (gw2_ref, gb2_ref))):
        for part in range(2):
            at_piece = 16 * layer_at + 8 * part
            block = ga[at_piece : at_piece + 8].astype(F32).reshape(LN, LN)
            gw_ref[part, 0] = block[0:CB, 0:CB]
            gbias_ref[part] = block[CB : CB + 1, 0:CB]

    for s in range(2):
        sent(RS1 + s, rb.at[s], NC)
        sent(AG1 + s, ab.at[s], NC)
        sent(RS2 + s, rb2.at[s], NC)
        sent(AG2 + s, ab2.at[s], NC)
        sent(A2 + s, recv2.at[s], NS)
        sent(A1 + s, recv1.at[s], NS)
        sent(A4 + s, recv4.at[s], NS)
        sent(A3 + s, recv3.at[s], NS)
    sent(GWR, gr, NS)
    sent(GWG, ga, NS)
    sent(GG, ggr, NS)


def write_out(*refs):
    count = (len(refs) - 1) // 2
    sems = refs[-1]
    copies = [
        pltpu.make_async_copy(refs[i], refs[count + i], sems.at[i]) for i in range(count)
    ]
    for copy in copies:
        copy.start()
    for copy in copies:
        copy.wait()


def on_device(members, gain, shift, w_first, b_first, w_second, b_second, cotangent):
    lon_out, lon_back, lat_out, lat_back = (jnp.asarray(t) for t in tables())
    anywhere = pl.BlockSpec(memory_space=pl.ANY)
    vmem = pl.BlockSpec(memory_space=pltpu.VMEM)
    stays = pl.BlockSpec(memory_space=pltpu.HBM)
    token = (HL, 1, 8, W * CB)
    piece = (2, NS, 4, PL)
    spectral = (2, 2, 4 * H, 2 * LN)
    folded = (2, 2, 2 * H, HB)
    results = (
        jax.ShapeDtypeStruct(token, BF16),
        jax.ShapeDtypeStruct(token, BF16),
        jax.ShapeDtypeStruct((2, 1, CB, CB), F32),
        jax.ShapeDtypeStruct((2, 1, CB), F32),
        jax.ShapeDtypeStruct((2, 1, CB, CB), F32),
        jax.ShapeDtypeStruct((2, 1, CB), F32),
        jax.ShapeDtypeStruct((1, CB), F32),
        jax.ShapeDtypeStruct((1, CB), F32),
    )
    outs = pl.pallas_call(
        layer,
        out_shape=tuple(pltpu.VMEM(r.shape, r.dtype) for r in results),
        in_specs=[stays] * 12,
        out_specs=tuple([vmem] * 8),
        scratch_shapes=[
            pltpu.VMEM(token, BF16),
            pltpu.VMEM(token, BF16),
            pltpu.VMEM((2, 4 * NS, WP), BF16),
            pltpu.VMEM((2, WP, 4 * NS), BF16),
            pltpu.VMEM((4 * H, 4 * H), BF16),
            pltpu.VMEM((4 * H, 4 * H), BF16),
            pltpu.VMEM((HL, 8 * WP, LN), F32),
            pltpu.VMEM((HL, 8 * WP, LN), F32),
            pltpu.VMEM((2, WP, PL), BF16),
            pltpu.VMEM((2, 4 * HL, WP, LN), F32),
            pltpu.VMEM((2, 4 * HL, WP, LN), F32),
        ]
        + [pltpu.VMEM(piece, BF16)] * 8
        + [pltpu.VMEM((4 * H, HB), BF16)]
        + [pltpu.VMEM(spectral, BF16)] * 5
        + [pltpu.VMEM(folded, BF16)] * 2
        + [
            pltpu.VMEM((2, 2 * LN, 2 * LN), BF16),
            pltpu.VMEM((8, 2 * LN), F32),
        ]
        + [
            pltpu.VMEM((2, 2 * LN, LN), F32),
            pltpu.VMEM((2, NC, 8, LN), F32),
            pltpu.VMEM((2, NC, 8, LN), F32),
            pltpu.VMEM((2, 8, LN), F32),
            pltpu.VMEM((2, 2 * NC, 8, LN), F32),
            pltpu.VMEM((2, 2 * LN, LN), F32),
        ]
        * 2
        + [
            pltpu.VMEM((NS, 16, LN), BF16),
            pltpu.VMEM((NS, 16, LN), BF16),
            pltpu.VMEM((16, LN), BF16),
            pltpu.VMEM((NS, 16, LN), BF16),
            pltpu.VMEM((2, LN), F32),
            pltpu.VMEM((NS, 2, LN), F32),
            pltpu.VMEM((2, 1, CB), F32),
            pltpu.VMEM((2, 1, CB, CB), BF16),
            pltpu.VMEM((2, 1, CB, CB), BF16),
            pltpu.VMEM((2, 1, CB), F32),
            pltpu.VMEM((2, 1, CB), F32),
            pltpu.SemaphoreType.DMA((16,)),
            pltpu.SemaphoreType.DMA((19,)),
            pltpu.SemaphoreType.DMA((19,)),
        ],
        compiler_params=pltpu.CompilerParams(
            collective_id=0, has_side_effects=True, vmem_limit_bytes=60 * 1024 * 1024
        ),
    )(
        jnp.transpose(members, (1, 2, 0, 3)),
        jnp.transpose(cotangent, (1, 2, 0, 3)),
        gain.reshape(1, CB),
        shift.reshape(1, CB),
        w_first,
        b_first,
        w_second,
        b_second,
        lon_out,
        lon_back,
        lat_out,
        lat_back,
    )
    outs = [pltpu.with_memory_space_constraint(o, pltpu.VMEM) for o in outs]
    mixed, grad_input, gw1, gb1, gw2, gb2, gg, gs = pl.pallas_call(
        write_out,
        out_shape=results,
        in_specs=[vmem] * 8,
        out_specs=tuple([anywhere] * 8),
        scratch_shapes=[pltpu.SemaphoreType.DMA((8,))],
    )(*outs)
    return (
        jnp.transpose(mixed, (2, 0, 1, 3)),
        jnp.transpose(grad_input, (2, 0, 1, 3)),
        gw1,
        gb1,
        gw2,
        gb2,
        gg.reshape(CB),
        gs.reshape(CB),
    )


def solution(mesh):
    placed = (
        P(None, "space", "chan", None),
        P("chan"),
        P("chan"),
        P(None, "chan", None, None),
        P(None, "chan", None),
        P(None, "chan", None, None),
        P(None, "chan", None),
        P(None, "space", "chan", None),
    )
    return jax.shard_map(
        on_device,
        mesh=mesh,
        in_specs=placed,
        out_specs=(
            P(None, "space", "chan", None),
            P(None, "space", "chan", None),
            P(None, "chan", None, None),
            P(None, "chan", None),
            P(None, "chan", None, None),
            P(None, "chan", None),
            P("chan"),
            P("chan"),
        ),
        check_vma=False,
    )
```

```python
import math

import jax
import jax.numpy as jnp
import ml_dtypes
import numpy as np
from jax import lax
from jax.experimental import pallas as pl
from jax.experimental.pallas import tpu as pltpu
from jax.sharding import PartitionSpec as P

C = 768
CB = 96
W = 180
WP = 192
MW = 64
H = 96
NS = 32
NC = 8
HL = H // NS
LN = 128
PL = 9 * LN
HB = 4 * CB

shrink_level = 0.05
norm_epsilon = 1e-05
gelu_scale = 0.7978845608
gelu_cubic = 0.044715
lon_factor = 1.0 / math.sqrt(W)
lat_factor = 1.0 / math.sqrt(H)

F32 = jnp.float32
BF16 = jnp.bfloat16
MESH = pl.DeviceIdType.MESH

RS1, AG1, A2, A1, A4, A3, RS2, AG2 = range(0, 16, 2)
GWR, GWG = range(16, 18)


def twiddle(length, columns):
    rows = np.arange(length)[:, None]
    cols = np.arange(columns)[None, :]
    angles = (rows * cols % length).astype(np.float32) * np.float32(2.0 * math.pi / length)
    return (
        np.cos(angles).astype(np.float32),
        np.sin(angles).astype(np.float32),
    )


def tables():
    bf = ml_dtypes.bfloat16
    cos_lon, sin_lon = (t.astype(bf).astype(np.float32) for t in twiddle(W, MW))
    cos_lat, sin_lat = (t.astype(bf).astype(np.float32) for t in twiddle(H, H))
    lon = np.zeros((NS, 2, 2, WP), np.float32)
    scaled = np.zeros_like(lon)
    for d in range(NS):
        for mm in range(2):
            m = 2 * d + mm
            lon[d, 0, mm, :W] = cos_lon[:, m]
            lon[d, 1, mm, :W] = -sin_lon[:, m]
            scaled[d, :, mm] = (1.0 if m == 0 else 2.0) * lon[d, :, mm]
    lon = lon.reshape(4 * NS, WP)
    scaled = scaled.reshape(4 * NS, WP)
    lat = np.zeros((2, 2, H, HL, NS, 2, 2), np.float32)
    for hh in range(HL):
        cos_part = cos_lat[:, hh::HL]
        sin_part = sin_lat[:, hh::HL]
        for mm in range(2):
            lat[mm, 0, :, hh, :, 0, mm] = cos_part
            lat[mm, 0, :, hh, :, 1, mm] = sin_part
            lat[mm, 1, :, hh, :, 0, mm] = -sin_part
            lat[mm, 1, :, hh, :, 1, mm] = cos_part
    lat = lat.reshape(4 * H, 4 * H)
    picked = np.zeros((HL, 4, 2, LN, LN), np.float32)
    for h in range(HL):
        for m in range(4):
            for q in range(2):
                picked[h, m, q, :CB, 8 * m + 3 * q + h] = 1.0
    return (
        np.stack([lon, scaled]).astype(bf),
        np.stack([lon.T, scaled.T]).astype(bf),
        lat.astype(bf),
        lat.T.astype(bf),
        picked.reshape(8 * HL * LN, LN).astype(bf),
    )


def dot(left, right):
    return lax.dot_general(left, right, (((1,), (0,)), ((), ())), preferred_element_type=F32)


def dot_nt(left, right):
    return lax.dot_general(left, right, (((1,), (1,)), ((), ())), preferred_element_type=F32)


def dot_tn(left, right):
    return lax.dot_general(left, right, (((0,), (0,)), ((), ())), preferred_element_type=F32)


def unpack(source, target, h):
    lane = lax.broadcasted_iota(jnp.int32, (8, LN), 1)

    def step(it, carry):
        for u in range(15):
            i = it * 15 + u
            chunk = source[h, 0, :, pl.ds(pl.multiple_of(i * 384, 128), 384)].astype(F32)
            v0, v1, v2 = chunk[:, :128], chunk[:, 128:256], chunk[:, 256:]
            parts = (
                v0,
                pltpu.roll(jnp.where(lane >= 96, v0, v1), 32, 1),
                pltpu.roll(jnp.where(lane >= 64, v1, v2), 64, 1),
                pltpu.roll(v2, 96, 1),
            )
            for q in range(4):
                target[h, pl.ds(pl.multiple_of(i * 32 + 8 * q, 8), 8), :] = parts[q]
        return carry

    lax.fori_loop(0, 3, step, 0)


def pack(source, target, h):
    lane = lax.broadcasted_iota(jnp.int32, (8, LN), 1)

    def step(it, carry):
        for u in range(15):
            i = it * 15 + u
            p0, p1, p2, p3 = (
                source[h, pl.ds(pl.multiple_of(i * 32 + 8 * q, 8), 8), :] for q in range(4)
            )
            r1 = pltpu.roll(p1, 96, 1)
            r2 = pltpu.roll(p2, 64, 1)
            r3 = pltpu.roll(p3, 32, 1)
            chunk = jnp.concatenate(
                [
                    jnp.where(lane < 96, p0, r1),
                    jnp.where(lane < 64, r1, r2),
                    jnp.where(lane < 32, r2, r3),
                ],
                axis=1,
            )
            target[h, 0, :, pl.ds(pl.multiple_of(i * 384, 128), 384)] = chunk.astype(BF16)
        return carry

    lax.fori_loop(0, 3, step, 0)


def layer(
    x_hbm, cot_hbm, gain_hbm, shift_hbm, w1_hbm, b1_hbm, w2_hbm, b2_hbm,
    d_hbm, e_hbm, l_hbm, m_hbm, pick_hbm,
    mixed_out, gin_out, gw1_ref, gb1_ref, gw2_ref, gb2_ref, gg_ref, gs_ref,
    xv, cv, dv, ev, lv, mv, tx, tc, xn, cen, gc,
    send1, send2, send3, send4, recv1, recv2, recv3, recv4,
    rc, lt, gsh, hid, gpost, gpre, sh, glat, wc, vec,
    acc, st, rb, ags, ab, at, acc2, st2, rb2, ags2, ab2, at2,
    gb, gr, gas, ga, invb, terms, pick, small, w1_v, w2_v, b1_v, b2_v,
    in_sems, send_sems, recv_sems,
):
    me_s = lax.axis_index("space")
    me_c = lax.axis_index("chan")

    loads = [pltpu.make_async_copy(x_hbm.at[h], xv.at[h], in_sems.at[h]) for h in range(HL)]
    loads += [pltpu.make_async_copy(cot_hbm.at[h], cv.at[h], in_sems.at[3 + h]) for h in range(HL)]
    loads += [
        pltpu.make_async_copy(d_hbm, dv, in_sems.at[6]),
        pltpu.make_async_copy(e_hbm, ev, in_sems.at[7]),
        pltpu.make_async_copy(l_hbm, lv, in_sems.at[8]),
        pltpu.make_async_copy(m_hbm, mv, in_sems.at[9]),
        pltpu.make_async_copy(gain_hbm, small.at[0], in_sems.at[10]),
        pltpu.make_async_copy(shift_hbm, small.at[1], in_sems.at[11]),
        pltpu.make_async_copy(w1_hbm, w1_v, in_sems.at[12]),
        pltpu.make_async_copy(b1_hbm, b1_v, in_sems.at[13]),
        pltpu.make_async_copy(w2_hbm, w2_v, in_sems.at[14]),
        pltpu.make_async_copy(b2_hbm, b2_v, in_sems.at[15]),
        pltpu.make_async_copy(pick_hbm, pick, in_sems.at[16]),
    ]
    for load in loads:
        load.start()

    barrier = pltpu.get_barrier_semaphore()

    def greet_space(r, carry):
        pl.semaphore_signal(
            barrier, inc=1, device_id={"space": lax.rem(me_s + r, NS)}, device_id_type=MESH
        )
        return carry

    def greet_chan(r, carry):
        pl.semaphore_signal(
            barrier, inc=1, device_id={"chan": lax.rem(me_c + r, NC)}, device_id_type=MESH
        )
        return carry

    lax.fori_loop(1, NC, greet_chan, 0)
    lax.fori_loop(1, NS, greet_space, 0)

    def spread(axis, index, piece, target, slot=None):
        slot = slot or (lambda t: target.at[t])
        count, me = (NS, me_s) if axis == "space" else (NC, me_c)

        def step(r, carry):
            t = lax.rem(me + r, count)
            pltpu.make_async_remote_copy(
                src_ref=piece(t),
                dst_ref=slot(me),
                send_sem=send_sems.at[index],
                recv_sem=recv_sems.at[index],
                device_id={axis: t},
                device_id_type=MESH,
            ).start()
            return carry

        lax.fori_loop(1, count, step, 0)
        pltpu.make_async_copy(piece(me), slot(me), recv_sems.at[index]).start()

    def arrived(index, target):
        pltpu.make_async_copy(target, target, recv_sems.at[index]).wait()

    def sent(index, target, count):
        rest = target.at[pl.ds(0, count - 1)]
        pltpu.make_async_copy(rest, rest, send_sems.at[index]).wait()

    tx[:, 8 * W :, :] = jnp.zeros((HL, 8 * (WP - W), LN), F32)
    tc[:, 8 * W :, :] = jnp.zeros((HL, 8 * (WP - W), LN), F32)
    acc[...] = jnp.zeros_like(acc)
    acc2[...] = jnp.zeros_like(acc2)
    ab[:, NC:] = jnp.zeros((2, NC, 8, LN), F32)
    ab2[:, NC:] = jnp.zeros((2, NC, 8, LN), F32)
    lane_t = lax.broadcasted_iota(jnp.int32, (4 * H, 2 * LN), 1)
    lane_h = lax.broadcasted_iota(jnp.int32, (H, LN), 1)
    lane_w = lax.broadcasted_iota(jnp.int32, (WP, LN), 1)

    def members_of(array, h, b):
        return array[h, pl.ds(b, WP, stride=8), :]

    def dense(tiles, lane):
        r1, r2, r3 = (pltpu.roll(tiles[i], LN - 32 * i, 1) for i in range(1, 4))
        return (
            jnp.where(lane < 96, tiles[0], r1),
            jnp.where(lane < 64, r1, r2),
            jnp.where(lane < 32, r2, r3),
        )

    def tile_of(array, rows, h, m, lane):
        start = HB * h + CB * m
        first, shift = start // LN * LN, start % LN
        left = array[rows, first : first + LN]
        if shift == 0:
            return left
        if shift > 32:
            right = array[rows, first + LN : first + 2 * LN]
            left = jnp.where(lane >= shift, left, right)
        return pltpu.roll(left, LN - shift, 1)

    def store_dense(s, h, tiles):
        for i, column in enumerate(dense(tiles, lane_w)):
            xn[s, :, HB * h + LN * i : HB * h + LN * i + LN] = column.astype(BF16)

    def pieces_of_sums(source, target):
        turned = jnp.transpose(source[...])
        for part in range(2):
            for m in range(4):
                target[4 * part + m] = turned[8 * m : 8 * m + 8, LN * part : LN * part + LN]

    def columns_of(source, target):
        turned = jnp.transpose(source[...].reshape(LN, LN))
        target[0:LN, 0:32] = turned[:, 0:32]
        target[LN:, 0:32] = turned[:, 32:64]

    for h in range(HL):
        loads[h].wait()
        unpack(xv, tx, h)

    def token_sums(s):
        total = jnp.zeros((WP, LN), F32)
        for m in range(4):
            for h in range(HL):
                tile = jnp.where(lane_w < CB, members_of(tx, h, 4 * s + m), 0.0)
                one = jnp.sum(tile, axis=1, keepdims=True)
                two = jnp.sum(tile * tile, axis=1, keepdims=True)
                total = jnp.where(lane_w == 8 * m + h, one, total)
                total = jnp.where(lane_w == 8 * m + 3 + h, two, total)
        acc[s, 0:WP, :] = total
        pieces_of_sums(acc.at[s], st.at[s])

    token_sums(0)
    pl.semaphore_wait(barrier, NS - 1 + NC - 1)
    spread("chan", RS1, lambda t: st.at[0, t], rb.at[0])
    token_sums(1)
    spread("chan", RS1 + 1, lambda t: st.at[1, t], rb.at[1])

    for k in range(10, 16):
        loads[k].wait()
    vec[...] = jnp.zeros_like(vec)
    vec[0:1, 0:CB] = small[0]
    vec[1:2, 0:CB] = small[1]
    for layer_at, (b_ref, w_ref) in enumerate(((b1_v, w1_v), (b2_v, w2_v))):
        vec[2 + layer_at : 3 + layer_at, 0:CB] = b_ref[0]
        vec[2 + layer_at : 3 + layer_at, LN : LN + CB] = b_ref[1]
        wc[layer_at] = jnp.zeros((2 * LN, 2 * LN), BF16)
        w_real, w_imag = w_ref[0, 0], w_ref[1, 0]
        wc[layer_at, 0:CB, 0:CB] = w_real
        wc[layer_at, 0:CB, LN : LN + CB] = w_imag
        wc[layer_at, LN : LN + CB, 0:CB] = -w_imag
        wc[layer_at, LN : LN + CB, LN : LN + CB] = w_real
    gain_row = vec[0:1, 0:LN]
    shift_row = vec[1:2, 0:LN]

    for h in range(HL):
        loads[3 + h].wait()
        unpack(cv, tc, h)
    loads[6].wait()

    def cotangent_spectra(s):
        for h in range(HL):
            store_dense(s, h, [members_of(tc, h, 4 * s + m) for m in range(4)])
        out = dot(dv[1], xn[s]) * lon_factor
        send2[s] = out.reshape(NS, 4, PL).astype(BF16)

    def share_statistics(s):
        arrived(RS1 + s, rb.at[s])
        sums = jnp.sum(rb[s], axis=0) * (1.0 / C)
        var_in = pltpu.roll(sums, 5, 0)
        inv = lax.rsqrt(var_in - sums * sums + norm_epsilon)
        row8 = lax.broadcasted_iota(jnp.int32, (8, LN), 0)
        ags[s] = jnp.where(row8 < 3, sums, jnp.where(row8 < 6, pltpu.roll(inv, 3, 0), 0.0))
        spread("chan", AG1 + s, lambda t: ags.at[s], ab.at[s])

    cotangent_spectra(0)
    share_statistics(0)
    share_statistics(1)
    spread("space", A2, lambda t: send2.at[0, t], recv2.at[0])
    cotangent_spectra(1)
    spread("space", A2 + 1, lambda t: send2.at[1, t], recv2.at[1])

    def send_normed(s):
        arrived(AG1 + s, ab.at[s, pl.ds(0, NC)])
        columns_of(ab.at[s], at.at[s])
        for h in range(HL):
            tiles = []
            for m in range(4):
                column = 8 * m + h
                mean_col = at[s, 0:WP, column : column + 1]
                inv_col = at[s, 0:WP, column + 3 : column + 4]
                inv_tile = jnp.broadcast_to(inv_col, (WP, LN))
                invb[s, 4 * h + m] = inv_tile
                centred = (members_of(tx, h, 4 * s + m) - mean_col) * inv_tile
                cen[s, 4 * h + m] = centred
                tiles.append(centred * gain_row + shift_row)
            store_dense(s, h, tiles)
        out = dot(dv[0], xn[s]) * lon_factor
        send1[s] = out.reshape(NS, 4, PL).astype(BF16)
        spread("space", A1 + s, lambda t: send1.at[s, t], recv1.at[s])

    send_normed(0)
    send_normed(1)

    def latitude(received, target, ones):
        for h in range(HL):
            rc[LN * h : LN * h + LN, :] = received[:, :, HB * h : HB * h + HB].reshape(LN, HB)
        out = dot(lv[...], rc[...]) * lat_factor
        for mm in range(2):
            for part in range(2):
                rows = slice(2 * H * mm + H * part, 2 * H * mm + H * part + H)
                for m in range(4):
                    tile = tile_of(out, rows, 0, m, lane_h)
                    if ones:
                        tile = jnp.where(lane_h == CB, 1.0 - part, tile)
                    target[mm, H * m : H * m + H, LN * part : LN * part + LN] = tile.astype(BF16)

    loads[8].wait()

    def mix(s):
        def step(i, carry):
            pre = dot(lt[s, i], wc[0]) + vec[2:3, :]
            t = jnp.tanh(gelu_scale * (pre + gelu_cubic * pre * pre * pre))
            hidden = 0.5 * pre * (1.0 + t)
            hidden = jnp.where(lane_t == CB, 1.0, hidden).astype(BF16)
            slope = 0.5 * (1.0 + t) + 0.5 * pre * (1.0 - t * t) * gelu_scale * (
                1.0 + 3.0 * gelu_cubic * pre * pre
            )
            hid[s, i] = hidden
            post = dot(hidden, wc[1]) + vec[3:4, :]
            shape = jnp.tanh(post * (1.0 / shrink_level))
            shrunk = post - shrink_level * shape
            grad_post = (gsh[s, i].astype(F32) * (shape * shape)).astype(BF16)
            gpost[s, i] = grad_post
            grad_pre = (dot_nt(grad_post, wc[1]) * slope).astype(BF16)
            gpre[s, i] = grad_pre
            grad_lat = dot_nt(grad_pre, wc[0])
            for source, target in ((shrunk, sh), (grad_lat, glat)):
                for part in range(2):
                    tiles = [
                        source[H * m : H * m + H, LN * part : LN * part + LN] for m in range(4)
                    ]
                    for j, column in enumerate(dense(tiles, lane_h)):
                        target[s, i, H * part : H * part + H, LN * j : LN * j + LN] = (
                            column.astype(BF16)
                        )
            return carry

        lax.fori_loop(0, 2, step, 0)

    def back(source, target):
        out = dot(mv[...], source[...].reshape(4 * H, HB)) * lat_factor
        for h in range(HL):
            piece = out[LN * h : LN * h + LN, :].reshape(NS, 4, HB)
            target[:, :, HB * h : HB * h + HB] = piece.astype(BF16)

    for s in range(2):
        arrived(A2 + s, recv2.at[s])
        latitude(recv2.at[s], gsh.at[s], False)
    loads[9].wait()
    for s in range(2):
        arrived(A1 + s, recv1.at[s])
        latitude(recv1.at[s], lt.at[s], True)
        mix(s)
        back(glat.at[s], send4.at[s])
        spread("space", A4 + s, lambda t, s=s: send4.at[s, t], recv4.at[s])
        back(sh.at[s], send3.at[s])
    spread("space", A3, lambda t: send3.at[:, t], recv3, lambda t: recv3.at[:, t])

    for layer_at, (left, right) in enumerate(((lt, gpre), (hid, gpost))):
        outer = dot_tn(left[...].reshape(16 * H, 2 * LN), right[...].reshape(16 * H, 2 * LN))
        real = outer[0:LN, 0:LN] + outer[LN:, LN:]
        imag = outer[0:LN, LN:] - outer[LN:, 0:LN]
        gb[16 * layer_at : 16 * layer_at + 8] = real.reshape(8, 16, LN).astype(BF16)
        gb[16 * layer_at + 8 : 16 * layer_at + 16] = imag.reshape(8, 16, LN).astype(BF16)

    loads[7].wait()
    loads[16].wait()
    norm_sums = [jnp.zeros((8, LN), F32), jnp.zeros((8, LN), F32)]

    def gradient_sums(s):
        arrived(A4 + s, recv4.at[s])
        out = dot(ev[0], recv4[s].reshape(4 * NS, PL)) * lon_factor
        for h in range(HL):
            for m in range(4):
                grad_normed = tile_of(out, slice(0, WP), h, m, lane_w)
                centred = cen[s, 4 * h + m]
                product = grad_normed * centred
                norm_sums[0] = norm_sums[0] + jnp.sum(product.reshape(WP // 8, 8, LN), axis=0)
                norm_sums[1] = norm_sums[1] + jnp.sum(grad_normed.reshape(WP // 8, 8, LN), axis=0)
                grad_centred = grad_normed * gain_row
                i = 4 * h + m
                gc[s, i] = grad_centred * invb[s, i]
                terms[:, 2 * LN * i : 2 * LN * i + LN] = grad_centred.astype(BF16)
                terms[:, 2 * LN * i + LN : 2 * LN * i + 2 * LN] = (
                    grad_centred * centred
                ).astype(BF16)
        acc2[s, 0:WP, :] = dot(terms[...], pick[...])
        pieces_of_sums(acc2.at[s], st2.at[s])
        spread("chan", RS2 + s, lambda t: st2.at[s, t], rb2.at[s])

    gradient_sums(0)
    gradient_sums(1)

    def share_gradient_sums(s):
        arrived(RS2 + s, rb2.at[s])
        ags2[s] = jnp.sum(rb2[s], axis=0) * (1.0 / C)
        spread("chan", AG2 + s, lambda t: ags2.at[s], ab2.at[s])

    share_gradient_sums(0)
    row16 = lax.broadcasted_iota(jnp.int32, (16, LN), 0)
    spare = jnp.where(
        row16 == 1,
        jnp.sum(norm_sums[0], axis=0, keepdims=True),
        jnp.sum(norm_sums[1], axis=0, keepdims=True),
    )
    gb[CB // 16] = jnp.where(
        (row16 == 1) | (row16 == 2), spare, gb[CB // 16].astype(F32)
    ).astype(BF16)
    spread("space", GWR, lambda t: gb.at[t], gr)

    def put_mixed(s):
        out = dot(ev[1], recv3[s].reshape(4 * NS, PL)) * lon_factor
        for h in range(HL):
            for m in range(4):
                put_members(tc, h, 4 * s + m, tile_of(out, slice(0, WP), h, m, lane_w))

    def put_members(array, h, b, tile):
        array[h, pl.ds(b, WP, stride=8), :] = tile

    def put_gradient(s):
        arrived(AG2 + s, ab2.at[s, pl.ds(0, NC)])
        columns_of(ab2.at[s], at2.at[s])
        inv = at[s]
        lane = lax.broadcasted_iota(jnp.int32, (2 * LN, LN), 1)
        at2[s] = at2[s] * jnp.where(lane % 8 < 3, pltpu.roll(inv, LN - 3, 1), inv)
        for h in range(HL):
            for m in range(4):
                column = 8 * m + h
                first = at2[s, 0:WP, column : column + 1]
                second = at2[s, 0:WP, column + 3 : column + 4]
                put_members(
                    tx, h, 4 * s + m, gc[s, 4 * h + m] - first - cen[s, 4 * h + m] * second
                )

    share_gradient_sums(1)
    put_gradient(0)
    arrived(GWR, gr)
    gas[...] = jnp.sum(gr[...].astype(F32), axis=0).astype(BF16)
    spread("space", GWG, lambda t: gas, ga)
    put_gradient(1)
    for h in range(HL):
        pack(tx, gin_out, h)
    arrived(A3, recv3)
    put_mixed(0)
    put_mixed(1)
    for h in range(HL):
        pack(tc, mixed_out, h)

    arrived(GWG, ga)
    for layer_at, (gw_ref, gbias_ref) in enumerate(((gw1_ref, gb1_ref), (gw2_ref, gb2_ref))):
        for part in range(2):
            at_piece = 16 * layer_at + 8 * part
            block = ga[at_piece : at_piece + 8].astype(F32).reshape(LN, LN)
            gw_ref[part, 0] = block[0:CB, 0:CB]
            gbias_ref[part] = block[CB : CB + 1, 0:CB]
            if layer_at == 0 and part == 0:
                gg_ref[...] = block[CB + 1 : CB + 2, 0:CB]
                gs_ref[...] = block[CB + 2 : CB + 3, 0:CB]

    for s in range(2):
        sent(RS1 + s, rb.at[s], NC)
        sent(AG1 + s, ab.at[s], NC)
        sent(RS2 + s, rb2.at[s], NC)
        sent(AG2 + s, ab2.at[s], NC)
        sent(A2 + s, recv2.at[s], NS)
        sent(A1 + s, recv1.at[s], NS)
        sent(A4 + s, recv4.at[s], NS)
    half = recv3.at[:, pl.ds(0, NS - 1)]
    pltpu.make_async_copy(half, half, send_sems.at[A3]).wait()
    sent(GWR, gr, NS)
    sent(GWG, ga, NS)


def write_out(*refs):
    count = (len(refs) - 1) // 2
    sems = refs[-1]
    copies = [
        pltpu.make_async_copy(refs[i], refs[count + i], sems.at[i]) for i in range(count)
    ]
    for copy in copies:
        copy.start()
    for copy in copies:
        copy.wait()


def on_device(members, gain, shift, w_first, b_first, w_second, b_second, cotangent):
    lon_out, lon_back, lat_out, lat_back, picks = (jnp.asarray(t) for t in tables())
    anywhere = pl.BlockSpec(memory_space=pl.ANY)
    vmem = pl.BlockSpec(memory_space=pltpu.VMEM)
    stays = pl.BlockSpec(memory_space=pltpu.HBM)
    token = (HL, 1, 8, W * CB)
    piece = (2, NS, 4, PL)
    spectral = (2, 2, 4 * H, 2 * LN)
    folded = (2, 2, 2 * H, HB)
    results = (
        jax.ShapeDtypeStruct(token, BF16),
        jax.ShapeDtypeStruct(token, BF16),
        jax.ShapeDtypeStruct((2, 1, CB, CB), F32),
        jax.ShapeDtypeStruct((2, 1, CB), F32),
        jax.ShapeDtypeStruct((2, 1, CB, CB), F32),
        jax.ShapeDtypeStruct((2, 1, CB), F32),
        jax.ShapeDtypeStruct((1, CB), F32),
        jax.ShapeDtypeStruct((1, CB), F32),
    )
    outs = pl.pallas_call(
        layer,
        out_shape=tuple(pltpu.VMEM(r.shape, r.dtype) for r in results),
        in_specs=[stays] * 13,
        out_specs=tuple([vmem] * 8),
        scratch_shapes=[
            pltpu.VMEM(token, BF16),
            pltpu.VMEM(token, BF16),
            pltpu.VMEM((2, 4 * NS, WP), BF16),
            pltpu.VMEM((2, WP, 4 * NS), BF16),
            pltpu.VMEM((4 * H, 4 * H), BF16),
            pltpu.VMEM((4 * H, 4 * H), BF16),
            pltpu.VMEM((HL, 8 * WP, LN), F32),
            pltpu.VMEM((HL, 8 * WP, LN), F32),
            pltpu.VMEM((2, WP, PL), BF16),
            pltpu.VMEM((2, 4 * HL, WP, LN), F32),
            pltpu.VMEM((2, 4 * HL, WP, LN), F32),
        ]
        + [pltpu.VMEM(piece, BF16)] * 8
        + [pltpu.VMEM((4 * H, HB), BF16)]
        + [pltpu.VMEM(spectral, BF16)] * 5
        + [pltpu.VMEM(folded, BF16)] * 2
        + [
            pltpu.VMEM((2, 2 * LN, 2 * LN), BF16),
            pltpu.VMEM((8, 2 * LN), F32),
        ]
        + [
            pltpu.VMEM((2, 2 * LN, LN), F32),
            pltpu.VMEM((2, NC, 8, LN), F32),
            pltpu.VMEM((2, NC, 8, LN), F32),
            pltpu.VMEM((2, 8, LN), F32),
            pltpu.VMEM((2, 2 * NC, 8, LN), F32),
            pltpu.VMEM((2, 2 * LN, LN), F32),
        ]
        * 2
        + [
            pltpu.VMEM((NS, 16, LN), BF16),
            pltpu.VMEM((NS, 16, LN), BF16),
            pltpu.VMEM((16, LN), BF16),
            pltpu.VMEM((NS, 16, LN), BF16),
            pltpu.VMEM((2, 4 * HL, WP, LN), F32),
            pltpu.VMEM((WP, 8 * HL * LN), BF16),
            pltpu.VMEM((8 * HL * LN, LN), BF16),
            pltpu.VMEM((2, 1, CB), F32),
            pltpu.VMEM((2, 1, CB, CB), BF16),
            pltpu.VMEM((2, 1, CB, CB), BF16),
            pltpu.VMEM((2, 1, CB), F32),
            pltpu.VMEM((2, 1, CB), F32),
            pltpu.SemaphoreType.DMA((17,)),
            pltpu.SemaphoreType.DMA((18,)),
            pltpu.SemaphoreType.DMA((18,)),
        ],
        compiler_params=pltpu.CompilerParams(
            collective_id=0, has_side_effects=True, vmem_limit_bytes=60 * 1024 * 1024
        ),
    )(
        jnp.transpose(members, (1, 2, 0, 3)),
        jnp.transpose(cotangent, (1, 2, 0, 3)),
        gain.reshape(1, CB),
        shift.reshape(1, CB),
        w_first,
        b_first,
        w_second,
        b_second,
        lon_out,
        lon_back,
        lat_out,
        lat_back,
        picks,
    )
    outs = [pltpu.with_memory_space_constraint(o, pltpu.VMEM) for o in outs]
    mixed, grad_input, gw1, gb1, gw2, gb2, gg, gs = pl.pallas_call(
        write_out,
        out_shape=results,
        in_specs=[vmem] * 8,
        out_specs=tuple([anywhere] * 8),
        scratch_shapes=[pltpu.SemaphoreType.DMA((8,))],
    )(*outs)
    return (
        jnp.transpose(mixed, (2, 0, 1, 3)),
        jnp.transpose(grad_input, (2, 0, 1, 3)),
        gw1,
        gb1,
        gw2,
        gb2,
        gg.reshape(CB),
        gs.reshape(CB),
    )


def solution(mesh):
    placed = (
        P(None, "space", "chan", None),
        P("chan"),
        P("chan"),
        P(None, "chan", None, None),
        P(None, "chan", None),
        P(None, "chan", None, None),
        P(None, "chan", None),
        P(None, "space", "chan", None),
    )
    return jax.shard_map(
        on_device,
        mesh=mesh,
        in_specs=placed,
        out_specs=(
            P(None, "space", "chan", None),
            P(None, "space", "chan", None),
            P(None, "chan", None, None),
            P(None, "chan", None),
            P(None, "chan", None, None),
            P(None, "chan", None),
            P("chan"),
            P("chan"),
        ),
        check_vma=False,
    )
```

```python
import math

import jax
import jax.numpy as jnp
import ml_dtypes
import numpy as np
from jax import lax
from jax.experimental import pallas as pl
from jax.experimental.pallas import tpu as pltpu
from jax.sharding import PartitionSpec as P

C = 768
CB = 96
W = 180
WP = 192
MW = 64
H = 96
NS = 32
NC = 8
HL = H // NS
LN = 128
PL = 9 * LN
HB = 4 * CB

shrink_level = 0.05
norm_epsilon = 1e-05
gelu_scale = 0.7978845608
gelu_cubic = 0.044715
lon_factor = 1.0 / math.sqrt(W)
lat_factor = 1.0 / math.sqrt(H)

F32 = jnp.float32
BF16 = jnp.bfloat16
MESH = pl.DeviceIdType.MESH

RS1, AG1, A2, A1, A4, A3, RS2, AG2 = range(0, 16, 2)
GWR, GWG = range(16, 18)


def twiddle(length, columns):
    rows = np.arange(length)[:, None]
    cols = np.arange(columns)[None, :]
    angles = (rows * cols % length).astype(np.float32) * np.float32(2.0 * math.pi / length)
    return (
        np.cos(angles).astype(np.float32),
        np.sin(angles).astype(np.float32),
    )


def tables():
    bf = ml_dtypes.bfloat16
    cos_lon, sin_lon = (t.astype(bf).astype(np.float32) for t in twiddle(W, MW))
    cos_lat, sin_lat = (t.astype(bf).astype(np.float32) for t in twiddle(H, H))
    lon = np.zeros((NS, 2, 2, WP), np.float32)
    scaled = np.zeros_like(lon)
    for d in range(NS):
        for mm in range(2):
            m = 2 * d + mm
            lon[d, 0, mm, :W] = cos_lon[:, m]
            lon[d, 1, mm, :W] = -sin_lon[:, m]
            scaled[d, :, mm] = (1.0 if m == 0 else 2.0) * lon[d, :, mm]
    lon = lon.reshape(4 * NS, WP)
    scaled = scaled.reshape(4 * NS, WP)
    lat = np.zeros((2, 2, H, HL, NS, 2, 2), np.float32)
    for hh in range(HL):
        cos_part = cos_lat[:, hh::HL]
        sin_part = sin_lat[:, hh::HL]
        for mm in range(2):
            lat[mm, 0, :, hh, :, 0, mm] = cos_part
            lat[mm, 0, :, hh, :, 1, mm] = sin_part
            lat[mm, 1, :, hh, :, 0, mm] = -sin_part
            lat[mm, 1, :, hh, :, 1, mm] = cos_part
    lat = lat.reshape(4 * H, 4 * H)
    picked = np.zeros((HL, 4, 2, LN, LN), np.float32)
    for h in range(HL):
        for m in range(4):
            for q in range(2):
                picked[h, m, q, :CB, 8 * m + 3 * q + h] = 1.0
    return (
        np.stack([lon, scaled]).astype(bf),
        np.stack([lon.T, scaled.T]).astype(bf),
        lat.astype(bf),
        lat.T.astype(bf),
        picked.reshape(8 * HL * LN, LN).astype(bf),
    )


def dot(left, right):
    return lax.dot_general(left, right, (((1,), (0,)), ((), ())), preferred_element_type=F32)


def dot_nt(left, right):
    return lax.dot_general(left, right, (((1,), (1,)), ((), ())), preferred_element_type=F32)


def dot_tn(left, right):
    return lax.dot_general(left, right, (((0,), (0,)), ((), ())), preferred_element_type=F32)


def unpack(source, target, h):
    lane = lax.broadcasted_iota(jnp.int32, (8, LN), 1)

    def step(it, carry):
        for u in range(15):
            i = it * 15 + u
            chunk = source[h, 0, :, pl.ds(pl.multiple_of(i * 384, 128), 384)].astype(F32)
            v0, v1, v2 = chunk[:, :128], chunk[:, 128:256], chunk[:, 256:]
            parts = (
                v0,
                pltpu.roll(jnp.where(lane >= 96, v0, v1), 32, 1),
                pltpu.roll(jnp.where(lane >= 64, v1, v2), 64, 1),
                pltpu.roll(v2, 96, 1),
            )
            for q in range(4):
                target[h, pl.ds(pl.multiple_of(i * 32 + 8 * q, 8), 8), :] = parts[q]
        return carry

    lax.fori_loop(0, 3, step, 0)


def pack(source, target, h):
    lane = lax.broadcasted_iota(jnp.int32, (8, LN), 1)

    def step(it, carry):
        for u in range(15):
            i = it * 15 + u
            p0, p1, p2, p3 = (
                source[h, pl.ds(pl.multiple_of(i * 32 + 8 * q, 8), 8), :] for q in range(4)
            )
            r1 = pltpu.roll(p1, 96, 1)
            r2 = pltpu.roll(p2, 64, 1)
            r3 = pltpu.roll(p3, 32, 1)
            chunk = jnp.concatenate(
                [
                    jnp.where(lane < 96, p0, r1),
                    jnp.where(lane < 64, r1, r2),
                    jnp.where(lane < 32, r2, r3),
                ],
                axis=1,
            )
            target[h, 0, :, pl.ds(pl.multiple_of(i * 384, 128), 384)] = chunk.astype(BF16)
        return carry

    lax.fori_loop(0, 3, step, 0)


def layer(
    x_hbm, cot_hbm, gain_hbm, shift_hbm, w1_hbm, b1_hbm, w2_hbm, b2_hbm,
    d_hbm, e_hbm, l_hbm, m_hbm, pick_hbm,
    mixed_out, gin_out, gw1_ref, gb1_ref, gw2_ref, gb2_ref, gg_ref, gs_ref,
    xv, cv, dv, ev, lv, mv, tx, tc, xn, cen, gc,
    send1, send2, send3, send4, recv1, recv2, recv3, recv4,
    rc, lt, gsh, hid, gpost, gpre, sh, glat, wc, vec,
    acc, st, rb, ags, ab, at, acc2, st2, rb2, ags2, ab2, at2,
    gb, gr, gas, ga, invb, terms, pick, small, w1_v, w2_v, b1_v, b2_v,
    in_sems, send_sems, recv_sems,
):
    me_s = lax.axis_index("space")
    me_c = lax.axis_index("chan")

    loads = [pltpu.make_async_copy(x_hbm.at[h], xv.at[h], in_sems.at[h]) for h in range(HL)]
    loads += [pltpu.make_async_copy(cot_hbm.at[h], cv.at[h], in_sems.at[3 + h]) for h in range(HL)]
    loads += [
        pltpu.make_async_copy(d_hbm, dv, in_sems.at[6]),
        pltpu.make_async_copy(e_hbm, ev, in_sems.at[7]),
        pltpu.make_async_copy(l_hbm, lv, in_sems.at[8]),
        pltpu.make_async_copy(m_hbm, mv, in_sems.at[9]),
        pltpu.make_async_copy(gain_hbm, small.at[0], in_sems.at[10]),
        pltpu.make_async_copy(shift_hbm, small.at[1], in_sems.at[11]),
        pltpu.make_async_copy(w1_hbm, w1_v, in_sems.at[12]),
        pltpu.make_async_copy(b1_hbm, b1_v, in_sems.at[13]),
        pltpu.make_async_copy(w2_hbm, w2_v, in_sems.at[14]),
        pltpu.make_async_copy(b2_hbm, b2_v, in_sems.at[15]),
        pltpu.make_async_copy(pick_hbm, pick, in_sems.at[16]),
    ]
    for load in loads:
        load.start()

    barrier = pltpu.get_barrier_semaphore()

    def greet_space(r, carry):
        pl.semaphore_signal(
            barrier, inc=1, device_id={"space": lax.rem(me_s + r, NS)}, device_id_type=MESH
        )
        return carry

    def greet_chan(r, carry):
        pl.semaphore_signal(
            barrier, inc=1, device_id={"chan": lax.rem(me_c + r, NC)}, device_id_type=MESH
        )
        return carry

    lax.fori_loop(1, NC, greet_chan, 0)
    lax.fori_loop(1, NS, greet_space, 0)

    def spread(axis, index, piece, target, slot=None):
        slot = slot or (lambda t: target.at[t])
        count, me = (NS, me_s) if axis == "space" else (NC, me_c)

        def step(r, carry):
            t = lax.rem(me + r, count)
            pltpu.make_async_remote_copy(
                src_ref=piece(t),
                dst_ref=slot(me),
                send_sem=send_sems.at[index],
                recv_sem=recv_sems.at[index],
                device_id={axis: t},
                device_id_type=MESH,
            ).start()
            return carry

        lax.fori_loop(1, count, step, 0)
        pltpu.make_async_copy(piece(me), slot(me), recv_sems.at[index]).start()

    def arrived(index, target):
        pltpu.make_async_copy(target, target, recv_sems.at[index]).wait()

    def sent(index, target, count):
        rest = target.at[pl.ds(0, count - 1)]
        pltpu.make_async_copy(rest, rest, send_sems.at[index]).wait()

    tx[:, 8 * W :, :] = jnp.zeros((HL, 8 * (WP - W), LN), F32)
    tc[:, 8 * W :, :] = jnp.zeros((HL, 8 * (WP - W), LN), F32)
    acc[...] = jnp.zeros_like(acc)
    acc2[...] = jnp.zeros_like(acc2)
    ab[:, NC:] = jnp.zeros((2, NC, 8, LN), F32)
    ab2[:, NC:] = jnp.zeros((2, NC, 8, LN), F32)
    lane_t = lax.broadcasted_iota(jnp.int32, (4 * H, 2 * LN), 1)
    lane_h = lax.broadcasted_iota(jnp.int32, (H, LN), 1)
    lane_w = lax.broadcasted_iota(jnp.int32, (WP, LN), 1)

    def members_of(array, h, b):
        return array[h, pl.ds(b, WP, stride=8), :]

    def dense(tiles, lane):
        r1, r2, r3 = (pltpu.roll(tiles[i], LN - 32 * i, 1) for i in range(1, 4))
        return (
            jnp.where(lane < 96, tiles[0], r1),
            jnp.where(lane < 64, r1, r2),
            jnp.where(lane < 32, r2, r3),
        )

    def tile_of(array, rows, h, m, lane):
        start = HB * h + CB * m
        first, shift = start // LN * LN, start % LN
        left = array[rows, first : first + LN]
        if shift == 0:
            return left
        if shift > 32:
            right = array[rows, first + LN : first + 2 * LN]
            left = jnp.where(lane >= shift, left, right)
        return pltpu.roll(left, LN - shift, 1)

    def store_dense(s, h, tiles):
        for i, column in enumerate(dense(tiles, lane_w)):
            xn[s, :, HB * h + LN * i : HB * h + LN * i + LN] = column.astype(BF16)

    def pieces_of_sums(source, target):
        turned = jnp.transpose(source[...])
        for part in range(2):
            for m in range(4):
                target[4 * part + m] = turned[8 * m : 8 * m + 8, LN * part : LN * part + LN]

    def columns_of(source, target):
        turned = jnp.transpose(source[...].reshape(LN, LN))
        target[0:LN, 0:32] = turned[:, 0:32]
        target[LN:, 0:32] = turned[:, 32:64]

    for h in range(HL):
        loads[h].wait()
        unpack(xv, tx, h)

    def token_sums(s):
        total = jnp.zeros((WP, LN), F32)
        for m in range(4):
            for h in range(HL):
                tile = jnp.where(lane_w < CB, members_of(tx, h, 4 * s + m), 0.0)
                one = jnp.sum(tile, axis=1, keepdims=True)
                two = jnp.sum(tile * tile, axis=1, keepdims=True)
                total = jnp.where(lane_w == 8 * m + h, one, total)
                total = jnp.where(lane_w == 8 * m + 3 + h, two, total)
        acc[s, 0:WP, :] = total
        pieces_of_sums(acc.at[s], st.at[s])

    token_sums(0)
    pl.semaphore_wait(barrier, NS - 1 + NC - 1)
    spread("chan", RS1, lambda t: st.at[0, t], rb.at[0])
    token_sums(1)
    spread("chan", RS1 + 1, lambda t: st.at[1, t], rb.at[1])

    for k in range(10, 16):
        loads[k].wait()
    vec[...] = jnp.zeros_like(vec)
    vec[0:1, 0:CB] = small[0]
    vec[1:2, 0:CB] = small[1]
    for layer_at, (b_ref, w_ref) in enumerate(((b1_v, w1_v), (b2_v, w2_v))):
        vec[2 + layer_at : 3 + layer_at, 0:CB] = b_ref[0]
        vec[2 + layer_at : 3 + layer_at, LN : LN + CB] = b_ref[1]
        wc[layer_at] = jnp.zeros((2 * LN, 2 * LN), BF16)
        w_real, w_imag = w_ref[0, 0], w_ref[1, 0]
        wc[layer_at, 0:CB, 0:CB] = w_real
        wc[layer_at, 0:CB, LN : LN + CB] = w_imag
        wc[layer_at, LN : LN + CB, 0:CB] = -w_imag
        wc[layer_at, LN : LN + CB, LN : LN + CB] = w_real
    gain_row = vec[0:1, 0:LN]
    shift_row = vec[1:2, 0:LN]

    for h in range(HL):
        loads[3 + h].wait()
        unpack(cv, tc, h)
    loads[6].wait()

    def cotangent_spectra(s):
        for h in range(HL):
            store_dense(s, h, [members_of(tc, h, 4 * s + m) for m in range(4)])
        out = dot(dv[1], xn[s]) * lon_factor
        send2[s] = out.reshape(NS, 4, PL).astype(BF16)

    def share_statistics(s):
        arrived(RS1 + s, rb.at[s])
        sums = jnp.sum(rb[s], axis=0) * (1.0 / C)
        var_in = pltpu.roll(sums, 5, 0)
        inv = lax.rsqrt(var_in - sums * sums + norm_epsilon)
        row8 = lax.broadcasted_iota(jnp.int32, (8, LN), 0)
        ags[s] = jnp.where(row8 < 3, sums, jnp.where(row8 < 6, pltpu.roll(inv, 3, 0), 0.0))
        spread("chan", AG1 + s, lambda t: ags.at[s], ab.at[s])

    cotangent_spectra(0)
    spread("space", A2, lambda t: send2.at[0, t], recv2.at[0])
    share_statistics(0)
    cotangent_spectra(1)
    spread("space", A2 + 1, lambda t: send2.at[1, t], recv2.at[1])
    share_statistics(1)

    def send_normed(s):
        arrived(AG1 + s, ab.at[s, pl.ds(0, NC)])
        columns_of(ab.at[s], at.at[s])
        for h in range(HL):
            tiles = []
            for m in range(4):
                column = 8 * m + h
                mean_col = at[s, 0:WP, column : column + 1]
                inv_col = at[s, 0:WP, column + 3 : column + 4]
                inv_tile = jnp.broadcast_to(inv_col, (WP, LN))
                invb[s, 4 * h + m] = inv_tile
                centred = (members_of(tx, h, 4 * s + m) - mean_col) * inv_tile
                cen[s, 4 * h + m] = centred
                tiles.append(centred * gain_row + shift_row)
            store_dense(s, h, tiles)
        out = dot(dv[0], xn[s]) * lon_factor
        send1[s] = out.reshape(NS, 4, PL).astype(BF16)
        spread("space", A1 + s, lambda t: send1.at[s, t], recv1.at[s])

    send_normed(0)
    send_normed(1)

    def latitude(received, target, ones):
        for h in range(HL):
            rc[LN * h : LN * h + LN, :] = received[:, :, HB * h : HB * h + HB].reshape(LN, HB)
        out = dot(lv[...], rc[...]) * lat_factor
        for mm in range(2):
            for part in range(2):
                rows = slice(2 * H * mm + H * part, 2 * H * mm + H * part + H)
                for m in range(4):
                    tile = tile_of(out, rows, 0, m, lane_h)
                    if ones:
                        tile = jnp.where(lane_h == CB, 1.0 - part, tile)
                    target[mm, H * m : H * m + H, LN * part : LN * part + LN] = tile.astype(BF16)

    loads[8].wait()

    def mix(s):
        def step(i, carry):
            pre = dot(lt[s, i], wc[0]) + vec[2:3, :]
            t = jnp.tanh(gelu_scale * (pre + gelu_cubic * pre * pre * pre))
            hidden = 0.5 * pre * (1.0 + t)
            hidden = jnp.where(lane_t == CB, 1.0, hidden).astype(BF16)
            slope = 0.5 * (1.0 + t) + 0.5 * pre * (1.0 - t * t) * gelu_scale * (
                1.0 + 3.0 * gelu_cubic * pre * pre
            )
            hid[s, i] = hidden
            post = dot(hidden, wc[1]) + vec[3:4, :]
            shape = jnp.tanh(post * (1.0 / shrink_level))
            shrunk = post - shrink_level * shape
            grad_post = (gsh[s, i].astype(F32) * (shape * shape)).astype(BF16)
            gpost[s, i] = grad_post
            grad_pre = (dot_nt(grad_post, wc[1]) * slope).astype(BF16)
            gpre[s, i] = grad_pre
            grad_lat = dot_nt(grad_pre, wc[0])
            for source, target in ((shrunk, sh), (grad_lat, glat)):
                for part in range(2):
                    tiles = [
                        source[H * m : H * m + H, LN * part : LN * part + LN] for m in range(4)
                    ]
                    for j, column in enumerate(dense(tiles, lane_h)):
                        target[s, i, H * part : H * part + H, LN * j : LN * j + LN] = (
                            column.astype(BF16)
                        )
            return carry

        lax.fori_loop(0, 2, step, 0)

    def back(source, target):
        out = dot(mv[...], source[...].reshape(4 * H, HB)) * lat_factor
        for h in range(HL):
            piece = out[LN * h : LN * h + LN, :].reshape(NS, 4, HB)
            target[:, :, HB * h : HB * h + HB] = piece.astype(BF16)

    for s in range(2):
        arrived(A2 + s, recv2.at[s])
        latitude(recv2.at[s], gsh.at[s], False)
    loads[9].wait()
    for s in range(2):
        arrived(A1 + s, recv1.at[s])
        latitude(recv1.at[s], lt.at[s], True)
        mix(s)
        back(glat.at[s], send4.at[s])
        spread("space", A4 + s, lambda t, s=s: send4.at[s, t], recv4.at[s])
        if s == 1:
            spread("space", A3, lambda t: send3.at[0, t], recv3.at[0])
        back(sh.at[s], send3.at[s])

    for layer_at, (left, right) in enumerate(((lt, gpre), (hid, gpost))):
        outer = dot_tn(left[...].reshape(16 * H, 2 * LN), right[...].reshape(16 * H, 2 * LN))
        real = outer[0:LN, 0:LN] + outer[LN:, LN:]
        imag = outer[0:LN, LN:] - outer[LN:, 0:LN]
        gb[16 * layer_at : 16 * layer_at + 8] = real.reshape(8, 16, LN).astype(BF16)
        gb[16 * layer_at + 8 : 16 * layer_at + 16] = imag.reshape(8, 16, LN).astype(BF16)

    spread("space", GWR, lambda t: gb.at[t], gr)
    spread("space", A3 + 1, lambda t: send3.at[1, t], recv3.at[1])

    loads[7].wait()
    loads[16].wait()
    norm_sums = [jnp.zeros((8, LN), F32), jnp.zeros((8, LN), F32)]

    def gradient_sums(s):
        arrived(A4 + s, recv4.at[s])
        out = dot(ev[0], recv4[s].reshape(4 * NS, PL)) * lon_factor
        for h in range(HL):
            for m in range(4):
                grad_normed = tile_of(out, slice(0, WP), h, m, lane_w)
                centred = cen[s, 4 * h + m]
                product = grad_normed * centred
                norm_sums[0] = norm_sums[0] + jnp.sum(product.reshape(WP // 8, 8, LN), axis=0)
                norm_sums[1] = norm_sums[1] + jnp.sum(grad_normed.reshape(WP // 8, 8, LN), axis=0)
                grad_centred = grad_normed * gain_row
                i = 4 * h + m
                gc[s, i] = grad_centred * invb[s, i]
                terms[:, 2 * LN * i : 2 * LN * i + LN] = grad_centred.astype(BF16)
                terms[:, 2 * LN * i + LN : 2 * LN * i + 2 * LN] = (
                    grad_centred * centred
                ).astype(BF16)
        acc2[s, 0:WP, :] = dot(terms[...], pick[...])
        pieces_of_sums(acc2.at[s], st2.at[s])
        spread("chan", RS2 + s, lambda t: st2.at[s, t], rb2.at[s])

    gradient_sums(0)
    gradient_sums(1)

    def share_gradient_sums(s):
        arrived(RS2 + s, rb2.at[s])
        ags2[s] = jnp.sum(rb2[s], axis=0) * (1.0 / C)
        spread("chan", AG2 + s, lambda t: ags2.at[s], ab2.at[s])

    share_gradient_sums(0)
    def put_mixed(s):
        out = dot(ev[1], recv3[s].reshape(4 * NS, PL)) * lon_factor
        for h in range(HL):
            for m in range(4):
                put_members(tc, h, 4 * s + m, tile_of(out, slice(0, WP), h, m, lane_w))

    def put_members(array, h, b, tile):
        array[h, pl.ds(b, WP, stride=8), :] = tile

    def put_gradient(s):
        arrived(AG2 + s, ab2.at[s, pl.ds(0, NC)])
        columns_of(ab2.at[s], at2.at[s])
        inv = at[s]
        lane = lax.broadcasted_iota(jnp.int32, (2 * LN, LN), 1)
        at2[s] = at2[s] * jnp.where(lane % 8 < 3, pltpu.roll(inv, LN - 3, 1), inv)
        for h in range(HL):
            for m in range(4):
                column = 8 * m + h
                first = at2[s, 0:WP, column : column + 1]
                second = at2[s, 0:WP, column + 3 : column + 4]
                put_members(
                    tx, h, 4 * s + m, gc[s, 4 * h + m] - first - cen[s, 4 * h + m] * second
                )

    arrived(A3, recv3.at[0])
    put_mixed(0)
    share_gradient_sums(1)
    put_gradient(0)
    arrived(GWR, gr)
    gas[0:16] = jnp.sum(gr[...].astype(F32), axis=0).astype(BF16)
    row8 = lax.broadcasted_iota(jnp.int32, (8, LN), 0)
    gas[16:24] = jnp.where(
        row8 == 0,
        jnp.sum(norm_sums[0], axis=0, keepdims=True),
        jnp.where(row8 == 1, jnp.sum(norm_sums[1], axis=0, keepdims=True), 0.0),
    ).astype(BF16)
    spread("space", GWG, lambda t: gas, ga)
    put_gradient(1)
    for h in range(HL):
        pack(tx, gin_out, h)
    arrived(A3 + 1, recv3.at[1])
    put_mixed(1)
    for h in range(HL):
        pack(tc, mixed_out, h)

    arrived(GWG, ga)
    both = jnp.sum(ga[:, 16:24].astype(F32), axis=0)
    gg_ref[...] = both[0:1, 0:CB]
    gs_ref[...] = both[1:2, 0:CB]
    for layer_at, (gw_ref, gbias_ref) in enumerate(((gw1_ref, gb1_ref), (gw2_ref, gb2_ref))):
        for part in range(2):
            at_piece = 16 * layer_at + 8 * part
            block = ga[at_piece : at_piece + 8, 0:16].astype(F32).reshape(LN, LN)
            gw_ref[part, 0] = block[0:CB, 0:CB]
            gbias_ref[part] = block[CB : CB + 1, 0:CB]

    for s in range(2):
        sent(RS1 + s, rb.at[s], NC)
        sent(AG1 + s, ab.at[s], NC)
        sent(RS2 + s, rb2.at[s], NC)
        sent(AG2 + s, ab2.at[s], NC)
        sent(A2 + s, recv2.at[s], NS)
        sent(A1 + s, recv1.at[s], NS)
        sent(A4 + s, recv4.at[s], NS)
    sent(A3, recv3.at[0], NS)
    sent(A3 + 1, recv3.at[1], NS)
    sent(GWR, gr, NS)
    sent(GWG, ga, NS)


def write_out(*refs):
    count = (len(refs) - 1) // 2
    sems = refs[-1]
    copies = [
        pltpu.make_async_copy(refs[i], refs[count + i], sems.at[i]) for i in range(count)
    ]
    for copy in copies:
        copy.start()
    for copy in copies:
        copy.wait()


def on_device(members, gain, shift, w_first, b_first, w_second, b_second, cotangent):
    lon_out, lon_back, lat_out, lat_back, picks = (jnp.asarray(t) for t in tables())
    anywhere = pl.BlockSpec(memory_space=pl.ANY)
    vmem = pl.BlockSpec(memory_space=pltpu.VMEM)
    stays = pl.BlockSpec(memory_space=pltpu.HBM)
    token = (HL, 1, 8, W * CB)
    piece = (2, NS, 4, PL)
    spectral = (2, 2, 4 * H, 2 * LN)
    folded = (2, 2, 2 * H, HB)
    results = (
        jax.ShapeDtypeStruct(token, BF16),
        jax.ShapeDtypeStruct(token, BF16),
        jax.ShapeDtypeStruct((2, 1, CB, CB), F32),
        jax.ShapeDtypeStruct((2, 1, CB), F32),
        jax.ShapeDtypeStruct((2, 1, CB, CB), F32),
        jax.ShapeDtypeStruct((2, 1, CB), F32),
        jax.ShapeDtypeStruct((1, CB), F32),
        jax.ShapeDtypeStruct((1, CB), F32),
    )
    outs = pl.pallas_call(
        layer,
        out_shape=tuple(pltpu.VMEM(r.shape, r.dtype) for r in results),
        in_specs=[stays] * 13,
        out_specs=tuple([vmem] * 8),
        scratch_shapes=[
            pltpu.VMEM(token, BF16),
            pltpu.VMEM(token, BF16),
            pltpu.VMEM((2, 4 * NS, WP), BF16),
            pltpu.VMEM((2, WP, 4 * NS), BF16),
            pltpu.VMEM((4 * H, 4 * H), BF16),
            pltpu.VMEM((4 * H, 4 * H), BF16),
            pltpu.VMEM((HL, 8 * WP, LN), F32),
            pltpu.VMEM((HL, 8 * WP, LN), F32),
            pltpu.VMEM((2, WP, PL), BF16),
            pltpu.VMEM((2, 4 * HL, WP, LN), F32),
            pltpu.VMEM((2, 4 * HL, WP, LN), F32),
        ]
        + [pltpu.VMEM(piece, BF16)] * 8
        + [pltpu.VMEM((4 * H, HB), BF16)]
        + [pltpu.VMEM(spectral, BF16)] * 5
        + [pltpu.VMEM(folded, BF16)] * 2
        + [
            pltpu.VMEM((2, 2 * LN, 2 * LN), BF16),
            pltpu.VMEM((8, 2 * LN), F32),
        ]
        + [
            pltpu.VMEM((2, 2 * LN, LN), F32),
            pltpu.VMEM((2, NC, 8, LN), F32),
            pltpu.VMEM((2, NC, 8, LN), F32),
            pltpu.VMEM((2, 8, LN), F32),
            pltpu.VMEM((2, 2 * NC, 8, LN), F32),
            pltpu.VMEM((2, 2 * LN, LN), F32),
        ]
        * 2
        + [
            pltpu.VMEM((NS, 16, LN), BF16),
            pltpu.VMEM((NS, 16, LN), BF16),
            pltpu.VMEM((24, LN), BF16),
            pltpu.VMEM((NS, 24, LN), BF16),
            pltpu.VMEM((2, 4 * HL, WP, LN), F32),
            pltpu.VMEM((WP, 8 * HL * LN), BF16),
            pltpu.VMEM((8 * HL * LN, LN), BF16),
            pltpu.VMEM((2, 1, CB), F32),
            pltpu.VMEM((2, 1, CB, CB), BF16),
            pltpu.VMEM((2, 1, CB, CB), BF16),
            pltpu.VMEM((2, 1, CB), F32),
            pltpu.VMEM((2, 1, CB), F32),
            pltpu.SemaphoreType.DMA((17,)),
            pltpu.SemaphoreType.DMA((18,)),
            pltpu.SemaphoreType.DMA((18,)),
        ],
        compiler_params=pltpu.CompilerParams(
            collective_id=0, has_side_effects=True, vmem_limit_bytes=60 * 1024 * 1024
        ),
    )(
        jnp.transpose(members, (1, 2, 0, 3)),
        jnp.transpose(cotangent, (1, 2, 0, 3)),
        gain.reshape(1, CB),
        shift.reshape(1, CB),
        w_first,
        b_first,
        w_second,
        b_second,
        lon_out,
        lon_back,
        lat_out,
        lat_back,
        picks,
    )
    outs = [pltpu.with_memory_space_constraint(o, pltpu.VMEM) for o in outs]
    mixed, grad_input, gw1, gb1, gw2, gb2, gg, gs = pl.pallas_call(
        write_out,
        out_shape=results,
        in_specs=[vmem] * 8,
        out_specs=tuple([anywhere] * 8),
        scratch_shapes=[pltpu.SemaphoreType.DMA((8,))],
    )(*outs)
    return (
        jnp.transpose(mixed, (2, 0, 1, 3)),
        jnp.transpose(grad_input, (2, 0, 1, 3)),
        gw1,
        gb1,
        gw2,
        gb2,
        gg.reshape(CB),
        gs.reshape(CB),
    )


def solution(mesh):
    placed = (
        P(None, "space", "chan", None),
        P("chan"),
        P("chan"),
        P(None, "chan", None, None),
        P(None, "chan", None),
        P(None, "chan", None, None),
        P(None, "chan", None),
        P(None, "space", "chan", None),
    )
    return jax.shard_map(
        on_device,
        mesh=mesh,
        in_specs=placed,
        out_specs=(
            P(None, "space", "chan", None),
            P(None, "space", "chan", None),
            P(None, "chan", None, None),
            P(None, "chan", None),
            P(None, "chan", None, None),
            P(None, "chan", None),
            P("chan"),
            P("chan"),
        ),
        check_vma=False,
    )
```

```python
import math

import jax
import jax.numpy as jnp
import ml_dtypes
import numpy as np
from jax import lax
from jax.experimental import pallas as pl
from jax.experimental.pallas import tpu as pltpu
from jax.sharding import PartitionSpec as P

C = 768
CB = 96
W = 180
WP = 192
MW = 64
H = 96
NS = 32
NC = 8
HL = H // NS
LN = 128
PL = 9 * LN
HB = 4 * CB

shrink_level = 0.05
norm_epsilon = 1e-05
gelu_scale = 0.7978845608
gelu_cubic = 0.044715
lon_factor = 1.0 / math.sqrt(W)
lat_factor = 1.0 / math.sqrt(H)

F32 = jnp.float32
BF16 = jnp.bfloat16
MESH = pl.DeviceIdType.MESH

RS1, AG1, A2, A1, A4, A3, RS2, AG2 = range(0, 16, 2)
GWR, GWG = range(16, 18)


def twiddle(length, columns):
    rows = np.arange(length)[:, None]
    cols = np.arange(columns)[None, :]
    angles = (rows * cols % length).astype(np.float32) * np.float32(2.0 * math.pi / length)
    return (
        np.cos(angles).astype(np.float32),
        np.sin(angles).astype(np.float32),
    )


def tables():
    bf = ml_dtypes.bfloat16
    cos_lon, sin_lon = (t.astype(bf).astype(np.float32) for t in twiddle(W, MW))
    cos_lat, sin_lat = (t.astype(bf).astype(np.float32) for t in twiddle(H, H))
    lon = np.zeros((NS, 2, 2, WP), np.float32)
    scaled = np.zeros_like(lon)
    for d in range(NS):
        for mm in range(2):
            m = 2 * d + mm
            lon[d, 0, mm, :W] = cos_lon[:, m]
            lon[d, 1, mm, :W] = -sin_lon[:, m]
            scaled[d, :, mm] = (1.0 if m == 0 else 2.0) * lon[d, :, mm]
    lon = lon.reshape(4 * NS, WP)
    scaled = scaled.reshape(4 * NS, WP)
    lat = np.zeros((2, 2, H, HL, NS, 2, 2), np.float32)
    for hh in range(HL):
        cos_part = cos_lat[:, hh::HL]
        sin_part = sin_lat[:, hh::HL]
        for mm in range(2):
            lat[mm, 0, :, hh, :, 0, mm] = cos_part
            lat[mm, 0, :, hh, :, 1, mm] = sin_part
            lat[mm, 1, :, hh, :, 0, mm] = -sin_part
            lat[mm, 1, :, hh, :, 1, mm] = cos_part
    lat = lat.reshape(4 * H, 4 * H)
    picked = np.zeros((HL, 4, 2, LN, LN), np.float32)
    for h in range(HL):
        for m in range(4):
            for q in range(2):
                picked[h, m, q, :CB, 8 * m + 3 * q + h] = 1.0
    return (
        np.stack([lon, scaled]).astype(bf),
        np.stack([lon.T, scaled.T]).astype(bf),
        lat.astype(bf),
        lat.T.astype(bf),
        picked.reshape(8 * HL * LN, LN).astype(bf),
    )


def dot(left, right):
    return lax.dot_general(left, right, (((1,), (0,)), ((), ())), preferred_element_type=F32)


def dot_nt(left, right):
    return lax.dot_general(left, right, (((1,), (1,)), ((), ())), preferred_element_type=F32)


def dot_tn(left, right):
    return lax.dot_general(left, right, (((0,), (0,)), ((), ())), preferred_element_type=F32)


def unpack(source, target, h):
    lane = lax.broadcasted_iota(jnp.int32, (8, LN), 1)

    def step(it, carry):
        for u in range(15):
            i = it * 15 + u
            chunk = source[h, 0, :, pl.ds(pl.multiple_of(i * 384, 128), 384)].astype(F32)
            v0, v1, v2 = chunk[:, :128], chunk[:, 128:256], chunk[:, 256:]
            parts = (
                v0,
                pltpu.roll(jnp.where(lane >= 96, v0, v1), 32, 1),
                pltpu.roll(jnp.where(lane >= 64, v1, v2), 64, 1),
                pltpu.roll(v2, 96, 1),
            )
            for q in range(4):
                target[h, pl.ds(pl.multiple_of(i * 32 + 8 * q, 8), 8), :] = parts[q]
        return carry

    lax.fori_loop(0, 3, step, 0)


def pack(source, target, h):
    lane = lax.broadcasted_iota(jnp.int32, (8, LN), 1)

    def step(it, carry):
        for u in range(15):
            i = it * 15 + u
            p0, p1, p2, p3 = (
                source[h, pl.ds(pl.multiple_of(i * 32 + 8 * q, 8), 8), :] for q in range(4)
            )
            r1 = pltpu.roll(p1, 96, 1)
            r2 = pltpu.roll(p2, 64, 1)
            r3 = pltpu.roll(p3, 32, 1)
            chunk = jnp.concatenate(
                [
                    jnp.where(lane < 96, p0, r1),
                    jnp.where(lane < 64, r1, r2),
                    jnp.where(lane < 32, r2, r3),
                ],
                axis=1,
            )
            target[h, 0, :, pl.ds(pl.multiple_of(i * 384, 128), 384)] = chunk.astype(BF16)
        return carry

    lax.fori_loop(0, 3, step, 0)


def layer(
    x_hbm, cot_hbm, gain_hbm, shift_hbm, w1_hbm, b1_hbm, w2_hbm, b2_hbm,
    d_hbm, e_hbm, l_hbm, m_hbm, pick_hbm,
    mixed_out, gin_out, gw1_ref, gb1_ref, gw2_ref, gb2_ref, gg_ref, gs_ref,
    xv, cv, dv, ev, lv, mv, tx, tc, xn, cen, gc,
    send1, send2, send3, send4, recv1, recv2, recv3, recv4,
    rc, lt, gsh, hid, gpost, gpre, sh, glat, wc, vec,
    acc, st, rb, ags, ab, at, acc2, st2, rb2, ags2, ab2, at2,
    gb, gr, gas, ga, invb, terms, pick, small, w1_v, w2_v, b1_v, b2_v,
    in_sems, send_sems, recv_sems,
):
    me_s = lax.axis_index("space")
    me_c = lax.axis_index("chan")

    loads = [pltpu.make_async_copy(x_hbm.at[h], xv.at[h], in_sems.at[h]) for h in range(HL)]
    loads += [pltpu.make_async_copy(cot_hbm.at[h], cv.at[h], in_sems.at[3 + h]) for h in range(HL)]
    loads += [
        pltpu.make_async_copy(d_hbm, dv, in_sems.at[6]),
        pltpu.make_async_copy(e_hbm, ev, in_sems.at[7]),
        pltpu.make_async_copy(l_hbm, lv, in_sems.at[8]),
        pltpu.make_async_copy(m_hbm, mv, in_sems.at[9]),
        pltpu.make_async_copy(gain_hbm, small.at[0], in_sems.at[10]),
        pltpu.make_async_copy(shift_hbm, small.at[1], in_sems.at[11]),
        pltpu.make_async_copy(w1_hbm, w1_v, in_sems.at[12]),
        pltpu.make_async_copy(b1_hbm, b1_v, in_sems.at[13]),
        pltpu.make_async_copy(w2_hbm, w2_v, in_sems.at[14]),
        pltpu.make_async_copy(b2_hbm, b2_v, in_sems.at[15]),
        pltpu.make_async_copy(pick_hbm, pick, in_sems.at[16]),
    ]
    for load in loads:
        load.start()

    barrier = pltpu.get_barrier_semaphore()

    def greet_space(r, carry):
        pl.semaphore_signal(
            barrier, inc=1, device_id={"space": lax.rem(me_s + r, NS)}, device_id_type=MESH
        )
        return carry

    def greet_chan(r, carry):
        pl.semaphore_signal(
            barrier, inc=1, device_id={"chan": lax.rem(me_c + r, NC)}, device_id_type=MESH
        )
        return carry

    lax.fori_loop(1, NC, greet_chan, 0)
    lax.fori_loop(1, NS, greet_space, 0)

    def spread(axis, index, piece, target, slot=None):
        slot = slot or (lambda t: target.at[t])
        count, me = (NS, me_s) if axis == "space" else (NC, me_c)

        def step(r, carry):
            t = lax.rem(me + r, count)
            pltpu.make_async_remote_copy(
                src_ref=piece(t),
                dst_ref=slot(me),
                send_sem=send_sems.at[index],
                recv_sem=recv_sems.at[index],
                device_id={axis: t},
                device_id_type=MESH,
            ).start()
            return carry

        lax.fori_loop(1, count, step, 0)
        pltpu.make_async_copy(piece(me), slot(me), recv_sems.at[index]).start()

    def arrived(index, target):
        pltpu.make_async_copy(target, target, recv_sems.at[index]).wait()

    def sent(index, target, count):
        rest = target.at[pl.ds(0, count - 1)]
        pltpu.make_async_copy(rest, rest, send_sems.at[index]).wait()

    tx[:, 8 * W :, :] = jnp.zeros((HL, 8 * (WP - W), LN), F32)
    tc[:, 8 * W :, :] = jnp.zeros((HL, 8 * (WP - W), LN), F32)
    acc[...] = jnp.zeros_like(acc)
    acc2[...] = jnp.zeros_like(acc2)
    ab[:, NC:] = jnp.zeros((2, NC, 8, LN), F32)
    ab2[:, NC:] = jnp.zeros((2, NC, 8, LN), F32)
    lane_t = lax.broadcasted_iota(jnp.int32, (4 * H, 2 * LN), 1)
    lane_h = lax.broadcasted_iota(jnp.int32, (H, LN), 1)
    lane_w = lax.broadcasted_iota(jnp.int32, (WP, LN), 1)

    def members_of(array, h, b):
        return array[h, pl.ds(b, WP, stride=8), :]

    def dense(tiles, lane):
        r1, r2, r3 = (pltpu.roll(tiles[i], LN - 32 * i, 1) for i in range(1, 4))
        return (
            jnp.where(lane < 96, tiles[0], r1),
            jnp.where(lane < 64, r1, r2),
            jnp.where(lane < 32, r2, r3),
        )

    def tile_of(array, rows, h, m, lane):
        start = HB * h + CB * m
        first, shift = start // LN * LN, start % LN
        left = array[rows, first : first + LN]
        if shift == 0:
            return left
        if shift > 32:
            right = array[rows, first + LN : first + 2 * LN]
            left = jnp.where(lane >= shift, left, right)
        return pltpu.roll(left, LN - shift, 1)

    def store_dense(s, h, tiles):
        for i, column in enumerate(dense(tiles, lane_w)):
            xn[s, :, HB * h + LN * i : HB * h + LN * i + LN] = column.astype(BF16)

    def pieces_of_sums(source, target):
        turned = jnp.transpose(source[...])
        for part in range(2):
            for m in range(4):
                target[4 * part + m] = turned[8 * m : 8 * m + 8, LN * part : LN * part + LN]

    def columns_of(source, target):
        turned = jnp.transpose(source[...].reshape(LN, LN))
        target[0:LN, 0:32] = turned[:, 0:32]
        target[LN:, 0:32] = turned[:, 32:64]

    for h in range(HL):
        loads[h].wait()
        unpack(xv, tx, h)

    def token_sums(s):
        total = jnp.zeros((WP, LN), F32)
        for m in range(4):
            for h in range(HL):
                tile = jnp.where(lane_w < CB, members_of(tx, h, 4 * s + m), 0.0)
                one = jnp.sum(tile, axis=1, keepdims=True)
                two = jnp.sum(tile * tile, axis=1, keepdims=True)
                total = jnp.where(lane_w == 8 * m + h, one, total)
                total = jnp.where(lane_w == 8 * m + 3 + h, two, total)
        acc[s, 0:WP, :] = total
        pieces_of_sums(acc.at[s], st.at[s])

    token_sums(0)
    pl.semaphore_wait(barrier, NS - 1 + NC - 1)
    spread("chan", RS1, lambda t: st.at[0, t], rb.at[0])
    token_sums(1)
    spread("chan", RS1 + 1, lambda t: st.at[1, t], rb.at[1])

    for k in range(10, 16):
        loads[k].wait()
    vec[...] = jnp.zeros_like(vec)
    vec[0:1, 0:CB] = small[0]
    vec[1:2, 0:CB] = small[1]
    for layer_at, (b_ref, w_ref) in enumerate(((b1_v, w1_v), (b2_v, w2_v))):
        vec[2 + layer_at : 3 + layer_at, 0:CB] = b_ref[0]
        vec[2 + layer_at : 3 + layer_at, LN : LN + CB] = b_ref[1]
        wc[layer_at] = jnp.zeros((2 * LN, 2 * LN), BF16)
        w_real, w_imag = w_ref[0, 0], w_ref[1, 0]
        wc[layer_at, 0:CB, 0:CB] = w_real
        wc[layer_at, 0:CB, LN : LN + CB] = w_imag
        wc[layer_at, LN : LN + CB, 0:CB] = -w_imag
        wc[layer_at, LN : LN + CB, LN : LN + CB] = w_real
    gain_row = vec[0:1, 0:LN]
    shift_row = vec[1:2, 0:LN]

    for h in range(HL):
        loads[3 + h].wait()
        unpack(cv, tc, h)
    loads[6].wait()

    def cotangent_spectra(s):
        for h in range(HL):
            store_dense(s, h, [members_of(tc, h, 4 * s + m) for m in range(4)])
        out = dot(dv[1], xn[s]) * lon_factor
        send2[s] = out.reshape(NS, 4, PL).astype(BF16)

    def share_statistics(s):
        arrived(RS1 + s, rb.at[s])
        sums = jnp.sum(rb[s], axis=0) * (1.0 / C)
        var_in = pltpu.roll(sums, 5, 0)
        inv = lax.rsqrt(var_in - sums * sums + norm_epsilon)
        row8 = lax.broadcasted_iota(jnp.int32, (8, LN), 0)
        ags[s] = jnp.where(row8 < 3, sums, jnp.where(row8 < 6, pltpu.roll(inv, 3, 0), 0.0))
        spread("chan", AG1 + s, lambda t: ags.at[s], ab.at[s])

    cotangent_spectra(0)
    spread("space", A2, lambda t: send2.at[0, t], recv2.at[0])
    share_statistics(0)
    cotangent_spectra(1)
    spread("space", A2 + 1, lambda t: send2.at[1, t], recv2.at[1])
    share_statistics(1)

    def send_normed(s):
        arrived(AG1 + s, ab.at[s, pl.ds(0, NC)])
        columns_of(ab.at[s], at.at[s])
        for h in range(HL):
            tiles = []
            for m in range(4):
                column = 8 * m + h
                mean_col = at[s, 0:WP, column : column + 1]
                inv_col = at[s, 0:WP, column + 3 : column + 4]
                inv_tile = jnp.broadcast_to(inv_col, (WP, LN))
                invb[s, 4 * h + m] = inv_tile
                centred = (members_of(tx, h, 4 * s + m) - mean_col) * inv_tile
                cen[s, 4 * h + m] = centred
                tiles.append(centred * gain_row + shift_row)
            store_dense(s, h, tiles)
        out = dot(dv[0], xn[s]) * lon_factor
        send1[s] = out.reshape(NS, 4, PL).astype(BF16)
        spread("space", A1 + s, lambda t: send1.at[s, t], recv1.at[s])

    send_normed(0)
    send_normed(1)

    def latitude(received, target, ones):
        for h in range(HL):
            rc[LN * h : LN * h + LN, :] = received[:, :, HB * h : HB * h + HB].reshape(LN, HB)
        out = dot(lv[...], rc[...]) * lat_factor
        for mm in range(2):
            for part in range(2):
                rows = slice(2 * H * mm + H * part, 2 * H * mm + H * part + H)
                for m in range(4):
                    tile = tile_of(out, rows, 0, m, lane_h)
                    if ones:
                        tile = jnp.where(lane_h == CB, 1.0 - part, tile)
                    target[mm, H * m : H * m + H, LN * part : LN * part + LN] = tile.astype(BF16)

    loads[8].wait()

    def mix(s):
        def step(i, carry):
            pre = dot(lt[s, i], wc[0]) + vec[2:3, :]
            t = jnp.tanh(gelu_scale * (pre + gelu_cubic * pre * pre * pre))
            hidden = 0.5 * pre * (1.0 + t)
            hidden = jnp.where(lane_t == CB, 1.0, hidden).astype(BF16)
            slope = 0.5 * (1.0 + t) + 0.5 * pre * (1.0 - t * t) * gelu_scale * (
                1.0 + 3.0 * gelu_cubic * pre * pre
            )
            hid[s, i] = hidden
            post = dot(hidden, wc[1]) + vec[3:4, :]
            shape = jnp.tanh(post * (1.0 / shrink_level))
            shrunk = post - shrink_level * shape
            grad_post = (gsh[s, i].astype(F32) * (shape * shape)).astype(BF16)
            gpost[s, i] = grad_post
            grad_pre = (dot_nt(grad_post, wc[1]) * slope).astype(BF16)
            gpre[s, i] = grad_pre
            grad_lat = dot_nt(grad_pre, wc[0])
            for source, target in ((shrunk, sh), (grad_lat, glat)):
                for part in range(2):
                    tiles = [
                        source[H * m : H * m + H, LN * part : LN * part + LN] for m in range(4)
                    ]
                    for j, column in enumerate(dense(tiles, lane_h)):
                        target[s, i, H * part : H * part + H, LN * j : LN * j + LN] = (
                            column.astype(BF16)
                        )
            return carry

        lax.fori_loop(0, 2, step, 0)

    def back(source, target):
        out = dot(mv[...], source[...].reshape(4 * H, HB)) * lat_factor
        for h in range(HL):
            piece = out[LN * h : LN * h + LN, :].reshape(NS, 4, HB)
            target[:, :, HB * h : HB * h + HB] = piece.astype(BF16)

    for s in range(2):
        arrived(A2 + s, recv2.at[s])
        latitude(recv2.at[s], gsh.at[s], False)
    loads[9].wait()
    for s in range(2):
        arrived(A1 + s, recv1.at[s])
        latitude(recv1.at[s], lt.at[s], True)
        mix(s)
        back(glat.at[s], send4.at[s])
        spread("space", A4 + s, lambda t, s=s: send4.at[s, t], recv4.at[s])
    back(sh.at[0], send3.at[0])
    spread("space", A3, lambda t: send3.at[0, t], recv3.at[0])
    back(sh.at[1], send3.at[1])

    for layer_at, (left, right) in enumerate(((lt, gpre), (hid, gpost))):
        outer = dot_tn(left[...].reshape(16 * H, 2 * LN), right[...].reshape(16 * H, 2 * LN))
        real = outer[0:LN, 0:LN] + outer[LN:, LN:]
        imag = outer[0:LN, LN:] - outer[LN:, 0:LN]
        gb[16 * layer_at : 16 * layer_at + 8] = real.reshape(8, 16, LN).astype(BF16)
        gb[16 * layer_at + 8 : 16 * layer_at + 16] = imag.reshape(8, 16, LN).astype(BF16)

    spread("space", GWR, lambda t: gb.at[t], gr)
    spread("space", A3 + 1, lambda t: send3.at[1, t], recv3.at[1])

    loads[7].wait()
    loads[16].wait()
    norm_sums = [jnp.zeros((8, LN), F32), jnp.zeros((8, LN), F32)]

    def gradient_sums(s):
        arrived(A4 + s, recv4.at[s])
        out = dot(ev[0], recv4[s].reshape(4 * NS, PL)) * lon_factor
        for h in range(HL):
            for m in range(4):
                grad_normed = tile_of(out, slice(0, WP), h, m, lane_w)
                centred = cen[s, 4 * h + m]
                product = grad_normed * centred
                norm_sums[0] = norm_sums[0] + jnp.sum(product.reshape(WP // 8, 8, LN), axis=0)
                norm_sums[1] = norm_sums[1] + jnp.sum(grad_normed.reshape(WP // 8, 8, LN), axis=0)
                grad_centred = grad_normed * gain_row
                i = 4 * h + m
                gc[s, i] = grad_centred * invb[s, i]
                terms[:, 2 * LN * i : 2 * LN * i + LN] = grad_centred.astype(BF16)
                terms[:, 2 * LN * i + LN : 2 * LN * i + 2 * LN] = (
                    grad_centred * centred
                ).astype(BF16)
        acc2[s, 0:WP, :] = dot(terms[...], pick[...])
        pieces_of_sums(acc2.at[s], st2.at[s])
        spread("chan", RS2 + s, lambda t: st2.at[s, t], rb2.at[s])

    gradient_sums(0)
    gradient_sums(1)

    def share_gradient_sums(s):
        arrived(RS2 + s, rb2.at[s])
        ags2[s] = jnp.sum(rb2[s], axis=0) * (1.0 / C)
        spread("chan", AG2 + s, lambda t: ags2.at[s], ab2.at[s])

    share_gradient_sums(0)
    def put_mixed(s):
        out = dot(ev[1], recv3[s].reshape(4 * NS, PL)) * lon_factor
        for h in range(HL):
            for m in range(4):
                put_members(tc, h, 4 * s + m, tile_of(out, slice(0, WP), h, m, lane_w))

    def put_members(array, h, b, tile):
        array[h, pl.ds(b, WP, stride=8), :] = tile

    def put_gradient(s):
        arrived(AG2 + s, ab2.at[s, pl.ds(0, NC)])
        columns_of(ab2.at[s], at2.at[s])
        inv = at[s]
        lane = lax.broadcasted_iota(jnp.int32, (2 * LN, LN), 1)
        at2[s] = at2[s] * jnp.where(lane % 8 < 3, pltpu.roll(inv, LN - 3, 1), inv)
        for h in range(HL):
            for m in range(4):
                column = 8 * m + h
                first = at2[s, 0:WP, column : column + 1]
                second = at2[s, 0:WP, column + 3 : column + 4]
                put_members(
                    tx, h, 4 * s + m, gc[s, 4 * h + m] - first - cen[s, 4 * h + m] * second
                )

    arrived(A3, recv3.at[0])
    put_mixed(0)
    share_gradient_sums(1)
    put_gradient(0)
    arrived(GWR, gr)
    gas[0:16] = jnp.sum(gr[...].astype(F32), axis=0).astype(BF16)
    row8 = lax.broadcasted_iota(jnp.int32, (8, LN), 0)
    gas[16:24] = jnp.where(
        row8 == 0,
        jnp.sum(norm_sums[0], axis=0, keepdims=True),
        jnp.where(row8 == 1, jnp.sum(norm_sums[1], axis=0, keepdims=True), 0.0),
    ).astype(BF16)
    spread("space", GWG, lambda t: gas, ga)
    put_gradient(1)
    for h in range(HL):
        pack(tx, gin_out, h)
    arrived(A3 + 1, recv3.at[1])
    put_mixed(1)
    for h in range(HL):
        pack(tc, mixed_out, h)

    arrived(GWG, ga)
    both = jnp.sum(ga[:, 16:24].astype(F32), axis=0)
    gg_ref[...] = both[0:1, 0:CB]
    gs_ref[...] = both[1:2, 0:CB]
    for layer_at, (gw_ref, gbias_ref) in enumerate(((gw1_ref, gb1_ref), (gw2_ref, gb2_ref))):
        for part in range(2):
            at_piece = 16 * layer_at + 8 * part
            block = ga[at_piece : at_piece + 8, 0:16].astype(F32).reshape(LN, LN)
            gw_ref[part, 0] = block[0:CB, 0:CB]
            gbias_ref[part] = block[CB : CB + 1, 0:CB]

    for s in range(2):
        sent(RS1 + s, rb.at[s], NC)
        sent(AG1 + s, ab.at[s], NC)
        sent(RS2 + s, rb2.at[s], NC)
        sent(AG2 + s, ab2.at[s], NC)
        sent(A2 + s, recv2.at[s], NS)
        sent(A1 + s, recv1.at[s], NS)
        sent(A4 + s, recv4.at[s], NS)
    sent(A3, recv3.at[0], NS)
    sent(A3 + 1, recv3.at[1], NS)
    sent(GWR, gr, NS)
    sent(GWG, ga, NS)


def write_out(*refs):
    count = (len(refs) - 1) // 2
    sems = refs[-1]
    copies = [
        pltpu.make_async_copy(refs[i], refs[count + i], sems.at[i]) for i in range(count)
    ]
    for copy in copies:
        copy.start()
    for copy in copies:
        copy.wait()


def on_device(members, gain, shift, w_first, b_first, w_second, b_second, cotangent):
    lon_out, lon_back, lat_out, lat_back, picks = (jnp.asarray(t) for t in tables())
    anywhere = pl.BlockSpec(memory_space=pl.ANY)
    vmem = pl.BlockSpec(memory_space=pltpu.VMEM)
    stays = pl.BlockSpec(memory_space=pltpu.HBM)
    token = (HL, 1, 8, W * CB)
    piece = (2, NS, 4, PL)
    spectral = (2, 2, 4 * H, 2 * LN)
    folded = (2, 2, 2 * H, HB)
    results = (
        jax.ShapeDtypeStruct(token, BF16),
        jax.ShapeDtypeStruct(token, BF16),
        jax.ShapeDtypeStruct((2, 1, CB, CB), F32),
        jax.ShapeDtypeStruct((2, 1, CB), F32),
        jax.ShapeDtypeStruct((2, 1, CB, CB), F32),
        jax.ShapeDtypeStruct((2, 1, CB), F32),
        jax.ShapeDtypeStruct((1, CB), F32),
        jax.ShapeDtypeStruct((1, CB), F32),
    )
    outs = pl.pallas_call(
        layer,
        out_shape=tuple(pltpu.VMEM(r.shape, r.dtype) for r in results),
        in_specs=[stays] * 13,
        out_specs=tuple([vmem] * 8),
        scratch_shapes=[
            pltpu.VMEM(token, BF16),
            pltpu.VMEM(token, BF16),
            pltpu.VMEM((2, 4 * NS, WP), BF16),
            pltpu.VMEM((2, WP, 4 * NS), BF16),
            pltpu.VMEM((4 * H, 4 * H), BF16),
            pltpu.VMEM((4 * H, 4 * H), BF16),
            pltpu.VMEM((HL, 8 * WP, LN), F32),
            pltpu.VMEM((HL, 8 * WP, LN), F32),
            pltpu.VMEM((2, WP, PL), BF16),
            pltpu.VMEM((2, 4 * HL, WP, LN), F32),
            pltpu.VMEM((2, 4 * HL, WP, LN), F32),
        ]
        + [pltpu.VMEM(piece, BF16)] * 8
        + [pltpu.VMEM((4 * H, HB), BF16)]
        + [pltpu.VMEM(spectral, BF16)] * 5
        + [pltpu.VMEM(folded, BF16)] * 2
        + [
            pltpu.VMEM((2, 2 * LN, 2 * LN), BF16),
            pltpu.VMEM((8, 2 * LN), F32),
        ]
        + [
            pltpu.VMEM((2, 2 * LN, LN), F32),
            pltpu.VMEM((2, NC, 8, LN), F32),
            pltpu.VMEM((2, NC, 8, LN), F32),
            pltpu.VMEM((2, 8, LN), F32),
            pltpu.VMEM((2, 2 * NC, 8, LN), F32),
            pltpu.VMEM((2, 2 * LN, LN), F32),
        ]
        * 2
        + [
            pltpu.VMEM((NS, 16, LN), BF16),
            pltpu.VMEM((NS, 16, LN), BF16),
            pltpu.VMEM((24, LN), BF16),
            pltpu.VMEM((NS, 24, LN), BF16),
            pltpu.VMEM((2, 4 * HL, WP, LN), F32),
            pltpu.VMEM((WP, 8 * HL * LN), BF16),
            pltpu.VMEM((8 * HL * LN, LN), BF16),
            pltpu.VMEM((2, 1, CB), F32),
            pltpu.VMEM((2, 1, CB, CB), BF16),
            pltpu.VMEM((2, 1, CB, CB), BF16),
            pltpu.VMEM((2, 1, CB), F32),
            pltpu.VMEM((2, 1, CB), F32),
            pltpu.SemaphoreType.DMA((17,)),
            pltpu.SemaphoreType.DMA((18,)),
            pltpu.SemaphoreType.DMA((18,)),
        ],
        compiler_params=pltpu.CompilerParams(
            collective_id=0, has_side_effects=True, vmem_limit_bytes=60 * 1024 * 1024
        ),
    )(
        jnp.transpose(members, (1, 2, 0, 3)),
        jnp.transpose(cotangent, (1, 2, 0, 3)),
        gain.reshape(1, CB),
        shift.reshape(1, CB),
        w_first,
        b_first,
        w_second,
        b_second,
        lon_out,
        lon_back,
        lat_out,
        lat_back,
        picks,
    )
    outs = [pltpu.with_memory_space_constraint(o, pltpu.VMEM) for o in outs]
    mixed, grad_input, gw1, gb1, gw2, gb2, gg, gs = pl.pallas_call(
        write_out,
        out_shape=results,
        in_specs=[vmem] * 8,
        out_specs=tuple([anywhere] * 8),
        scratch_shapes=[pltpu.SemaphoreType.DMA((8,))],
    )(*outs)
    return (
        jnp.transpose(mixed, (2, 0, 1, 3)),
        jnp.transpose(grad_input, (2, 0, 1, 3)),
        gw1,
        gb1,
        gw2,
        gb2,
        gg.reshape(CB),
        gs.reshape(CB),
    )


def solution(mesh):
    placed = (
        P(None, "space", "chan", None),
        P("chan"),
        P("chan"),
        P(None, "chan", None, None),
        P(None, "chan", None),
        P(None, "chan", None, None),
        P(None, "chan", None),
        P(None, "space", "chan", None),
    )
    return jax.shard_map(
        on_device,
        mesh=mesh,
        in_specs=placed,
        out_specs=(
            P(None, "space", "chan", None),
            P(None, "space", "chan", None),
            P(None, "chan", None, None),
            P(None, "chan", None),
            P(None, "chan", None, None),
            P(None, "chan", None),
            P("chan"),
            P("chan"),
        ),
        check_vma=False,
    )
```
